32 devices in a mesh: frames: 2 (over y), az: 8 (over z, x), rg: 2 (over core).
Axes of the slice: x: 2, y: 2, z: 4, core: 2. Of those that a mesh axis runs over, the one named last changes fastest.
Arguments:
- raw: bfloat16 [2, 512, 8, 2048], P(None, ('frames', 'az'), None, 'rg'), parts along dimension 1, may hold values from -6 to 6
- stolt_weights: bfloat16 [4, 16, 256, 128], P(None, 'rg'), may hold values from -0.375 to 0.375
- band_start: int32 [4, 16], replicated, may hold values from 0 to 14, as said below
Outputs:
- image: bfloat16 [2, 512, 8, 2048], P(None, ('frames', 'az'), None, 'rg'), parts along dimension 1
The draws below stay inside these ranges and needn't reach their ends.
There are 2 independent parts, one for each index of `frames`. The reference program is written for one: setup_inputs(seed, part) draws one part's arguments, and reference() takes and returns one part's arrays. A program takes and returns all parts, laid end to end along the dimension named above; an argument that names none is the same for every part. Nothing has to cross between parts.
Inputs may be any that keep to these rules, and one draw needn't show every extreme that they name: band_start[g, j] is (j) - 1 or (j), clipped to the range; for every block j from 1 to 14 some slab has (j) - 1 and some slab has (j).
All inputs are finite; a program needn't handle non-finite values.
Results may differ from the reference program's by a relative error of at most 0.001.
Values may be sent and summed in bfloat16 or wider, within the bound.
No kernel may reach another device: no remote copies, remote signals or barrier semaphores. Data moves between devices by JAX's collectives and lax.ppermute only.
A program may use at most 64 MiB of HBM per device.

```python
import jax
import jax.numpy as jnp
from jax import lax

LINES_DEV = 256
NR = 2048
SLABS = 4
GROUPS = 8
NA = 2048
NB = 16


def draw_band_start(key, part):
    block_total = NR // 128
    key_shift, key_first, key_second = jax.random.split(key, 3)
    shifts = jax.random.randint(key_shift, (SLABS, block_total), 0, 2)
    first_slab = jax.random.randint(key_first, (1, block_total), 0, SLABS)
    second_slab = (first_slab + jax.random.randint(key_second, (1, block_total), 1, SLABS)) % SLABS
    slab_ids = jnp.arange(SLABS, dtype=jnp.int32)[:, None]
    shifts = jnp.where(slab_ids == first_slab, 0, jnp.where(slab_ids == second_slab, 1, shifts))
    blocks = jnp.arange(block_total, dtype=jnp.int32)[None, :]
    return jnp.clip(blocks - shifts, 0, block_total - 2).astype(jnp.int32)


def steps_of(own_key, shape, pieces, low, largest):
    gain, own = 1.0, jax.random.fold_in(own_key, 6)
    for axis_at, shards_of in pieces:
        draws = jnp.exp(jax.random.uniform(jax.random.fold_in(own, axis_at), (shards_of,), jnp.float32, low / len(pieces), largest / len(pieces)))
        gain = gain * jnp.repeat(draws, shape[axis_at] // shards_of).reshape([-1 if axis == axis_at else 1 for axis in range(len(shape))])
    return gain


def centred(key, shape, width, limit, shards=(), held_as=jnp.bfloat16):
    array = jax.random.normal(key, shape, jnp.float32) * width
    if len(shards) > 0:
        array = steps_of(key, shape, shards, -0.22, 0.18) * array
    return jnp.clip(array, min=-limit, max=limit).astype(held_as)


def setup_inputs(seed: int = 0, part: int = 0) -> dict:
    keys = jax.random.split(jax.random.key(seed), 4)
    own_keys = jax.random.split(jax.random.fold_in(keys[3], part), 4)
    return {
        "raw": centred(own_keys[0], (2, LINES_DEV, GROUPS, NR), 1.0, 6.0, ((1, 8), (3, 2))),
        "stolt_weights": centred(keys[1], (SLABS, NB, 256, 128), 256 ** -0.5, 0.375, ((1, 2),)),
        "band_start": draw_band_start(jax.random.fold_in(keys[3], 71), part),
    }


def reference(raw, stolt_weights, band_start):
    echo_lines = raw.astype(jnp.float32).transpose(0, 2, 1, 3).reshape(2, NA, NR)
    spectrum = jnp.fft.fft(echo_lines[0] + 1j * echo_lines[1], axis=0, norm="ortho")
    spectrum_ri = jnp.stack([jnp.real(spectrum), jnp.imag(spectrum)]).astype(jnp.float32)
    slab_rows = NA // SLABS
    slab_parts = []
    for slab_index in range(SLABS):
        slab_data = spectrum_ri[:, slab_index * slab_rows:(slab_index + 1) * slab_rows]
        columns = []
        for block_index in range(NR // 128):
            first_bin = (band_start[slab_index, block_index] * 128).astype(jnp.int32)
            window = lax.dynamic_slice_in_dim(slab_data, first_bin, 256, 2)
            weight_block = stolt_weights[slab_index, block_index].astype(jnp.float32)
            columns.append(jnp.einsum("crb,bo->cro", window, weight_block, precision=lax.Precision.HIGHEST))
        slab_parts.append(jnp.concatenate(columns, 2))
    focused = jnp.concatenate(slab_parts, 1)
    image_c = jnp.fft.ifft(focused[0] + 1j * focused[1], axis=0, norm="ortho")
    image_ri = jnp.stack([jnp.real(image_c), jnp.imag(image_c)])
    image_ri = image_ri.reshape(2, GROUPS, LINES_DEV, NR).transpose(0, 2, 1, 3)
    return image_ri.astype(jnp.bfloat16)
```

```python
import functools
import math

import jax
import jax.numpy as jnp
import numpy as np
from jax import lax
from jax.experimental import pallas as pl
from jax.experimental.pallas import tpu as pltpu
from jax.sharding import PartitionSpec as P

LINES_DEV = 256
SLABS = 4
TILE = 128
BF16 = jnp.bfloat16
F32 = jnp.float32
CODE_STEPS = 256.0
FULL = 32767.0


def with_halo(cells, sides, width):
    for axis, dim in sides:
        count = lax.axis_size(axis)
        ends = count - 1
        head = lax.slice_in_dim(cells, 0, width, axis=dim)
        tail = lax.slice_in_dim(cells, cells.shape[dim] - width, cells.shape[dim], axis=dim)
        cells = jnp.concatenate(
            [
                lax.ppermute(tail, axis, [(i, (i + 1) % count) for i in range(ends)]),
                cells,
                lax.ppermute(head, axis, [((i + 1) % count, i) for i in range(ends)]),
            ],
            axis=dim,
        )
    return cells


def dft_table(length, direction, factor):
    counter = jnp.arange(length, dtype=jnp.int32)
    product = counter[:, None] * counter[None, :] % length
    angles = product.astype(jnp.float32) * (2.0 * math.pi / length)
    cosine = jnp.cos(angles) * factor
    sines = jnp.sin(angles) * (factor * direction)
    return jnp.stack([jnp.stack([cosine, -sines], 1), jnp.stack([sines, cosine], 1)], 0)


def rotate(real_part, imag_part, phase_index, line_total, direction):
    angles = phase_index.astype(jnp.float32) * (2.0 * math.pi / line_total)
    cosine = jnp.cos(angles)
    sines = jnp.sin(angles) * direction
    return (real_part * cosine - imag_part * sines, imag_part * cosine + real_part * sines)


def stolt(slab_source, weights, starts, slab_rows):
    pieces = []
    for slab_index in range(weights.shape[0]):
        slab_data = slab_source[:, slab_index * slab_rows : (slab_index + 1) * slab_rows, :]

        def window_at(start_bin):
            return lax.dynamic_slice_in_dim(slab_data, start_bin, 256, 2)

        windows = jax.vmap(window_at)(starts[slab_index])
        remixed = jnp.einsum(
            "jcmb,jbo->cmjo",
            windows,
            weights[slab_index].astype(jnp.float32),
            precision=lax.Precision.HIGHEST,
        )
        pieces.append(remixed.reshape(2, slab_rows, -1))
    return jnp.concatenate(pieces, 1)


def generic_body(raw, stolt_weights, band_start):
    groups = lax.axis_size("az")
    az_index = lax.axis_index("az")
    rg_index = lax.axis_index("rg")
    part_lines = raw.shape[1]
    bin_count = raw.shape[3]
    line_total = LINES_DEV * groups
    short_forward = dft_table(groups, -1.0, 1.0 / math.sqrt(groups))
    spread = jnp.einsum(
        "dkcp,cmpr->dmkr", short_forward, raw.astype(jnp.float32), precision=lax.Precision.HIGHEST
    )
    line_index = az_index * part_lines + jnp.arange(part_lines, dtype=jnp.int32)
    freq_index = jnp.arange(groups, dtype=jnp.int32)
    phase_index = line_index[:, None] * freq_index[None, :] % line_total
    real_part, imag_part = rotate(spread[0], spread[1], phase_index[:, :, None], line_total, -1.0)
    twisted = jnp.stack([real_part, imag_part])
    long_forward = dft_table(LINES_DEV, -1.0, 1.0 / math.sqrt(LINES_DEV))
    spectrum = jnp.einsum(
        "dkcm,cmjr->dkjr",
        long_forward,
        lax.all_to_all(twisted, "az", split_axis=2, concat_axis=1, tiled=True),
        precision=lax.Precision.HIGHEST,
    )
    spectrum_rows = spectrum[:, :, 0, :]
    slab_rows = LINES_DEV // SLABS
    block_count = bin_count // 128
    padded = with_halo(spectrum_rows, (("rg", 2),), 128)
    local_band = lax.dynamic_slice_in_dim(band_start, rg_index * block_count, block_count, 1)
    starts = (local_band - rg_index * block_count) * 128 + 128
    remapped = stolt(padded, stolt_weights, starts, slab_rows)
    long_inverse = dft_table(LINES_DEV, 1.0, 1.0 / math.sqrt(LINES_DEV))
    lines_back = jnp.einsum(
        "dmck,ckr->dmr", long_inverse, remapped, precision=lax.Precision.HIGHEST
    )
    all_lines = jnp.arange(LINES_DEV, dtype=jnp.int32)
    back_index = all_lines * az_index % line_total
    real_part, imag_part = rotate(
        lines_back[0], lines_back[1], back_index[:, None], line_total, 1.0
    )
    unrolled = jnp.stack([real_part, imag_part])[:, :, None, :]
    short_inverse = dft_table(groups, 1.0, 1.0 / math.sqrt(groups))
    focused = jnp.einsum(
        "dpck,cmkr->dmpr",
        short_inverse,
        lax.all_to_all(unrolled, "az", split_axis=1, concat_axis=2, tiled=True),
        precision=lax.Precision.HIGHEST,
    )
    return focused.astype(jnp.bfloat16)


NDEV = 8
MLOC = LINES_DEV // NDEV
ROWS = 2 * MLOC
HALF = 16
VMEM_LIMIT = 48 * 1024 * 1024


def split2(x):
    hi = x.astype(BF16)
    lo = (x - hi.astype(F32)).astype(BF16)
    return hi, lo


def mm(a, b):
    return jnp.dot(a, b, preferred_element_type=F32)


def short_forward_table():
    k1, co, mo = np.meshgrid(np.arange(8), np.arange(2), np.arange(HALF), indexing="ij")
    ci, mi, p = np.meshgrid(np.arange(2), np.arange(HALF), np.arange(8), indexing="ij")
    k1, co, mo = (v.reshape(-1, 1) for v in (k1, co, mo))
    ci, mi, p = (v.reshape(1, -1) for v in (ci, mi, p))
    turn = (k1 * p + 2 * (co - ci)) % 8
    unit = np.array([1, math.sqrt(0.5), 0, -math.sqrt(0.5), -1, -math.sqrt(0.5), 0, math.sqrt(0.5)])
    table = np.where(mo == mi, unit[turn], 0.0).astype(np.float32)
    hi = table.astype(jnp.bfloat16)
    lo = (table - hi.astype(np.float32)).astype(jnp.bfloat16)
    return np.stack([hi, lo])


def cos_pair(turn, total, factor):
    value = jnp.cos(turn.astype(F32) * (2.0 * math.pi / total)) * factor
    hi = lax.reduce_precision(value, 8, 7)
    return jnp.stack([hi.astype(BF16), (value - hi).astype(BF16)])


def long_turn(row, col, me):
    k2 = row // 128 * 64 + row % 64
    co = row // 64 % 2
    ci = col // LINES_DEV
    line = ((col // MLOC % NDEV) ^ me) * MLOC + col % MLOC
    total = NDEV * LINES_DEV
    return (line * (NDEV * k2 + me) + (co - ci + 4) * (total // 4)) % total


def long_tables(me):
    total = NDEV * LINES_DEV
    shape = (2 * LINES_DEV, 2 * LINES_DEV)
    a = lax.broadcasted_iota(jnp.int32, shape, 0)
    b = lax.broadcasted_iota(jnp.int32, shape, 1)
    forward = cos_pair(long_turn(a, b, me), total, 1.0 / 32.0)
    inverse = cos_pair(long_turn(b, a, me), total, 1.0 / 64.0)
    return forward, inverse


def short_inverse_table(me):
    a = lax.broadcasted_iota(jnp.int32, (256, 256), 0)
    b = lax.broadcasted_iota(jnp.int32, (256, 256), 1)
    co, mo, p = a // 128, a // 8 % HALF, a % 8
    k1, ci, mi = (b // 32) ^ me, b // HALF % 2, b % HALF
    turn = (k1 * p + 2 * (ci - co) + 8) % 8
    value = jnp.cos(turn.astype(F32) * (2.0 * math.pi / 8))
    value = jnp.where(mo == mi, value, 0.0)
    hi = lax.reduce_precision(value, 8, 7)
    return jnp.stack([hi.astype(BF16), (value - hi).astype(BF16)])


def store_coded(out_ref, pieces, tiles):
    peak = None
    for _, value in pieces:
        top = jnp.max(jnp.abs(value), axis=0, keepdims=True)
        peak = top if peak is None else jnp.maximum(peak, top)
    code = jnp.ceil(jnp.log2(jnp.maximum(peak, 1e-30) * (1.0 / FULL)) * CODE_STEPS + 0.01)
    inverse = jnp.exp2(code * (-1.0 / CODE_STEPS))
    for row, value in pieces:
        coded = jnp.round(value * inverse).astype(jnp.int32).astype(jnp.int16)
        for tile in range(tiles):
            at = tile * ROWS + row
            out_ref[at : at + value.shape[0], :] = coded[:, tile * TILE : (tile + 1) * TILE]
    which = lax.broadcasted_iota(jnp.int32, (16, TILE), 0)
    scales = jnp.zeros((16, TILE), F32)
    for tile in range(tiles):
        scales = jnp.where(which == tile, code[:, tile * TILE : (tile + 1) * TILE], scales)
    out_ref[tiles * ROWS : tiles * ROWS + 16, :] = scales.astype(jnp.int32).astype(jnp.int16)


def load_scales(ref, tiles):
    code = ref[tiles * ROWS : tiles * ROWS + 16, :].astype(jnp.int32).astype(F32)
    return jnp.exp2(code * (1.0 / CODE_STEPS))


def load_coded(ref, scale_row, at):
    return ref[pl.ds(at, ROWS), :].astype(jnp.int32).astype(F32) * scale_row


def spread_kernel(me_ref, x_ref, table_ref, *out_refs):
    me = me_ref[0]
    hi, lo = [
        jnp.concatenate(
            [table_ref[part, pl.ds(pl.multiple_of((me ^ i) * 32, 32), 32), :] for i in range(NDEV)], 0
        )
        for part in range(2)
    ]
    halves = []
    for h in range(2):
        at = h * 128
        x = jnp.concatenate([x_ref[at : at + 128, :], x_ref[256 + at : 256 + at + 128, :]], 0)
        halves.append(mm(hi, x) + mm(lo, x))
    tiles = x_ref.shape[1] // TILE
    for i in range(NDEV):
        pieces = []
        for c in range(2):
            for h in range(2):
                at = i * 32 + c * HALF
                pieces.append((c * MLOC + h * HALF, halves[h][at : at + HALF, :]))
        store_coded(out_refs[i], pieces, tiles)


def gather_columns(refs, scales, at_rows, rows_of):
    columns = []
    for at, row in zip(at_rows, rows_of):
        parts = [load_coded(ref, scale[row : row + 1, :], at) for ref, scale in zip(refs, scales)]
        columns.append(
            jnp.concatenate([v[:MLOC] for v in parts] + [v[MLOC:] for v in parts], 0)
        )
    return split2(jnp.concatenate(columns, 1) if len(columns) > 1 else columns[0])


def long_product(table_ref, hi, lo):
    return mm(table_ref[0], hi) + mm(table_ref[0], lo) + mm(table_ref[1], hi)


def edge_kernel(side_ref, table_ref, *refs):
    in_refs, out_ref = refs[:NDEV], refs[NDEV]
    tiles = (in_refs[0].shape[0] - 16) // ROWS
    edge = side_ref[0]
    parts = []
    which = lax.broadcasted_iota(jnp.int32, (16, TILE), 0)
    for ref in in_refs:
        scales = load_scales(ref, tiles)
        scale = jnp.sum(jnp.where(which == edge, scales, 0.0), axis=0, keepdims=True)
        parts.append(load_coded(ref, scale, pl.multiple_of(edge * ROWS, ROWS)))
    x = jnp.concatenate([v[:MLOC] for v in parts] + [v[MLOC:] for v in parts], 0)
    hi, lo = split2(x)
    out_ref[0], out_ref[1] = split2(long_product(table_ref, hi, lo))


def forward_kernel(table_ref, *refs):
    in_refs, out_ref = refs[:NDEV], refs[NDEV]
    tiles = (in_refs[0].shape[0] - 16) // ROWS
    scales = [load_scales(ref, tiles) for ref in in_refs]
    for tile in range(0, tiles, 2):
        pair = (tile, tile + 1)
        hi, lo = gather_columns(in_refs, scales, [t * ROWS for t in pair], pair)
        result = long_product(table_ref, hi, lo)
        for at, t in enumerate(pair):
            out_ref[t, 0], out_ref[t, 1] = split2(result[:, at * TILE : (at + 1) * TILE])


def remap_kernel(starts_ref, spectrum_ref, weights_ref, table_ref, *refs):
    out_refs, hi_ref, lo_ref = refs[:NDEV], refs[NDEV], refs[NDEV + 1]
    tiles = weights_ref.shape[1]
    for j in range(tiles):
        for g in range(SLABS):
            first = starts_ref[g, j]
            second = lax.rem(first + 1, tiles + 1)
            rows = slice(g * 128, (g + 1) * 128)
            window = jnp.concatenate(
                [
                    jnp.concatenate([spectrum_ref[first, part, rows, :], spectrum_ref[second, part, rows, :]], 1)
                    for part in range(2)
                ],
                0,
            )
            both = mm(window, weights_ref[g, j])
            hi, lo = split2(both[:128] + both[128:])
            hi_ref[rows, j * TILE : (j + 1) * TILE] = hi
            lo_ref[rows, j * TILE : (j + 1) * TILE] = lo
    lines = long_product(table_ref, hi_ref[...], lo_ref[...])
    for i in range(NDEV):
        pieces = []
        for c in range(2):
            at = c * LINES_DEV + i * MLOC
            pieces.append((c * MLOC, lines[at : at + MLOC, :]))
        store_coded(out_refs[i], pieces, tiles)


def image_kernel(table_ref, *refs):
    in_refs, out_ref = refs[:NDEV], refs[NDEV]
    tiles = (in_refs[0].shape[0] - 16) // ROWS
    scales = [load_scales(ref, tiles) for ref in in_refs]
    for tile in range(0, tiles, 2):
        values = [
            jnp.concatenate(
                [load_coded(ref, scale[t : t + 1, :], t * ROWS) for t in (tile, tile + 1)], 1
            )
            for ref, scale in zip(in_refs, scales)
        ]
        for h in range(2):
            x = jnp.concatenate(
                [v[c * MLOC + h * HALF : c * MLOC + (h + 1) * HALF] for v in values for c in range(2)], 0
            )
            hi, lo = split2(x)
            result = (mm(table_ref[0], hi) + mm(table_ref[0], lo) + mm(table_ref[1], hi)).astype(BF16)
            for c in range(2):
                at = c * 256 + h * 128
                out_ref[at : at + 128, tile * TILE : (tile + 2) * TILE] = result[c * 128 : (c + 1) * 128]


def vmem_call(kernel, name, out_shape, smem=0, vmem=0, scratch=()):
    return pl.pallas_call(
        kernel,
        name=name,
        out_shape=out_shape,
        in_specs=[pl.BlockSpec(memory_space=pltpu.SMEM)] * smem
        + [pl.BlockSpec(memory_space=pltpu.VMEM)] * vmem,
        out_specs=jax.tree.map(lambda _: pl.BlockSpec(memory_space=pltpu.VMEM), out_shape),
        scratch_shapes=scratch,
        compiler_params=pltpu.CompilerParams(vmem_limit_bytes=VMEM_LIMIT),
    )


def exchange(messages):
    out = list(messages)
    for i in (6, 7, 4, 5, 3, 2, 1):
        out[i] = lax.ppermute(messages[i], "az", [(d, d ^ i) for d in range(NDEV)])
    return out


def fast_body(raw, stolt_weights, band_start):
    me = lax.axis_index("az").astype(jnp.int32)
    rg = lax.axis_index("rg").astype(jnp.int32)
    bins = raw.shape[3]
    tiles = bins // TILE
    message = [jax.ShapeDtypeStruct((tiles * ROWS + 16, TILE), jnp.int16)] * NDEV
    forward_table, inverse_table = long_tables(me)
    image_table = short_inverse_table(me)

    sent = vmem_call(spread_kernel, "spread", message, smem=1, vmem=2)(
        me[None], raw.reshape(2 * MLOC * NDEV, bins), jnp.asarray(short_forward_table())
    )
    got = exchange(sent)

    edge = vmem_call(
        edge_kernel, "edge", jax.ShapeDtypeStruct((2, 512, TILE), BF16), smem=1, vmem=1 + NDEV
    )(((1 - rg) * (tiles - 1))[None], forward_table, *got)
    halo = lax.ppermute(edge, "rg", [(0, 1), (1, 0)])
    spectrum = vmem_call(
        forward_kernel,
        "forward",
        jax.ShapeDtypeStruct((tiles + 1, 2, 512, TILE), BF16),
        vmem=1 + NDEV,
    )(forward_table, *got)
    spectrum = lax.dynamic_update_slice_in_dim(spectrum, halo[None], tiles, 0)

    local = lax.dynamic_slice_in_dim(band_start, rg * tiles, tiles, 1) - rg * tiles
    slots = (local + (tiles + 1)) % (tiles + 1)
    back = vmem_call(
        remap_kernel,
        "remap",
        message,
        smem=1,
        vmem=3,
        scratch=[pltpu.VMEM((512, bins), BF16), pltpu.VMEM((512, bins), BF16)],
    )(slots, spectrum, stolt_weights, inverse_table)
    lines = exchange(back)

    image = vmem_call(
        image_kernel, "image", jax.ShapeDtypeStruct((2 * MLOC * NDEV, bins), BF16), vmem=1 + NDEV
    )(image_table, *lines)
    return image.reshape(2, MLOC, NDEV, bins)


def body(raw, stolt_weights, band_start):
    fast = (
        lax.axis_size("az") == NDEV
        and lax.axis_size("rg") == 2
        and raw.shape[1:3] == (MLOC, NDEV)
        and raw.shape[3] % (2 * TILE) == 0
    )
    return (fast_body if fast else generic_body)(raw, stolt_weights, band_start)


def solution(mesh):
    placed = (P(None, ("frames", "az"), None, "rg"), P(None, "rg", None, None), P())
    return jax.shard_map(
        body,
        mesh=mesh,
        in_specs=placed,
        out_specs=P(None, ("frames", "az"), None, "rg"),
        check_vma=False,
    )
```

```python
import functools
import math

import jax
import jax.numpy as jnp
import numpy as np
from jax import lax
from jax.experimental import pallas as pl
from jax.experimental.pallas import tpu as pltpu
from jax.sharding import PartitionSpec as P

LINES_DEV = 256
SLABS = 4
TILE = 128
BF16 = jnp.bfloat16
F32 = jnp.float32
CODE_STEPS = 256.0
FULL = 32767.0


def with_halo(cells, sides, width):
    for axis, dim in sides:
        count = lax.axis_size(axis)
        ends = count - 1
        head = lax.slice_in_dim(cells, 0, width, axis=dim)
        tail = lax.slice_in_dim(cells, cells.shape[dim] - width, cells.shape[dim], axis=dim)
        cells = jnp.concatenate(
            [
                lax.ppermute(tail, axis, [(i, (i + 1) % count) for i in range(ends)]),
                cells,
                lax.ppermute(head, axis, [((i + 1) % count, i) for i in range(ends)]),
            ],
            axis=dim,
        )
    return cells


def dft_table(length, direction, factor):
    counter = jnp.arange(length, dtype=jnp.int32)
    product = counter[:, None] * counter[None, :] % length
    angles = product.astype(jnp.float32) * (2.0 * math.pi / length)
    cosine = jnp.cos(angles) * factor
    sines = jnp.sin(angles) * (factor * direction)
    return jnp.stack([jnp.stack([cosine, -sines], 1), jnp.stack([sines, cosine], 1)], 0)


def rotate(real_part, imag_part, phase_index, line_total, direction):
    angles = phase_index.astype(jnp.float32) * (2.0 * math.pi / line_total)
    cosine = jnp.cos(angles)
    sines = jnp.sin(angles) * direction
    return (real_part * cosine - imag_part * sines, imag_part * cosine + real_part * sines)


def stolt(slab_source, weights, starts, slab_rows):
    pieces = []
    for slab_index in range(weights.shape[0]):
        slab_data = slab_source[:, slab_index * slab_rows : (slab_index + 1) * slab_rows, :]

        def window_at(start_bin):
            return lax.dynamic_slice_in_dim(slab_data, start_bin, 256, 2)

        windows = jax.vmap(window_at)(starts[slab_index])
        remixed = jnp.einsum(
            "jcmb,jbo->cmjo",
            windows,
            weights[slab_index].astype(jnp.float32),
            precision=lax.Precision.HIGHEST,
        )
        pieces.append(remixed.reshape(2, slab_rows, -1))
    return jnp.concatenate(pieces, 1)


def generic_body(raw, stolt_weights, band_start):
    groups = lax.axis_size("az")
    az_index = lax.axis_index("az")
    rg_index = lax.axis_index("rg")
    part_lines = raw.shape[1]
    bin_count = raw.shape[3]
    line_total = LINES_DEV * groups
    short_forward = dft_table(groups, -1.0, 1.0 / math.sqrt(groups))
    spread = jnp.einsum(
        "dkcp,cmpr->dmkr", short_forward, raw.astype(jnp.float32), precision=lax.Precision.HIGHEST
    )
    line_index = az_index * part_lines + jnp.arange(part_lines, dtype=jnp.int32)
    freq_index = jnp.arange(groups, dtype=jnp.int32)
    phase_index = line_index[:, None] * freq_index[None, :] % line_total
    real_part, imag_part = rotate(spread[0], spread[1], phase_index[:, :, None], line_total, -1.0)
    twisted = jnp.stack([real_part, imag_part])
    long_forward = dft_table(LINES_DEV, -1.0, 1.0 / math.sqrt(LINES_DEV))
    spectrum = jnp.einsum(
        "dkcm,cmjr->dkjr",
        long_forward,
        lax.all_to_all(twisted, "az", split_axis=2, concat_axis=1, tiled=True),
        precision=lax.Precision.HIGHEST,
    )
    spectrum_rows = spectrum[:, :, 0, :]
    slab_rows = LINES_DEV // SLABS
    block_count = bin_count // 128
    padded = with_halo(spectrum_rows, (("rg", 2),), 128)
    local_band = lax.dynamic_slice_in_dim(band_start, rg_index * block_count, block_count, 1)
    starts = (local_band - rg_index * block_count) * 128 + 128
    remapped = stolt(padded, stolt_weights, starts, slab_rows)
    long_inverse = dft_table(LINES_DEV, 1.0, 1.0 / math.sqrt(LINES_DEV))
    lines_back = jnp.einsum(
        "dmck,ckr->dmr", long_inverse, remapped, precision=lax.Precision.HIGHEST
    )
    all_lines = jnp.arange(LINES_DEV, dtype=jnp.int32)
    back_index = all_lines * az_index % line_total
    real_part, imag_part = rotate(
        lines_back[0], lines_back[1], back_index[:, None], line_total, 1.0
    )
    unrolled = jnp.stack([real_part, imag_part])[:, :, None, :]
    short_inverse = dft_table(groups, 1.0, 1.0 / math.sqrt(groups))
    focused = jnp.einsum(
        "dpck,cmkr->dmpr",
        short_inverse,
        lax.all_to_all(unrolled, "az", split_axis=1, concat_axis=2, tiled=True),
        precision=lax.Precision.HIGHEST,
    )
    return focused.astype(jnp.bfloat16)


NDEV = 8
MLOC = LINES_DEV // NDEV
ROWS = 2 * MLOC
HALF = 16
TAIL = 8
TILES = 8
LINES = 2 * LINES_DEV
SIDE = LINES_DEV // 2
ORDER = (1, 2, 4, 5, 6, 7, 3, 0)
PLACE = tuple(ORDER.index(i) for i in range(NDEV))
VMEM_LIMIT = 20 * 1024 * 1024


def split2(x):
    hi = x.astype(BF16)
    lo = (x - hi.astype(F32)).astype(BF16)
    return hi, lo


def mm(a, b):
    return jnp.dot(a, b, preferred_element_type=F32)


def product3(table, pair):
    return mm(table[0], pair[0]) + mm(table[0], pair[1]) + mm(table[1], pair[0])


def table_pair(table):
    hi = table.astype(jnp.bfloat16)
    return np.stack([hi, (table - hi.astype(np.float32)).astype(jnp.bfloat16)])


def short_table(upper):
    k1, co, mo = np.meshgrid(np.arange(8), np.arange(2), np.arange(HALF), indexing="ij")
    ci, mi, p = np.meshgrid(np.arange(2), np.arange(HALF), np.arange(8), indexing="ij")
    k1, co, mo = (v.reshape(-1, 1) for v in (k1, co, mo))
    ci, mi, p = (v.reshape(1, -1) for v in (ci, mi, p))
    turn = (k1 * (2 * p + upper) + 4 * (co - ci)) % 16
    unit = np.cos(2 * np.pi * np.arange(16) / 16)
    unit[[4, 12]] = 0.0
    return np.where(mo == mi, unit[turn], 0.0).astype(np.float32)


def long_base():
    k2 = np.arange(LINES_DEV).reshape(-1, 2).T.reshape(1, -1)
    angle = 2 * np.pi * (np.arange(SIDE).reshape(-1, 1) * k2 % LINES_DEV) / LINES_DEV
    return np.stack([np.cos(angle), np.sin(angle)]).astype(np.float32)


def rows_at(index, size):
    return pl.ds(pl.multiple_of(index * size, size), size)


def tiles_of(ref):
    return (ref.shape[-2] - TAIL) // ROWS


def store_coded(out_ref, pieces):
    tiles = tiles_of(out_ref)
    peak = None
    for _, value in pieces:
        top = jnp.max(jnp.abs(value), axis=0, keepdims=True)
        peak = top if peak is None else jnp.maximum(peak, top)
    code = jnp.ceil(jnp.log2(jnp.maximum(peak, 1e-30) * (1.0 / FULL)) * CODE_STEPS + 0.01)
    inverse = jnp.exp2(code * (-1.0 / CODE_STEPS))
    for row, value in pieces:
        coded = jnp.round(value * inverse).astype(jnp.int32).astype(jnp.int16)
        for tile in range(tiles):
            at = tile * ROWS + row
            out_ref[at : at + value.shape[0], :] = coded[:, tile * TILE : (tile + 1) * TILE]
    which = lax.broadcasted_iota(jnp.int32, (TAIL, TILE), 0)
    scales = jnp.zeros((TAIL, TILE), F32)
    for tile in range(tiles):
        scales = jnp.where(which == tile, code[:, tile * TILE : (tile + 1) * TILE], scales)
    out_ref[tiles * ROWS : tiles * ROWS + TAIL, :] = scales.astype(jnp.int32).astype(jnp.int16)


def load_scales(ref):
    at = tiles_of(ref) * ROWS
    code = ref[at : at + TAIL, :].astype(jnp.int32).astype(F32)
    return jnp.exp2(code * (1.0 / CODE_STEPS))


def load_columns(ref, scales, tiles):
    parts = []
    for t in tiles:
        value = ref[t * ROWS : (t + 1) * ROWS, :].astype(jnp.int32).astype(F32)
        parts.append(value * scales[t : t + 1, :])
    return jnp.concatenate(parts, 1)


def tile_pairs(tiles):
    return [(t, t + 1) for t in range(0, tiles, 2)]


def in_order(refs):
    return [refs[at] for at in PLACE]


def sign_of(me):
    return (1 - 2 * (me // 4)).astype(F32)


def spread_kernel(me_ref, x_ref, table_ref, *out_refs):
    me = me_ref[0]
    hi, lo = [
        jnp.concatenate([table_ref[me // 4, part, rows_at(me ^ i, 32), :] for i in range(NDEV)], 0)
        for part in range(2)
    ]
    halves = []
    for h in range(2):
        at = h * 128
        x = jnp.concatenate([x_ref[at : at + 128, :], x_ref[256 + at : 256 + at + 128, :]], 0)
        halves.append(mm(hi, x) + mm(lo, x))
    for n, out_ref in enumerate(out_refs):
        pieces = []
        for c in range(2):
            for h in range(2):
                at = n * 32 + c * HALF
                pieces.append((c * MLOC + h * HALF, halves[h][at : at + HALF, :]))
        store_coded(out_ref, pieces)


def tables_kernel(me_ref, base_ref, short_ref, forward_ref, inverse_ref, image_ref):
    me = me_ref[0]
    step = 2.0 * math.pi / (NDEV * LINES_DEV)
    blocks = []
    for i in range(4):
        slot = (me & 3) ^ i
        line = lax.broadcasted_iota(jnp.int32, (MLOC, TILE), 0) + slot * MLOC
        angle = (line * me).astype(F32) * step
        turn_cos, turn_sin = jnp.cos(angle) * (1.0 / 64.0), jnp.sin(angle) * (1.0 / 64.0)
        cosine, sine = [base_ref[n, rows_at(slot, MLOC), :] for n in range(2)]
        turn_cos = jnp.concatenate([turn_cos, turn_cos], 1)
        turn_sin = jnp.concatenate([turn_sin, turn_sin], 1)
        blocks.append((cosine * turn_cos - sine * turn_sin, sine * turn_cos + cosine * turn_sin))
    whole = [jnp.concatenate([b[n] for b in blocks], 0) for n in range(2)]
    for parity in range(2):
        co, si = [w[:, parity * SIDE : (parity + 1) * SIDE] for w in whole]
        inverse = jnp.concatenate([jnp.concatenate([co, -si], 1), jnp.concatenate([si, co], 1)], 0)
        ct, st = co.T * 2.0, si.T * 2.0
        forward = jnp.concatenate([jnp.concatenate([ct, st], 1), jnp.concatenate([-st, ct], 1)], 0)
        for ref, value in ((inverse_ref, inverse), (forward_ref, forward)):
            ref[0, parity], ref[1, parity] = split2(value)
    for part in range(2):
        rows = [short_ref[me // 4, part, rows_at(me ^ i, 32), :] for i in range(NDEV)]
        image_ref[part] = jnp.concatenate(rows, 0).astype(F32).T.astype(BF16)


def forward_kernel(me_ref, rg_ref, table_ref, *refs):
    in_refs, (out_ref, edge_ref) = in_order(refs[:NDEV]), refs[NDEV:]
    sign = sign_of(me_ref[0])
    scales = [load_scales(ref) for ref in in_refs]
    for tiles in tile_pairs(TILES):
        values = [load_columns(ref, scale, tiles) for ref, scale in zip(in_refs, scales)]
        sums = [values[i] + values[i + 4] for i in range(4)]
        gaps = [(values[i] - values[i + 4]) * sign for i in range(4)]
        for parity, lines in enumerate((sums, gaps)):
            lines = jnp.concatenate([v[:MLOC] for v in lines] + [v[MLOC:] for v in lines], 0)
            result = product3((table_ref[0, parity], table_ref[1, parity]), split2(lines))
            for at, t in enumerate(tiles):
                for part, half in enumerate(split2(result[:, at * TILE : (at + 1) * TILE])):
                    out_ref[t, part, parity * 256 : (parity + 1) * 256, :] = half
    edge_ref[...] = out_ref[(1 - rg_ref[0]) * (TILES - 1)]


def remap_block(starts_ref, weights_ref, rg, j, tile_at):
    for g in range(SLABS):
        at = starts_ref[g, rg * TILES + j] - rg * TILES
        window = []
        for part in range(2):
            for parity in range(2):
                for c in range(2):
                    row = parity * 256 + c * 128 + g * 32
                    rows = slice(row, row + 32)
                    window.append(jnp.concatenate([tile_at(at + n, part, rows) for n in range(2)], 1))
        both = mm(jnp.concatenate(window, 0), weights_ref[g, j])
        yield g, split2(both[:128] + both[128:])


def focus_rows(g):
    return [(parity, c * 128 + g * 32) for parity in range(2) for c in range(2)]


def inner_kernel(rg_ref, starts_ref, spectrum_ref, weights_ref, focus_ref):
    rg = rg_ref[0]
    for n in range(TILES - 1):
        j = n + rg
        for g, pair in remap_block(
            starts_ref, weights_ref, rg, j, lambda t, part, rows: spectrum_ref[t, part, rows, :]
        ):
            for part, half in enumerate(pair):
                for at, (parity, row) in enumerate(focus_rows(g)):
                    focus_ref[part, parity, n, row : row + 32, :] = half[at * 32 : (at + 1) * 32]


def outer_kernel(me_ref, rg_ref, starts_ref, spectrum_ref, halo_ref, weights_ref, table_ref, focus_ref, *refs):
    out_refs, window_ref = refs[:NDEV], refs[NDEV]
    me, rg = me_ref[0], rg_ref[0]
    first = 6 - 7 * rg
    window_ref[2 - 2 * rg] = halo_ref[...]
    for n in range(2):
        window_ref[rg + n] = spectrum_ref[(1 - rg) * 6 + n]
    face = [[[None] * 8 for _ in range(2)] for _ in range(2)]
    for g, pair in remap_block(
        starts_ref,
        weights_ref,
        rg,
        (1 - rg) * (TILES - 1),
        lambda t, part, rows: window_ref[t - first, part, rows, :],
    ):
        for part, half in enumerate(pair):
            for at, (parity, row) in enumerate(focus_rows(g)):
                face[part][parity][row // 32] = half[at * 32 : (at + 1) * 32]
    results = []
    for parity in range(2):
        pair = []
        for part in range(2):
            block = jnp.concatenate(face[part][parity], 0)
            inner = [focus_ref[part, parity, n] for n in range(TILES - 1)]
            pair.append(
                jnp.concatenate(
                    [jnp.where(rg == 1, block, inner[0])]
                    + [jnp.where(rg == 1, inner[n - 1], inner[n]) for n in range(1, TILES - 1)]
                    + [jnp.where(rg == 1, inner[-1], block)],
                    1,
                )
            )
        results.append(product3((table_ref[0, parity], table_ref[1, parity]), pair))
    even, odd = results[0], results[1] * sign_of(me)
    for i, out_ref in enumerate(out_refs):
        lines = even + odd if i < 4 else even - odd
        pieces = []
        for c in range(2):
            at = c * SIDE + (i % 4) * MLOC
            pieces.append((c * MLOC, lines[at : at + MLOC, :]))
        store_coded(out_ref, pieces)


def image_kernel(table_ref, *refs):
    in_refs, out_ref = in_order(refs[:NDEV]), refs[NDEV]
    scales = [load_scales(ref) for ref in in_refs]
    for tiles in tile_pairs(TILES):
        values = [load_columns(ref, scale, tiles) for ref, scale in zip(in_refs, scales)]
        for h in range(2):
            x = jnp.concatenate(
                [v[c * MLOC + h * HALF : c * MLOC + (h + 1) * HALF] for v in values for c in range(2)], 0
            )
            result = product3(table_ref, split2(x)).astype(BF16)
            for c in range(2):
                at = c * 256 + h * 128
                columns = slice(tiles[0] * TILE, (tiles[0] + 2) * TILE)
                out_ref[at : at + 128, columns] = result[c * 128 : (c + 1) * 128]


def vmem_call(kernel, name, out_shape, smem=0, vmem=0, scratch=()):
    return pl.pallas_call(
        kernel,
        name=name,
        out_shape=out_shape,
        in_specs=[pl.BlockSpec(memory_space=pltpu.SMEM)] * smem
        + [pl.BlockSpec(memory_space=pltpu.VMEM)] * vmem,
        out_specs=jax.tree.map(lambda _: pl.BlockSpec(memory_space=pltpu.VMEM), out_shape),
        scratch_shapes=scratch,
        compiler_params=pltpu.CompilerParams(vmem_limit_bytes=VMEM_LIMIT),
    )


def after(value, *others):
    return lax.optimization_barrier((value, *others))[0]


def exchange(messages):
    return [
        lax.ppermute(messages[i], "az", [(d, d ^ i) for d in range(NDEV)]) if i else messages[0]
        for i in ORDER
    ]


def fast_body(raw, stolt_weights, band_start):
    me = lax.axis_index("az").astype(jnp.int32)[None]
    rg = lax.axis_index("rg").astype(jnp.int32)[None]
    bins = raw.shape[3]
    message = jax.ShapeDtypeStruct((TILES * ROWS + TAIL, TILE), jnp.int16)
    short = jnp.asarray(np.stack([table_pair(short_table(upper)) for upper in range(2)]))
    long_shape = jax.ShapeDtypeStruct((2, 2, LINES_DEV, LINES_DEV), BF16)

    sent = vmem_call(spread_kernel, "spread", [message] * NDEV, smem=1, vmem=2)(
        me, raw.reshape(LINES, bins), short
    )
    got = exchange(sent)
    forward_table, inverse_table, image_table = vmem_call(
        tables_kernel,
        "tables",
        [long_shape, long_shape, jax.ShapeDtypeStruct((2, 256, 256), BF16)],
        smem=1,
        vmem=2,
    )(after(me, *sent), jnp.asarray(long_base()), short)

    spectrum, edge = vmem_call(
        forward_kernel,
        "forward",
        [jax.ShapeDtypeStruct((TILES, 2, LINES, TILE), BF16), jax.ShapeDtypeStruct((2, LINES, TILE), BF16)],
        smem=2,
        vmem=1 + NDEV,
    )(me, rg, forward_table, *got)
    halo = lax.ppermute(edge, "rg", [(0, 1), (1, 0)])
    focus = vmem_call(
        inner_kernel,
        "inner",
        jax.ShapeDtypeStruct((2, 2, TILES - 1, LINES_DEV, TILE), BF16),
        smem=2,
        vmem=2,
    )(rg, band_start, spectrum, stolt_weights)
    back = vmem_call(
        outer_kernel,
        "outer",
        [message] * NDEV,
        smem=3,
        vmem=5,
        scratch=[pltpu.VMEM((3, 2, LINES, TILE), BF16)],
    )(me, rg, band_start, spectrum, halo, stolt_weights, inverse_table, focus)
    lines = exchange(back)
    image = vmem_call(image_kernel, "image", jax.ShapeDtypeStruct((LINES, bins), BF16), vmem=1 + NDEV)(
        image_table, *lines
    )
    return image.reshape(2, MLOC, NDEV, bins)


def body(raw, stolt_weights, band_start):
    fast = (
        lax.axis_size("az") == NDEV
        and lax.axis_size("rg") == 2
        and raw.shape[1:3] == (MLOC, NDEV)
        and raw.shape[3] == TILES * TILE
    )
    return (fast_body if fast else generic_body)(raw, stolt_weights, band_start)


def solution(mesh):
    placed = (P(None, ("frames", "az"), None, "rg"), P(None, "rg", None, None), P())
    return jax.shard_map(
        body,
        mesh=mesh,
        in_specs=placed,
        out_specs=P(None, ("frames", "az"), None, "rg"),
        check_vma=False,
    )
```

```python
import functools
import math

import jax
import jax.numpy as jnp
import numpy as np
from jax import lax
from jax.experimental import pallas as pl
from jax.experimental.pallas import tpu as pltpu
from jax.sharding import PartitionSpec as P

LINES_DEV = 256
SLABS = 4
TILE = 128
BF16 = jnp.bfloat16
F32 = jnp.float32
CODE_STEPS = 256.0
FULL = 32767.0


def with_halo(cells, sides, width):
    for axis, dim in sides:
        count = lax.axis_size(axis)
        ends = count - 1
        head = lax.slice_in_dim(cells, 0, width, axis=dim)
        tail = lax.slice_in_dim(cells, cells.shape[dim] - width, cells.shape[dim], axis=dim)
        cells = jnp.concatenate(
            [
                lax.ppermute(tail, axis, [(i, (i + 1) % count) for i in range(ends)]),
                cells,
                lax.ppermute(head, axis, [((i + 1) % count, i) for i in range(ends)]),
            ],
            axis=dim,
        )
    return cells


def dft_table(length, direction, factor):
    counter = jnp.arange(length, dtype=jnp.int32)
    product = counter[:, None] * counter[None, :] % length
    angles = product.astype(jnp.float32) * (2.0 * math.pi / length)
    cosine = jnp.cos(angles) * factor
    sines = jnp.sin(angles) * (factor * direction)
    return jnp.stack([jnp.stack([cosine, -sines], 1), jnp.stack([sines, cosine], 1)], 0)


def rotate(real_part, imag_part, phase_index, line_total, direction):
    angles = phase_index.astype(jnp.float32) * (2.0 * math.pi / line_total)
    cosine = jnp.cos(angles)
    sines = jnp.sin(angles) * direction
    return (real_part * cosine - imag_part * sines, imag_part * cosine + real_part * sines)


def stolt(slab_source, weights, starts, slab_rows):
    pieces = []
    for slab_index in range(weights.shape[0]):
        slab_data = slab_source[:, slab_index * slab_rows : (slab_index + 1) * slab_rows, :]

        def window_at(start_bin):
            return lax.dynamic_slice_in_dim(slab_data, start_bin, 256, 2)

        windows = jax.vmap(window_at)(starts[slab_index])
        remixed = jnp.einsum(
            "jcmb,jbo->cmjo",
            windows,
            weights[slab_index].astype(jnp.float32),
            precision=lax.Precision.HIGHEST,
        )
        pieces.append(remixed.reshape(2, slab_rows, -1))
    return jnp.concatenate(pieces, 1)


def generic_body(raw, stolt_weights, band_start):
    groups = lax.axis_size("az")
    az_index = lax.axis_index("az")
    rg_index = lax.axis_index("rg")
    part_lines = raw.shape[1]
    bin_count = raw.shape[3]
    line_total = LINES_DEV * groups
    short_forward = dft_table(groups, -1.0, 1.0 / math.sqrt(groups))
    spread = jnp.einsum(
        "dkcp,cmpr->dmkr", short_forward, raw.astype(jnp.float32), precision=lax.Precision.HIGHEST
    )
    line_index = az_index * part_lines + jnp.arange(part_lines, dtype=jnp.int32)
    freq_index = jnp.arange(groups, dtype=jnp.int32)
    phase_index = line_index[:, None] * freq_index[None, :] % line_total
    real_part, imag_part = rotate(spread[0], spread[1], phase_index[:, :, None], line_total, -1.0)
    twisted = jnp.stack([real_part, imag_part])
    long_forward = dft_table(LINES_DEV, -1.0, 1.0 / math.sqrt(LINES_DEV))
    spectrum = jnp.einsum(
        "dkcm,cmjr->dkjr",
        long_forward,
        lax.all_to_all(twisted, "az", split_axis=2, concat_axis=1, tiled=True),
        precision=lax.Precision.HIGHEST,
    )
    spectrum_rows = spectrum[:, :, 0, :]
    slab_rows = LINES_DEV // SLABS
    block_count = bin_count // 128
    padded = with_halo(spectrum_rows, (("rg", 2),), 128)
    local_band = lax.dynamic_slice_in_dim(band_start, rg_index * block_count, block_count, 1)
    starts = (local_band - rg_index * block_count) * 128 + 128
    remapped = stolt(padded, stolt_weights, starts, slab_rows)
    long_inverse = dft_table(LINES_DEV, 1.0, 1.0 / math.sqrt(LINES_DEV))
    lines_back = jnp.einsum(
        "dmck,ckr->dmr", long_inverse, remapped, precision=lax.Precision.HIGHEST
    )
    all_lines = jnp.arange(LINES_DEV, dtype=jnp.int32)
    back_index = all_lines * az_index % line_total
    real_part, imag_part = rotate(
        lines_back[0], lines_back[1], back_index[:, None], line_total, 1.0
    )
    unrolled = jnp.stack([real_part, imag_part])[:, :, None, :]
    short_inverse = dft_table(groups, 1.0, 1.0 / math.sqrt(groups))
    focused = jnp.einsum(
        "dpck,cmkr->dmpr",
        short_inverse,
        lax.all_to_all(unrolled, "az", split_axis=1, concat_axis=2, tiled=True),
        precision=lax.Precision.HIGHEST,
    )
    return focused.astype(jnp.bfloat16)


NDEV = 8
MLOC = LINES_DEV // NDEV
ROWS = 2 * MLOC
HALF = 16
TAIL = 8
TILES = 8
LINES = 2 * LINES_DEV
SIDE = LINES_DEV // 2
ORDER = (6, 1, 4, 5, 2, 3, 7, 0)
PLACE = tuple(ORDER.index(i) for i in range(NDEV))
VMEM_LIMIT = 20 * 1024 * 1024


def split2(x):
    hi = x.astype(BF16)
    lo = (x - hi.astype(F32)).astype(BF16)
    return hi, lo


def mm(a, b):
    return jnp.dot(a, b, preferred_element_type=F32)


def product3(table, pair):
    return mm(table[0], pair[0]) + mm(table[0], pair[1]) + mm(table[1], pair[0])


def table_pair(table):
    hi = table.astype(jnp.bfloat16)
    return np.stack([hi, (table - hi.astype(np.float32)).astype(jnp.bfloat16)])


def short_table(upper):
    k1, co, mo = np.meshgrid(np.arange(8), np.arange(2), np.arange(HALF), indexing="ij")
    ci, mi, p = np.meshgrid(np.arange(2), np.arange(HALF), np.arange(8), indexing="ij")
    k1, co, mo = (v.reshape(-1, 1) for v in (k1, co, mo))
    ci, mi, p = (v.reshape(1, -1) for v in (ci, mi, p))
    turn = (k1 * (2 * p + upper) + 4 * (co - ci)) % 16
    unit = np.cos(2 * np.pi * np.arange(16) / 16)
    unit[[4, 12]] = 0.0
    return np.where(mo == mi, unit[turn], 0.0).astype(np.float32)


def long_base():
    k2 = np.arange(LINES_DEV).reshape(-1, 2).T.reshape(1, -1)
    angle = 2 * np.pi * (np.arange(SIDE).reshape(-1, 1) * k2 % LINES_DEV) / LINES_DEV
    return np.stack([np.cos(angle), np.sin(angle)]).astype(np.float32)


def rows_at(index, size):
    return pl.ds(pl.multiple_of(index * size, size), size)


def tiles_of(ref):
    return (ref.shape[-2] - TAIL) // ROWS


def store_coded(out_ref, pieces):
    tiles = tiles_of(out_ref)
    peak = None
    for _, value in pieces:
        top = jnp.max(jnp.abs(value), axis=0, keepdims=True)
        peak = top if peak is None else jnp.maximum(peak, top)
    code = jnp.ceil(jnp.log2(jnp.maximum(peak, 1e-30) * (1.0 / FULL)) * CODE_STEPS + 0.01)
    inverse = jnp.exp2(code * (-1.0 / CODE_STEPS))
    for row, value in pieces:
        coded = jnp.round(value * inverse).astype(jnp.int32).astype(jnp.int16)
        for tile in range(tiles):
            at = tile * ROWS + row
            out_ref[at : at + value.shape[0], :] = coded[:, tile * TILE : (tile + 1) * TILE]
    which = lax.broadcasted_iota(jnp.int32, (TAIL, TILE), 0)
    scales = jnp.zeros((TAIL, TILE), F32)
    for tile in range(tiles):
        scales = jnp.where(which == tile, code[:, tile * TILE : (tile + 1) * TILE], scales)
    out_ref[tiles * ROWS : tiles * ROWS + TAIL, :] = scales.astype(jnp.int32).astype(jnp.int16)


def load_scales(ref):
    at = tiles_of(ref) * ROWS
    code = ref[at : at + TAIL, :].astype(jnp.int32).astype(F32)
    return jnp.exp2(code * (1.0 / CODE_STEPS))


def load_columns(ref, scales, tiles):
    parts = []
    for t in tiles:
        value = ref[t * ROWS : (t + 1) * ROWS, :].astype(jnp.int32).astype(F32)
        parts.append(value * scales[t : t + 1, :])
    return jnp.concatenate(parts, 1)


def tile_pairs(tiles):
    return [(t, t + 1) for t in range(0, tiles, 2)]


def in_order(refs):
    return [refs[at] for at in PLACE]


def sign_of(me):
    return (1 - 2 * (me // 4)).astype(F32)


def spread_kernel(me_ref, x_ref, table_ref, *out_refs):
    me = me_ref[0]
    hi, lo = [
        jnp.concatenate([table_ref[me // 4, part, rows_at(me ^ i, 32), :] for i in range(NDEV)], 0)
        for part in range(2)
    ]
    halves = []
    for h in range(2):
        at = h * 128
        x = jnp.concatenate([x_ref[at : at + 128, :], x_ref[256 + at : 256 + at + 128, :]], 0)
        halves.append(mm(hi, x) + mm(lo, x))
    for n, out_ref in enumerate(out_refs):
        pieces = []
        for c in range(2):
            for h in range(2):
                at = n * 32 + c * HALF
                pieces.append((c * MLOC + h * HALF, halves[h][at : at + HALF, :]))
        store_coded(out_ref, pieces)


def tables_kernel(me_ref, base_ref, short_ref, forward_ref, inverse_ref, image_ref):
    me = me_ref[0]
    step = 2.0 * math.pi / (NDEV * LINES_DEV)
    blocks = []
    for i in range(4):
        slot = (me & 3) ^ i
        line = lax.broadcasted_iota(jnp.int32, (MLOC, TILE), 0) + slot * MLOC
        angle = (line * me).astype(F32) * step
        turn_cos, turn_sin = jnp.cos(angle) * (1.0 / 64.0), jnp.sin(angle) * (1.0 / 64.0)
        cosine, sine = [base_ref[n, rows_at(slot, MLOC), :] for n in range(2)]
        turn_cos = jnp.concatenate([turn_cos, turn_cos], 1)
        turn_sin = jnp.concatenate([turn_sin, turn_sin], 1)
        blocks.append((cosine * turn_cos - sine * turn_sin, sine * turn_cos + cosine * turn_sin))
    whole = [jnp.concatenate([b[n] for b in blocks], 0) for n in range(2)]
    for parity in range(2):
        co, si = [w[:, parity * SIDE : (parity + 1) * SIDE] for w in whole]
        inverse = jnp.concatenate([jnp.concatenate([co, -si], 1), jnp.concatenate([si, co], 1)], 0)
        ct, st = co.T * 2.0, si.T * 2.0
        forward = jnp.concatenate([jnp.concatenate([ct, st], 1), jnp.concatenate([-st, ct], 1)], 0)
        for ref, value in ((inverse_ref, inverse), (forward_ref, forward)):
            ref[0, parity], ref[1, parity] = split2(value)
    for part in range(2):
        rows = [short_ref[me // 4, part, rows_at(me ^ i, 32), :] for i in range(NDEV)]
        image_ref[part] = jnp.concatenate(rows, 0).astype(F32).T.astype(BF16)


def forward_kernel(me_ref, rg_ref, table_ref, *refs):
    in_refs, (out_ref, edge_ref) = in_order(refs[:NDEV]), refs[NDEV:]
    sign = sign_of(me_ref[0])
    scales = [load_scales(ref) for ref in in_refs]
    for tiles in tile_pairs(TILES):
        values = [load_columns(ref, scale, tiles) for ref, scale in zip(in_refs, scales)]
        sums = [values[i] + values[i + 4] for i in range(4)]
        gaps = [(values[i] - values[i + 4]) * sign for i in range(4)]
        for parity, lines in enumerate((sums, gaps)):
            lines = jnp.concatenate([v[:MLOC] for v in lines] + [v[MLOC:] for v in lines], 0)
            result = product3((table_ref[0, parity], table_ref[1, parity]), split2(lines))
            for at, t in enumerate(tiles):
                for part, half in enumerate(split2(result[:, at * TILE : (at + 1) * TILE])):
                    out_ref[t, part, parity * 256 : (parity + 1) * 256, :] = half
    edge_ref[...] = out_ref[(1 - rg_ref[0]) * (TILES - 1)]


def remap_block(starts_ref, weights_ref, rg, j, tile_at):
    for g in range(SLABS):
        at = starts_ref[g, rg * TILES + j] - rg * TILES
        window = []
        for part in range(2):
            for parity in range(2):
                for c in range(2):
                    row = parity * 256 + c * 128 + g * 32
                    rows = slice(row, row + 32)
                    window.append(jnp.concatenate([tile_at(at + n, part, rows) for n in range(2)], 1))
        both = mm(jnp.concatenate(window, 0), weights_ref[g, j])
        yield g, split2(both[:128] + both[128:])


def focus_rows(g):
    return [(parity, c * 128 + g * 32) for parity in range(2) for c in range(2)]


def inner_kernel(rg_ref, starts_ref, spectrum_ref, weights_ref, focus_ref):
    rg = rg_ref[0]
    for n in range(TILES - 1):
        j = n + rg
        for g, pair in remap_block(
            starts_ref, weights_ref, rg, j, lambda t, part, rows: spectrum_ref[t, part, rows, :]
        ):
            for part, half in enumerate(pair):
                for at, (parity, row) in enumerate(focus_rows(g)):
                    focus_ref[part, parity, n, row : row + 32, :] = half[at * 32 : (at + 1) * 32]


def outer_kernel(me_ref, rg_ref, starts_ref, spectrum_ref, halo_ref, weights_ref, table_ref, focus_ref, *refs):
    out_refs, window_ref = refs[:NDEV], refs[NDEV]
    me, rg = me_ref[0], rg_ref[0]
    first = 6 - 7 * rg
    window_ref[2 - 2 * rg] = halo_ref[...]
    for n in range(2):
        window_ref[rg + n] = spectrum_ref[(1 - rg) * 6 + n]
    face = [[[None] * 8 for _ in range(2)] for _ in range(2)]
    for g, pair in remap_block(
        starts_ref,
        weights_ref,
        rg,
        (1 - rg) * (TILES - 1),
        lambda t, part, rows: window_ref[t - first, part, rows, :],
    ):
        for part, half in enumerate(pair):
            for at, (parity, row) in enumerate(focus_rows(g)):
                face[part][parity][row // 32] = half[at * 32 : (at + 1) * 32]
    results = []
    for parity in range(2):
        pair = []
        for part in range(2):
            block = jnp.concatenate(face[part][parity], 0)
            inner = [focus_ref[part, parity, n] for n in range(TILES - 1)]
            pair.append(
                jnp.concatenate(
                    [jnp.where(rg == 1, block, inner[0])]
                    + [jnp.where(rg == 1, inner[n - 1], inner[n]) for n in range(1, TILES - 1)]
                    + [jnp.where(rg == 1, inner[-1], block)],
                    1,
                )
            )
        results.append(product3((table_ref[0, parity], table_ref[1, parity]), pair))
    even, odd = results[0], results[1] * sign_of(me)
    for i, out_ref in enumerate(out_refs):
        lines = even + odd if i < 4 else even - odd
        pieces = []
        for c in range(2):
            at = c * SIDE + (i % 4) * MLOC
            pieces.append((c * MLOC, lines[at : at + MLOC, :]))
        store_coded(out_ref, pieces)


def image_kernel(table_ref, *refs):
    in_refs, out_ref = in_order(refs[:NDEV]), refs[NDEV]
    scales = [load_scales(ref) for ref in in_refs]
    for tiles in tile_pairs(TILES):
        values = [load_columns(ref, scale, tiles) for ref, scale in zip(in_refs, scales)]
        for h in range(2):
            x = jnp.concatenate(
                [v[c * MLOC + h * HALF : c * MLOC + (h + 1) * HALF] for v in values for c in range(2)], 0
            )
            result = product3(table_ref, split2(x)).astype(BF16)
            for c in range(2):
                at = c * 256 + h * 128
                columns = slice(tiles[0] * TILE, (tiles[0] + 2) * TILE)
                out_ref[at : at + 128, columns] = result[c * 128 : (c + 1) * 128]


def vmem_call(kernel, name, out_shape, smem=0, vmem=0, scratch=()):
    return pl.pallas_call(
        kernel,
        name=name,
        out_shape=out_shape,
        in_specs=[pl.BlockSpec(memory_space=pltpu.SMEM)] * smem
        + [pl.BlockSpec(memory_space=pltpu.VMEM)] * vmem,
        out_specs=jax.tree.map(lambda _: pl.BlockSpec(memory_space=pltpu.VMEM), out_shape),
        scratch_shapes=scratch,
        compiler_params=pltpu.CompilerParams(vmem_limit_bytes=VMEM_LIMIT),
    )


def after(value, *others):
    return lax.optimization_barrier((value, *others))[0]


def exchange(messages):
    return [
        lax.ppermute(messages[i], "az", [(d, d ^ i) for d in range(NDEV)]) if i else messages[0]
        for i in ORDER
    ]


def fast_body(raw, stolt_weights, band_start):
    me = lax.axis_index("az").astype(jnp.int32)[None]
    rg = lax.axis_index("rg").astype(jnp.int32)[None]
    bins = raw.shape[3]
    message = jax.ShapeDtypeStruct((TILES * ROWS + TAIL, TILE), jnp.int16)
    short = jnp.asarray(np.stack([table_pair(short_table(upper)) for upper in range(2)]))
    long_shape = jax.ShapeDtypeStruct((2, 2, LINES_DEV, LINES_DEV), BF16)

    sent = vmem_call(spread_kernel, "spread", [message] * NDEV, smem=1, vmem=2)(
        me, raw.reshape(LINES, bins), short
    )
    got = exchange(sent)
    forward_table, inverse_table, image_table = vmem_call(
        tables_kernel,
        "tables",
        [long_shape, long_shape, jax.ShapeDtypeStruct((2, 256, 256), BF16)],
        smem=1,
        vmem=2,
    )(after(me, *sent), jnp.asarray(long_base()), short)

    spectrum, edge = vmem_call(
        forward_kernel,
        "forward",
        [jax.ShapeDtypeStruct((TILES, 2, LINES, TILE), BF16), jax.ShapeDtypeStruct((2, LINES, TILE), BF16)],
        smem=2,
        vmem=1 + NDEV,
    )(me, rg, forward_table, *got)
    halo = lax.ppermute(edge, "rg", [(0, 1), (1, 0)])
    focus = vmem_call(
        inner_kernel,
        "inner",
        jax.ShapeDtypeStruct((2, 2, TILES - 1, LINES_DEV, TILE), BF16),
        smem=2,
        vmem=2,
    )(rg, band_start, spectrum, stolt_weights)
    back = vmem_call(
        outer_kernel,
        "outer",
        [message] * NDEV,
        smem=3,
        vmem=5,
        scratch=[pltpu.VMEM((3, 2, LINES, TILE), BF16)],
    )(me, rg, band_start, spectrum, halo, stolt_weights, inverse_table, focus)
    lines = exchange(back)
    image = vmem_call(image_kernel, "image", jax.ShapeDtypeStruct((LINES, bins), BF16), vmem=1 + NDEV)(
        image_table, *lines
    )
    return image.reshape(2, MLOC, NDEV, bins)


def body(raw, stolt_weights, band_start):
    fast = (
        lax.axis_size("az") == NDEV
        and lax.axis_size("rg") == 2
        and raw.shape[1:3] == (MLOC, NDEV)
        and raw.shape[3] == TILES * TILE
    )
    return (fast_body if fast else generic_body)(raw, stolt_weights, band_start)


def solution(mesh):
    placed = (P(None, ("frames", "az"), None, "rg"), P(None, "rg", None, None), P())
    return jax.shard_map(
        body,
        mesh=mesh,
        in_specs=placed,
        out_specs=P(None, ("frames", "az"), None, "rg"),
        check_vma=False,
    )
```

```python
import functools
import math

import jax
import jax.numpy as jnp
import numpy as np
from jax import lax
from jax.experimental import pallas as pl
from jax.experimental.pallas import tpu as pltpu
from jax.sharding import PartitionSpec as P

LINES_DEV = 256
SLABS = 4
TILE = 128
BF16 = jnp.bfloat16
F32 = jnp.float32
CODE_STEPS = 256.0
FULL = 32767.0


def with_halo(cells, sides, width):
    for axis, dim in sides:
        count = lax.axis_size(axis)
        ends = count - 1
        head = lax.slice_in_dim(cells, 0, width, axis=dim)
        tail = lax.slice_in_dim(cells, cells.shape[dim] - width, cells.shape[dim], axis=dim)
        cells = jnp.concatenate(
            [
                lax.ppermute(tail, axis, [(i, (i + 1) % count) for i in range(ends)]),
                cells,
                lax.ppermute(head, axis, [((i + 1) % count, i) for i in range(ends)]),
            ],
            axis=dim,
        )
    return cells


def dft_table(length, direction, factor):
    counter = jnp.arange(length, dtype=jnp.int32)
    product = counter[:, None] * counter[None, :] % length
    angles = product.astype(jnp.float32) * (2.0 * math.pi / length)
    cosine = jnp.cos(angles) * factor
    sines = jnp.sin(angles) * (factor * direction)
    return jnp.stack([jnp.stack([cosine, -sines], 1), jnp.stack([sines, cosine], 1)], 0)


def rotate(real_part, imag_part, phase_index, line_total, direction):
    angles = phase_index.astype(jnp.float32) * (2.0 * math.pi / line_total)
    cosine = jnp.cos(angles)
    sines = jnp.sin(angles) * direction
    return (real_part * cosine - imag_part * sines, imag_part * cosine + real_part * sines)


def stolt(slab_source, weights, starts, slab_rows):
    pieces = []
    for slab_index in range(weights.shape[0]):
        slab_data = slab_source[:, slab_index * slab_rows : (slab_index + 1) * slab_rows, :]

        def window_at(start_bin):
            return lax.dynamic_slice_in_dim(slab_data, start_bin, 256, 2)

        windows = jax.vmap(window_at)(starts[slab_index])
        remixed = jnp.einsum(
            "jcmb,jbo->cmjo",
            windows,
            weights[slab_index].astype(jnp.float32),
            precision=lax.Precision.HIGHEST,
        )
        pieces.append(remixed.reshape(2, slab_rows, -1))
    return jnp.concatenate(pieces, 1)


def generic_body(raw, stolt_weights, band_start):
    groups = lax.axis_size("az")
    az_index = lax.axis_index("az")
    rg_index = lax.axis_index("rg")
    part_lines = raw.shape[1]
    bin_count = raw.shape[3]
    line_total = LINES_DEV * groups
    short_forward = dft_table(groups, -1.0, 1.0 / math.sqrt(groups))
    spread = jnp.einsum(
        "dkcp,cmpr->dmkr", short_forward, raw.astype(jnp.float32), precision=lax.Precision.HIGHEST
    )
    line_index = az_index * part_lines + jnp.arange(part_lines, dtype=jnp.int32)
    freq_index = jnp.arange(groups, dtype=jnp.int32)
    phase_index = line_index[:, None] * freq_index[None, :] % line_total
    real_part, imag_part = rotate(spread[0], spread[1], phase_index[:, :, None], line_total, -1.0)
    twisted = jnp.stack([real_part, imag_part])
    long_forward = dft_table(LINES_DEV, -1.0, 1.0 / math.sqrt(LINES_DEV))
    spectrum = jnp.einsum(
        "dkcm,cmjr->dkjr",
        long_forward,
        lax.all_to_all(twisted, "az", split_axis=2, concat_axis=1, tiled=True),
        precision=lax.Precision.HIGHEST,
    )
    spectrum_rows = spectrum[:, :, 0, :]
    slab_rows = LINES_DEV // SLABS
    block_count = bin_count // 128
    padded = with_halo(spectrum_rows, (("rg", 2),), 128)
    local_band = lax.dynamic_slice_in_dim(band_start, rg_index * block_count, block_count, 1)
    starts = (local_band - rg_index * block_count) * 128 + 128
    remapped = stolt(padded, stolt_weights, starts, slab_rows)
    long_inverse = dft_table(LINES_DEV, 1.0, 1.0 / math.sqrt(LINES_DEV))
    lines_back = jnp.einsum(
        "dmck,ckr->dmr", long_inverse, remapped, precision=lax.Precision.HIGHEST
    )
    all_lines = jnp.arange(LINES_DEV, dtype=jnp.int32)
    back_index = all_lines * az_index % line_total
    real_part, imag_part = rotate(
        lines_back[0], lines_back[1], back_index[:, None], line_total, 1.0
    )
    unrolled = jnp.stack([real_part, imag_part])[:, :, None, :]
    short_inverse = dft_table(groups, 1.0, 1.0 / math.sqrt(groups))
    focused = jnp.einsum(
        "dpck,cmkr->dmpr",
        short_inverse,
        lax.all_to_all(unrolled, "az", split_axis=1, concat_axis=2, tiled=True),
        precision=lax.Precision.HIGHEST,
    )
    return focused.astype(jnp.bfloat16)


NDEV = 8
MLOC = LINES_DEV // NDEV
ROWS = 2 * MLOC
HALF = 16
TAIL = 8
TILES = 8
LINES = 2 * LINES_DEV
SIDE = LINES_DEV // 2
OUT_ORDER = (6, 2, 4, 5, 1, 3, 7, 0)
BACK_ORDER = (6, 2, 4, 5, 1, 3, 7, 0)
VMEM_LIMIT = 20 * 1024 * 1024


def split2(x):
    hi = x.astype(BF16)
    lo = (x - hi.astype(F32)).astype(BF16)
    return hi, lo


def mm(a, b):
    return jnp.dot(a, b, preferred_element_type=F32)


def product3(table, pair):
    return mm(table[0], pair[0]) + mm(table[0], pair[1]) + mm(table[1], pair[0])


def table_pair(table):
    hi = table.astype(jnp.bfloat16)
    return np.stack([hi, (table - hi.astype(np.float32)).astype(jnp.bfloat16)])


def short_table(upper):
    k1, co, mo = np.meshgrid(np.arange(8), np.arange(2), np.arange(HALF), indexing="ij")
    ci, mi, p = np.meshgrid(np.arange(2), np.arange(HALF), np.arange(8), indexing="ij")
    k1, co, mo = (v.reshape(-1, 1) for v in (k1, co, mo))
    ci, mi, p = (v.reshape(1, -1) for v in (ci, mi, p))
    turn = (k1 * (2 * p + upper) + 4 * (co - ci)) % 16
    unit = np.cos(2 * np.pi * np.arange(16) / 16)
    unit[[4, 12]] = 0.0
    return np.where(mo == mi, unit[turn], 0.0).astype(np.float32)


def long_base():
    k2 = np.arange(LINES_DEV).reshape(-1, 2).T.reshape(1, -1)
    angle = 2 * np.pi * (np.arange(SIDE).reshape(-1, 1) * k2 % LINES_DEV) / LINES_DEV
    return np.stack([np.cos(angle), np.sin(angle)]).astype(np.float32)


def rows_at(index, size):
    return pl.ds(pl.multiple_of(index * size, size), size)


def tiles_of(ref):
    return (ref.shape[-2] - TAIL) // ROWS


def store_coded(out_ref, pieces):
    tiles = tiles_of(out_ref)
    peak = None
    for _, value in pieces:
        top = jnp.max(jnp.abs(value), axis=0, keepdims=True)
        peak = top if peak is None else jnp.maximum(peak, top)
    code = jnp.ceil(jnp.log2(jnp.maximum(peak, 1e-30) * (1.0 / FULL)) * CODE_STEPS + 0.01)
    inverse = jnp.exp2(code * (-1.0 / CODE_STEPS))
    for row, value in pieces:
        coded = jnp.round(value * inverse).astype(jnp.int32).astype(jnp.int16)
        for tile in range(tiles):
            at = tile * ROWS + row
            out_ref[at : at + value.shape[0], :] = coded[:, tile * TILE : (tile + 1) * TILE]
    which = lax.broadcasted_iota(jnp.int32, (TAIL, TILE), 0)
    scales = jnp.zeros((TAIL, TILE), F32)
    for tile in range(tiles):
        scales = jnp.where(which == tile, code[:, tile * TILE : (tile + 1) * TILE], scales)
    out_ref[tiles * ROWS : tiles * ROWS + TAIL, :] = scales.astype(jnp.int32).astype(jnp.int16)


def load_scales(ref):
    at = tiles_of(ref) * ROWS
    code = ref[at : at + TAIL, :].astype(jnp.int32).astype(F32)
    return jnp.exp2(code * (1.0 / CODE_STEPS))


def load_columns(ref, scales, tiles):
    parts = []
    for t in tiles:
        value = ref[t * ROWS : (t + 1) * ROWS, :].astype(jnp.int32).astype(F32)
        parts.append(value * scales[t : t + 1, :])
    return jnp.concatenate(parts, 1)


def tile_pairs(tiles):
    return [(t, t + 1) for t in range(0, tiles, 2)]


def in_order(refs, order):
    return [refs[order.index(i)] for i in range(NDEV)]


def sign_of(me):
    return (1 - 2 * (me // 4)).astype(F32)


def spread_kernel(me_ref, x_ref, table_ref, *out_refs):
    me = me_ref[0]
    hi, lo = [
        jnp.concatenate([table_ref[me // 4, part, rows_at(me ^ i, 32), :] for i in range(NDEV)], 0)
        for part in range(2)
    ]
    halves = []
    for h in range(2):
        at = h * 128
        x = jnp.concatenate([x_ref[at : at + 128, :], x_ref[256 + at : 256 + at + 128, :]], 0)
        halves.append(mm(hi, x) + mm(lo, x))
    for n, out_ref in enumerate(out_refs):
        pieces = []
        for c in range(2):
            for h in range(2):
                at = n * 32 + c * HALF
                pieces.append((c * MLOC + h * HALF, halves[h][at : at + HALF, :]))
        store_coded(out_ref, pieces)


def tables_kernel(me_ref, base_ref, short_ref, forward_ref, inverse_ref, image_ref):
    me = me_ref[0]
    step = 2.0 * math.pi / (NDEV * LINES_DEV)
    blocks = []
    for i in range(4):
        slot = (me & 3) ^ i
        line = lax.broadcasted_iota(jnp.int32, (MLOC, TILE), 0) + slot * MLOC
        angle = (line * me).astype(F32) * step
        turn_cos, turn_sin = jnp.cos(angle) * (1.0 / 64.0), jnp.sin(angle) * (1.0 / 64.0)
        cosine, sine = [base_ref[n, rows_at(slot, MLOC), :] for n in range(2)]
        turn_cos = jnp.concatenate([turn_cos, turn_cos], 1)
        turn_sin = jnp.concatenate([turn_sin, turn_sin], 1)
        blocks.append((cosine * turn_cos - sine * turn_sin, sine * turn_cos + cosine * turn_sin))
    whole = [jnp.concatenate([b[n] for b in blocks], 0) for n in range(2)]
    for parity in range(2):
        co, si = [w[:, parity * SIDE : (parity + 1) * SIDE] for w in whole]
        inverse = jnp.concatenate([jnp.concatenate([co, -si], 1), jnp.concatenate([si, co], 1)], 0)
        ct, st = co.T * 2.0, si.T * 2.0
        forward = jnp.concatenate([jnp.concatenate([ct, st], 1), jnp.concatenate([-st, ct], 1)], 0)
        for ref, value in ((inverse_ref, inverse), (forward_ref, forward)):
            ref[0, parity], ref[1, parity] = split2(value)
    for part in range(2):
        rows = [short_ref[me // 4, part, rows_at(me ^ i, 32), :] for i in range(NDEV)]
        image_ref[part] = jnp.concatenate(rows, 0).astype(F32).T.astype(BF16)


def forward_kernel(me_ref, rg_ref, table_ref, *refs):
    in_refs, (out_ref, edge_ref) = in_order(refs[:NDEV], OUT_ORDER), refs[NDEV:]
    sign = sign_of(me_ref[0])
    scales = [load_scales(ref) for ref in in_refs]
    for tiles in tile_pairs(TILES):
        values = [load_columns(ref, scale, tiles) for ref, scale in zip(in_refs, scales)]
        sums = [values[i] + values[i + 4] for i in range(4)]
        gaps = [(values[i] - values[i + 4]) * sign for i in range(4)]
        for parity, lines in enumerate((sums, gaps)):
            lines = jnp.concatenate([v[:MLOC] for v in lines] + [v[MLOC:] for v in lines], 0)
            result = product3((table_ref[0, parity], table_ref[1, parity]), split2(lines))
            for at, t in enumerate(tiles):
                for part, half in enumerate(split2(result[:, at * TILE : (at + 1) * TILE])):
                    out_ref[t, part, parity * 256 : (parity + 1) * 256, :] = half
    edge_ref[...] = out_ref[(1 - rg_ref[0]) * (TILES - 1)]


def remap_block(starts_ref, weights_ref, rg, j, tile_at):
    for g in range(SLABS):
        at = starts_ref[g, rg * TILES + j] - rg * TILES
        window = []
        for part in range(2):
            for parity in range(2):
                for c in range(2):
                    row = parity * 256 + c * 128 + g * 32
                    rows = slice(row, row + 32)
                    window.append(jnp.concatenate([tile_at(at + n, part, rows) for n in range(2)], 1))
        both = mm(jnp.concatenate(window, 0), weights_ref[g, j])
        yield g, split2(both[:128] + both[128:])


def focus_rows(g):
    return [(parity, c * 128 + g * 32) for parity in range(2) for c in range(2)]


def inner_kernel(rg_ref, starts_ref, spectrum_ref, weights_ref, focus_ref):
    rg = rg_ref[0]
    for n in range(TILES - 1):
        j = n + rg
        for g, pair in remap_block(
            starts_ref, weights_ref, rg, j, lambda t, part, rows: spectrum_ref[t, part, rows, :]
        ):
            for part, half in enumerate(pair):
                for at, (parity, row) in enumerate(focus_rows(g)):
                    focus_ref[part, parity, n, row : row + 32, :] = half[at * 32 : (at + 1) * 32]


def outer_kernel(me_ref, rg_ref, starts_ref, spectrum_ref, halo_ref, weights_ref, table_ref, focus_ref, *refs):
    out_refs, window_ref = refs[:NDEV], refs[NDEV]
    me, rg = me_ref[0], rg_ref[0]
    first = 6 - 7 * rg
    window_ref[2 - 2 * rg] = halo_ref[...]
    for n in range(2):
        window_ref[rg + n] = spectrum_ref[(1 - rg) * 6 + n]
    face = [[[None] * 8 for _ in range(2)] for _ in range(2)]
    for g, pair in remap_block(
        starts_ref,
        weights_ref,
        rg,
        (1 - rg) * (TILES - 1),
        lambda t, part, rows: window_ref[t - first, part, rows, :],
    ):
        for part, half in enumerate(pair):
            for at, (parity, row) in enumerate(focus_rows(g)):
                face[part][parity][row // 32] = half[at * 32 : (at + 1) * 32]
    results = []
    for parity in range(2):
        pair = []
        for part in range(2):
            block = jnp.concatenate(face[part][parity], 0)
            inner = [focus_ref[part, parity, n] for n in range(TILES - 1)]
            pair.append(
                jnp.concatenate(
                    [jnp.where(rg == 1, block, inner[0])]
                    + [jnp.where(rg == 1, inner[n - 1], inner[n]) for n in range(1, TILES - 1)]
                    + [jnp.where(rg == 1, inner[-1], block)],
                    1,
                )
            )
        results.append(product3((table_ref[0, parity], table_ref[1, parity]), pair))
    even, odd = results[0], results[1] * sign_of(me)
    for i, out_ref in enumerate(out_refs):
        lines = even + odd if i < 4 else even - odd
        pieces = []
        for c in range(2):
            at = c * SIDE + (i % 4) * MLOC
            pieces.append((c * MLOC, lines[at : at + MLOC, :]))
        store_coded(out_ref, pieces)


def image_kernel(table_ref, *refs):
    in_refs, out_ref = in_order(refs[:NDEV], BACK_ORDER), refs[NDEV]
    scales = [load_scales(ref) for ref in in_refs]
    for tiles in tile_pairs(TILES):
        values = [load_columns(ref, scale, tiles) for ref, scale in zip(in_refs, scales)]
        for h in range(2):
            x = jnp.concatenate(
                [v[c * MLOC + h * HALF : c * MLOC + (h + 1) * HALF] for v in values for c in range(2)], 0
            )
            result = product3(table_ref, split2(x)).astype(BF16)
            for c in range(2):
                at = c * 256 + h * 128
                columns = slice(tiles[0] * TILE, (tiles[0] + 2) * TILE)
                out_ref[at : at + 128, columns] = result[c * 128 : (c + 1) * 128]


def vmem_call(kernel, name, out_shape, smem=0, vmem=0, scratch=()):
    return pl.pallas_call(
        kernel,
        name=name,
        out_shape=out_shape,
        in_specs=[pl.BlockSpec(memory_space=pltpu.SMEM)] * smem
        + [pl.BlockSpec(memory_space=pltpu.VMEM)] * vmem,
        out_specs=jax.tree.map(lambda _: pl.BlockSpec(memory_space=pltpu.VMEM), out_shape),
        scratch_shapes=scratch,
        compiler_params=pltpu.CompilerParams(vmem_limit_bytes=VMEM_LIMIT),
    )


def after(value, *others):
    return lax.optimization_barrier((value, *others))[0]


def exchange(messages, order):
    return [
        lax.ppermute(messages[i], "az", [(d, d ^ i) for d in range(NDEV)]) if i else messages[0]
        for i in order
    ]


def fast_body(raw, stolt_weights, band_start):
    me = lax.axis_index("az").astype(jnp.int32)[None]
    rg = lax.axis_index("rg").astype(jnp.int32)[None]
    bins = raw.shape[3]
    message = jax.ShapeDtypeStruct((TILES * ROWS + TAIL, TILE), jnp.int16)
    short = jnp.asarray(np.stack([table_pair(short_table(upper)) for upper in range(2)]))
    long_shape = jax.ShapeDtypeStruct((2, 2, LINES_DEV, LINES_DEV), BF16)

    sent = vmem_call(spread_kernel, "spread", [message] * NDEV, smem=1, vmem=2)(
        me, raw.reshape(LINES, bins), short
    )
    got = exchange(sent, OUT_ORDER)
    forward_table, inverse_table, image_table = vmem_call(
        tables_kernel,
        "tables",
        [long_shape, long_shape, jax.ShapeDtypeStruct((2, 256, 256), BF16)],
        smem=1,
        vmem=2,
    )(after(me, sent[0]), jnp.asarray(long_base()), short)

    spectrum, edge = vmem_call(
        forward_kernel,
        "forward",
        [jax.ShapeDtypeStruct((TILES, 2, LINES, TILE), BF16), jax.ShapeDtypeStruct((2, LINES, TILE), BF16)],
        smem=2,
        vmem=1 + NDEV,
    )(me, rg, forward_table, *got)
    halo = lax.ppermute(edge, "rg", [(0, 1), (1, 0)])
    focus = vmem_call(
        inner_kernel,
        "inner",
        jax.ShapeDtypeStruct((2, 2, TILES - 1, LINES_DEV, TILE), BF16),
        smem=2,
        vmem=2,
    )(rg, band_start, spectrum, stolt_weights)
    back = vmem_call(
        outer_kernel,
        "outer",
        [message] * NDEV,
        smem=3,
        vmem=5,
        scratch=[pltpu.VMEM((3, 2, LINES, TILE), BF16)],
    )(me, rg, band_start, spectrum, halo, stolt_weights, inverse_table, focus)
    lines = exchange(back, BACK_ORDER)
    image = vmem_call(image_kernel, "image", jax.ShapeDtypeStruct((LINES, bins), BF16), vmem=1 + NDEV)(
        image_table, *lines
    )
    return image.reshape(2, MLOC, NDEV, bins)


def body(raw, stolt_weights, band_start):
    fast = (
        lax.axis_size("az") == NDEV
        and lax.axis_size("rg") == 2
        and raw.shape[1:3] == (MLOC, NDEV)
        and raw.shape[3] == TILES * TILE
    )
    return (fast_body if fast else generic_body)(raw, stolt_weights, band_start)


def solution(mesh):
    placed = (P(None, ("frames", "az"), None, "rg"), P(None, "rg", None, None), P())
    return jax.shard_map(
        body,
        mesh=mesh,
        in_specs=placed,
        out_specs=P(None, ("frames", "az"), None, "rg"),
        check_vma=False,
    )
```

```python
import functools
import math

import jax
import jax.numpy as jnp
import numpy as np
from jax import lax
from jax.experimental import pallas as pl
from jax.experimental.pallas import tpu as pltpu
from jax.sharding import PartitionSpec as P

LINES_DEV = 256
SLABS = 4
TILE = 128
BF16 = jnp.bfloat16
F32 = jnp.float32
CODE_STEPS = 256.0
FULL = 32767.0


def with_halo(cells, sides, width):
    for axis, dim in sides:
        count = lax.axis_size(axis)
        ends = count - 1
        head = lax.slice_in_dim(cells, 0, width, axis=dim)
        tail = lax.slice_in_dim(cells, cells.shape[dim] - width, cells.shape[dim], axis=dim)
        cells = jnp.concatenate(
            [
                lax.ppermute(tail, axis, [(i, (i + 1) % count) for i in range(ends)]),
                cells,
                lax.ppermute(head, axis, [((i + 1) % count, i) for i in range(ends)]),
            ],
            axis=dim,
        )
    return cells


def dft_table(length, direction, factor):
    counter = jnp.arange(length, dtype=jnp.int32)
    product = counter[:, None] * counter[None, :] % length
    angles = product.astype(jnp.float32) * (2.0 * math.pi / length)
    cosine = jnp.cos(angles) * factor
    sines = jnp.sin(angles) * (factor * direction)
    return jnp.stack([jnp.stack([cosine, -sines], 1), jnp.stack([sines, cosine], 1)], 0)


def rotate(real_part, imag_part, phase_index, line_total, direction):
    angles = phase_index.astype(jnp.float32) * (2.0 * math.pi / line_total)
    cosine = jnp.cos(angles)
    sines = jnp.sin(angles) * direction
    return (real_part * cosine - imag_part * sines, imag_part * cosine + real_part * sines)


def stolt(slab_source, weights, starts, slab_rows):
    pieces = []
    for slab_index in range(weights.shape[0]):
        slab_data = slab_source[:, slab_index * slab_rows : (slab_index + 1) * slab_rows, :]

        def window_at(start_bin):
            return lax.dynamic_slice_in_dim(slab_data, start_bin, 256, 2)

        windows = jax.vmap(window_at)(starts[slab_index])
        remixed = jnp.einsum(
            "jcmb,jbo->cmjo",
            windows,
            weights[slab_index].astype(jnp.float32),
            precision=lax.Precision.HIGHEST,
        )
        pieces.append(remixed.reshape(2, slab_rows, -1))
    return jnp.concatenate(pieces, 1)


def generic_body(raw, stolt_weights, band_start):
    groups = lax.axis_size("az")
    az_index = lax.axis_index("az")
    rg_index = lax.axis_index("rg")
    part_lines = raw.shape[1]
    bin_count = raw.shape[3]
    line_total = LINES_DEV * groups
    short_forward = dft_table(groups, -1.0, 1.0 / math.sqrt(groups))
    spread = jnp.einsum(
        "dkcp,cmpr->dmkr", short_forward, raw.astype(jnp.float32), precision=lax.Precision.HIGHEST
    )
    line_index = az_index * part_lines + jnp.arange(part_lines, dtype=jnp.int32)
    freq_index = jnp.arange(groups, dtype=jnp.int32)
    phase_index = line_index[:, None] * freq_index[None, :] % line_total
    real_part, imag_part = rotate(spread[0], spread[1], phase_index[:, :, None], line_total, -1.0)
    twisted = jnp.stack([real_part, imag_part])
    long_forward = dft_table(LINES_DEV, -1.0, 1.0 / math.sqrt(LINES_DEV))
    spectrum = jnp.einsum(
        "dkcm,cmjr->dkjr",
        long_forward,
        lax.all_to_all(twisted, "az", split_axis=2, concat_axis=1, tiled=True),
        precision=lax.Precision.HIGHEST,
    )
    spectrum_rows = spectrum[:, :, 0, :]
    slab_rows = LINES_DEV // SLABS
    block_count = bin_count // 128
    padded = with_halo(spectrum_rows, (("rg", 2),), 128)
    local_band = lax.dynamic_slice_in_dim(band_start, rg_index * block_count, block_count, 1)
    starts = (local_band - rg_index * block_count) * 128 + 128
    remapped = stolt(padded, stolt_weights, starts, slab_rows)
    long_inverse = dft_table(LINES_DEV, 1.0, 1.0 / math.sqrt(LINES_DEV))
    lines_back = jnp.einsum(
        "dmck,ckr->dmr", long_inverse, remapped, precision=lax.Precision.HIGHEST
    )
    all_lines = jnp.arange(LINES_DEV, dtype=jnp.int32)
    back_index = all_lines * az_index % line_total
    real_part, imag_part = rotate(
        lines_back[0], lines_back[1], back_index[:, None], line_total, 1.0
    )
    unrolled = jnp.stack([real_part, imag_part])[:, :, None, :]
    short_inverse = dft_table(groups, 1.0, 1.0 / math.sqrt(groups))
    focused = jnp.einsum(
        "dpck,cmkr->dmpr",
        short_inverse,
        lax.all_to_all(unrolled, "az", split_axis=1, concat_axis=2, tiled=True),
        precision=lax.Precision.HIGHEST,
    )
    return focused.astype(jnp.bfloat16)


NDEV = 8
MLOC = LINES_DEV // NDEV
ROWS = 2 * MLOC
HALF = 16
TAIL = 8
TILES = 8
LINES = 2 * LINES_DEV
SIDE = LINES_DEV // 2
OUT_ORDER = (6, 2, 4, 5, 1, 3, 7, 0)
BACK_ORDER = (6, 2, 4, 5, 1, 3, 7, 0)
VMEM_LIMIT = 20 * 1024 * 1024


def split2(x):
    hi = x.astype(BF16)
    lo = (x - hi.astype(F32)).astype(BF16)
    return hi, lo


def mm(a, b):
    return jnp.dot(a, b, preferred_element_type=F32)


def product3(table, pair):
    return mm(table[0], pair[0]) + mm(table[0], pair[1]) + mm(table[1], pair[0])


def short_table(me):
    row = lax.broadcasted_iota(jnp.int32, (16, 256), 0)
    column = lax.broadcasted_iota(jnp.int32, (16, 256), 1)
    residue = (row // 2) ^ me
    quarter = row % 2 - column // 128
    turn = (residue * (2 * (column % 8) + me // 4) + 4 * quarter + 16) % 16
    value = jnp.cos(turn.astype(F32) * (2.0 * math.pi / 16))
    line = lax.broadcasted_iota(jnp.int32, (HALF, 256), 1) // 8 % HALF
    same = line == lax.broadcasted_iota(jnp.int32, (HALF, 256), 0)
    return jnp.concatenate([jnp.where(same, value[n : n + 1], 0.0) for n in range(16)], 0)


def long_base():
    k2 = np.arange(LINES_DEV).reshape(-1, 2).T.reshape(1, -1)
    angle = 2 * np.pi * (np.arange(SIDE).reshape(-1, 1) * k2 % LINES_DEV) / LINES_DEV
    return np.stack([np.cos(angle), np.sin(angle)]).astype(np.float32)


def rows_at(index, size):
    return pl.ds(pl.multiple_of(index * size, size), size)


def tiles_of(ref):
    return (ref.shape[-2] - TAIL) // ROWS


def store_coded(out_ref, pieces):
    tiles = tiles_of(out_ref)
    peak = None
    for _, value in pieces:
        top = jnp.max(jnp.abs(value), axis=0, keepdims=True)
        peak = top if peak is None else jnp.maximum(peak, top)
    code = jnp.ceil(jnp.log2(jnp.maximum(peak, 1e-30) * (1.0 / FULL)) * CODE_STEPS + 0.01)
    inverse = jnp.exp2(code * (-1.0 / CODE_STEPS))
    for row, value in pieces:
        coded = jnp.round(value * inverse).astype(jnp.int32).astype(jnp.int16)
        for tile in range(tiles):
            at = tile * ROWS + row
            out_ref[at : at + value.shape[0], :] = coded[:, tile * TILE : (tile + 1) * TILE]
    which = lax.broadcasted_iota(jnp.int32, (TAIL, TILE), 0)
    scales = jnp.zeros((TAIL, TILE), F32)
    for tile in range(tiles):
        scales = jnp.where(which == tile, code[:, tile * TILE : (tile + 1) * TILE], scales)
    out_ref[tiles * ROWS : tiles * ROWS + TAIL, :] = scales.astype(jnp.int32).astype(jnp.int16)


def load_scales(ref):
    at = tiles_of(ref) * ROWS
    code = ref[at : at + TAIL, :].astype(jnp.int32).astype(F32)
    return jnp.exp2(code * (1.0 / CODE_STEPS))


def load_columns(ref, scales, tiles):
    parts = []
    for t in tiles:
        value = ref[t * ROWS : (t + 1) * ROWS, :].astype(jnp.int32).astype(F32)
        parts.append(value * scales[t : t + 1, :])
    return jnp.concatenate(parts, 1)


def tile_pairs(tiles):
    return [(t, t + 1) for t in range(0, tiles, 2)]


def in_order(refs, order):
    return [refs[order.index(i)] for i in range(NDEV)]


def sign_of(me):
    return (1 - 2 * (me // 4)).astype(F32)


def spread_kernel(me_ref, x_ref, *out_refs):
    hi, lo = split2(short_table(me_ref[0]))
    halves = []
    for h in range(2):
        at = h * 128
        x = jnp.concatenate([x_ref[at : at + 128, :], x_ref[256 + at : 256 + at + 128, :]], 0)
        halves.append(mm(hi, x) + mm(lo, x))
    for n, out_ref in enumerate(out_refs):
        pieces = []
        for c in range(2):
            for h in range(2):
                at = n * 32 + c * HALF
                pieces.append((c * MLOC + h * HALF, halves[h][at : at + HALF, :]))
        store_coded(out_ref, pieces)


def tables_kernel(me_ref, band_ref, base_ref, forward_ref, inverse_ref, image_ref, starts_ref):
    me = me_ref[0]
    step = 2.0 * math.pi / (NDEV * LINES_DEV)
    blocks = []
    for i in range(4):
        slot = (me & 3) ^ i
        line = lax.broadcasted_iota(jnp.int32, (MLOC, TILE), 0) + slot * MLOC
        angle = (line * me).astype(F32) * step
        turn_cos, turn_sin = jnp.cos(angle) * (1.0 / 64.0), jnp.sin(angle) * (1.0 / 64.0)
        cosine, sine = [base_ref[n, rows_at(slot, MLOC), :] for n in range(2)]
        turn_cos = jnp.concatenate([turn_cos, turn_cos], 1)
        turn_sin = jnp.concatenate([turn_sin, turn_sin], 1)
        blocks.append((cosine * turn_cos - sine * turn_sin, sine * turn_cos + cosine * turn_sin))
    whole = [jnp.concatenate([b[n] for b in blocks], 0) for n in range(2)]
    for parity in range(2):
        co, si = [w[:, parity * SIDE : (parity + 1) * SIDE] for w in whole]
        inverse = jnp.concatenate([jnp.concatenate([co, -si], 1), jnp.concatenate([si, co], 1)], 0)
        ct, st = co.T * 2.0, si.T * 2.0
        forward = jnp.concatenate([jnp.concatenate([ct, st], 1), jnp.concatenate([-st, ct], 1)], 0)
        for ref, value in ((inverse_ref, inverse), (forward_ref, forward)):
            ref[0, parity], ref[1, parity] = split2(value)
    image_ref[0], image_ref[1] = split2(short_table(me).T)
    starts_ref[...] = band_ref[...]


def forward_kernel(me_ref, rg_ref, table_ref, *refs):
    in_refs, (out_ref, edge_ref) = in_order(refs[:NDEV], OUT_ORDER), refs[NDEV:]
    sign = sign_of(me_ref[0])
    scales = [load_scales(ref) for ref in in_refs]
    for tiles in tile_pairs(TILES):
        values = [load_columns(ref, scale, tiles) for ref, scale in zip(in_refs, scales)]
        sums = [values[i] + values[i + 4] for i in range(4)]
        gaps = [(values[i] - values[i + 4]) * sign for i in range(4)]
        for parity, lines in enumerate((sums, gaps)):
            lines = jnp.concatenate([v[:MLOC] for v in lines] + [v[MLOC:] for v in lines], 0)
            result = product3((table_ref[0, parity], table_ref[1, parity]), split2(lines))
            for at, t in enumerate(tiles):
                for part, half in enumerate(split2(result[:, at * TILE : (at + 1) * TILE])):
                    out_ref[t, part, parity * 256 : (parity + 1) * 256, :] = half
    edge_ref[...] = out_ref[(1 - rg_ref[0]) * (TILES - 1)]


def remap_block(starts_ref, weights_ref, rg, j, tile_at):
    for g in range(SLABS):
        at = starts_ref[g, rg * TILES + j] - rg * TILES
        window = []
        for part in range(2):
            for parity in range(2):
                for c in range(2):
                    row = parity * 256 + c * 128 + g * 32
                    rows = slice(row, row + 32)
                    window.append(jnp.concatenate([tile_at(at + n, part, rows) for n in range(2)], 1))
        both = mm(jnp.concatenate(window, 0), weights_ref[g, j])
        yield g, split2(both[:128] + both[128:])


def focus_rows(g):
    return [(parity, c * 128 + g * 32) for parity in range(2) for c in range(2)]


def inner_kernel(rg_ref, starts_ref, spectrum_ref, weights_ref, focus_ref):
    rg = rg_ref[0]
    for n in range(TILES - 1):
        j = n + rg
        for g, pair in remap_block(
            starts_ref, weights_ref, rg, j, lambda t, part, rows: spectrum_ref[t, part, rows, :]
        ):
            for part, half in enumerate(pair):
                for at, (parity, row) in enumerate(focus_rows(g)):
                    focus_ref[part, parity, n, row : row + 32, :] = half[at * 32 : (at + 1) * 32]


def outer_kernel(me_ref, rg_ref, starts_ref, spectrum_ref, halo_ref, weights_ref, table_ref, focus_ref, *refs):
    out_refs, window_ref = refs[:NDEV], refs[NDEV]
    me, rg = me_ref[0], rg_ref[0]
    first = 6 - 7 * rg
    window_ref[2 - 2 * rg] = halo_ref[...]
    for n in range(2):
        window_ref[rg + n] = spectrum_ref[(1 - rg) * 6 + n]
    face = [[[None] * 8 for _ in range(2)] for _ in range(2)]
    for g, pair in remap_block(
        starts_ref,
        weights_ref,
        rg,
        (1 - rg) * (TILES - 1),
        lambda t, part, rows: window_ref[t - first, part, rows, :],
    ):
        for part, half in enumerate(pair):
            for at, (parity, row) in enumerate(focus_rows(g)):
                face[part][parity][row // 32] = half[at * 32 : (at + 1) * 32]
    results = []
    for parity in range(2):
        pair = []
        for part in range(2):
            block = jnp.concatenate(face[part][parity], 0)
            inner = [focus_ref[part, parity, n] for n in range(TILES - 1)]
            pair.append(
                jnp.concatenate(
                    [jnp.where(rg == 1, block, inner[0])]
                    + [jnp.where(rg == 1, inner[n - 1], inner[n]) for n in range(1, TILES - 1)]
                    + [jnp.where(rg == 1, inner[-1], block)],
                    1,
                )
            )
        results.append(product3((table_ref[0, parity], table_ref[1, parity]), pair))
    even, odd = results[0], results[1] * sign_of(me)
    for i, out_ref in enumerate(out_refs):
        lines = even + odd if i < 4 else even - odd
        pieces = []
        for c in range(2):
            at = c * SIDE + (i % 4) * MLOC
            pieces.append((c * MLOC, lines[at : at + MLOC, :]))
        store_coded(out_ref, pieces)


def image_kernel(table_ref, *refs):
    in_refs, out_ref = in_order(refs[:NDEV], BACK_ORDER), refs[NDEV]
    scales = [load_scales(ref) for ref in in_refs]
    for tiles in tile_pairs(TILES):
        values = [load_columns(ref, scale, tiles) for ref, scale in zip(in_refs, scales)]
        for h in range(2):
            x = jnp.concatenate(
                [v[c * MLOC + h * HALF : c * MLOC + (h + 1) * HALF] for v in values for c in range(2)], 0
            )
            result = product3(table_ref, split2(x)).astype(BF16)
            for c in range(2):
                at = c * 256 + h * 128
                columns = slice(tiles[0] * TILE, (tiles[0] + 2) * TILE)
                out_ref[at : at + 128, columns] = result[c * 128 : (c + 1) * 128]


def vmem_call(kernel, name, out_shape, smem=0, vmem=0, scratch=()):
    return pl.pallas_call(
        kernel,
        name=name,
        out_shape=out_shape,
        in_specs=[pl.BlockSpec(memory_space=pltpu.SMEM)] * smem
        + [pl.BlockSpec(memory_space=pltpu.VMEM)] * vmem,
        out_specs=jax.tree.map(lambda _: pl.BlockSpec(memory_space=pltpu.VMEM), out_shape),
        scratch_shapes=scratch,
        compiler_params=pltpu.CompilerParams(vmem_limit_bytes=VMEM_LIMIT),
    )


def after(value, *others):
    return lax.optimization_barrier((value, *others))[0]


def exchange(messages, order):
    return [
        lax.ppermute(messages[i], "az", [(d, d ^ i) for d in range(NDEV)]) if i else messages[0]
        for i in order
    ]


def fast_body(raw, stolt_weights, band_start):
    me = lax.axis_index("az").astype(jnp.int32)[None]
    rg = lax.axis_index("rg").astype(jnp.int32)[None]
    bins = raw.shape[3]
    message = jax.ShapeDtypeStruct((TILES * ROWS + TAIL, TILE), jnp.int16)
    long_shape = jax.ShapeDtypeStruct((2, 2, LINES_DEV, LINES_DEV), BF16)

    sent = vmem_call(spread_kernel, "spread", [message] * NDEV, smem=1, vmem=1)(
        me, raw.reshape(LINES, bins)
    )
    got = exchange(sent, OUT_ORDER)
    forward_table, inverse_table, image_table, starts = vmem_call(
        tables_kernel,
        "tables",
        [
            long_shape,
            long_shape,
            jax.ShapeDtypeStruct((2, 256, 256), BF16),
            jax.ShapeDtypeStruct(band_start.shape, band_start.dtype),
        ],
        smem=1,
        vmem=2,
    )(after(me, sent[0]), band_start, jnp.asarray(long_base()))

    spectrum, edge = vmem_call(
        forward_kernel,
        "forward",
        [jax.ShapeDtypeStruct((TILES, 2, LINES, TILE), BF16), jax.ShapeDtypeStruct((2, LINES, TILE), BF16)],
        smem=2,
        vmem=1 + NDEV,
    )(me, rg, forward_table, *got)
    halo = lax.ppermute(edge, "rg", [(0, 1), (1, 0)])
    focus = vmem_call(
        inner_kernel,
        "inner",
        jax.ShapeDtypeStruct((2, 2, TILES - 1, LINES_DEV, TILE), BF16),
        smem=2,
        vmem=2,
    )(rg, starts, spectrum, stolt_weights)
    back = vmem_call(
        outer_kernel,
        "outer",
        [message] * NDEV,
        smem=3,
        vmem=5,
        scratch=[pltpu.VMEM((3, 2, LINES, TILE), BF16)],
    )(me, rg, starts, spectrum, halo, stolt_weights, inverse_table, focus)
    lines = exchange(back, BACK_ORDER)
    image = vmem_call(image_kernel, "image", jax.ShapeDtypeStruct((LINES, bins), BF16), vmem=1 + NDEV)(
        image_table, *lines
    )
    return image.reshape(2, MLOC, NDEV, bins)


def body(raw, stolt_weights, band_start):
    fast = (
        lax.axis_size("az") == NDEV
        and lax.axis_size("rg") == 2
        and raw.shape[1:3] == (MLOC, NDEV)
        and raw.shape[3] == TILES * TILE
    )
    return (fast_body if fast else generic_body)(raw, stolt_weights, band_start)


def solution(mesh):
    placed = (P(None, ("frames", "az"), None, "rg"), P(None, "rg", None, None), P())
    return jax.shard_map(
        body,
        mesh=mesh,
        in_specs=placed,
        out_specs=P(None, ("frames", "az"), None, "rg"),
        check_vma=False,
    )
```

```python
import functools
import math

import jax
import jax.numpy as jnp
import numpy as np
from jax import lax
from jax.experimental import pallas as pl
from jax.experimental.pallas import tpu as pltpu
from jax.sharding import PartitionSpec as P

LINES_DEV = 256
SLABS = 4
TILE = 128
BF16 = jnp.bfloat16
F32 = jnp.float32
CODE_STEPS = 256.0
FULL = 32767.0


def with_halo(cells, sides, width):
    for axis, dim in sides:
        count = lax.axis_size(axis)
        ends = count - 1
        head = lax.slice_in_dim(cells, 0, width, axis=dim)
        tail = lax.slice_in_dim(cells, cells.shape[dim] - width, cells.shape[dim], axis=dim)
        cells = jnp.concatenate(
            [
                lax.ppermute(tail, axis, [(i, (i + 1) % count) for i in range(ends)]),
                cells,
                lax.ppermute(head, axis, [((i + 1) % count, i) for i in range(ends)]),
            ],
            axis=dim,
        )
    return cells


def dft_table(length, direction, factor):
    counter = jnp.arange(length, dtype=jnp.int32)
    product = counter[:, None] * counter[None, :] % length
    angles = product.astype(jnp.float32) * (2.0 * math.pi / length)
    cosine = jnp.cos(angles) * factor
    sines = jnp.sin(angles) * (factor * direction)
    return jnp.stack([jnp.stack([cosine, -sines], 1), jnp.stack([sines, cosine], 1)], 0)


def rotate(real_part, imag_part, phase_index, line_total, direction):
    angles = phase_index.astype(jnp.float32) * (2.0 * math.pi / line_total)
    cosine = jnp.cos(angles)
    sines = jnp.sin(angles) * direction
    return (real_part * cosine - imag_part * sines, imag_part * cosine + real_part * sines)


def stolt(slab_source, weights, starts, slab_rows):
    pieces = []
    for slab_index in range(weights.shape[0]):
        slab_data = slab_source[:, slab_index * slab_rows : (slab_index + 1) * slab_rows, :]

        def window_at(start_bin):
            return lax.dynamic_slice_in_dim(slab_data, start_bin, 256, 2)

        windows = jax.vmap(window_at)(starts[slab_index])
        remixed = jnp.einsum(
            "jcmb,jbo->cmjo",
            windows,
            weights[slab_index].astype(jnp.float32),
            precision=lax.Precision.HIGHEST,
        )
        pieces.append(remixed.reshape(2, slab_rows, -1))
    return jnp.concatenate(pieces, 1)


def generic_body(raw, stolt_weights, band_start):
    groups = lax.axis_size("az")
    az_index = lax.axis_index("az")
    rg_index = lax.axis_index("rg")
    part_lines = raw.shape[1]
    bin_count = raw.shape[3]
    line_total = LINES_DEV * groups
    short_forward = dft_table(groups, -1.0, 1.0 / math.sqrt(groups))
    spread = jnp.einsum(
        "dkcp,cmpr->dmkr", short_forward, raw.astype(jnp.float32), precision=lax.Precision.HIGHEST
    )
    line_index = az_index * part_lines + jnp.arange(part_lines, dtype=jnp.int32)
    freq_index = jnp.arange(groups, dtype=jnp.int32)
    phase_index = line_index[:, None] * freq_index[None, :] % line_total
    real_part, imag_part = rotate(spread[0], spread[1], phase_index[:, :, None], line_total, -1.0)
    twisted = jnp.stack([real_part, imag_part])
    long_forward = dft_table(LINES_DEV, -1.0, 1.0 / math.sqrt(LINES_DEV))
    spectrum = jnp.einsum(
        "dkcm,cmjr->dkjr",
        long_forward,
        lax.all_to_all(twisted, "az", split_axis=2, concat_axis=1, tiled=True),
        precision=lax.Precision.HIGHEST,
    )
    spectrum_rows = spectrum[:, :, 0, :]
    slab_rows = LINES_DEV // SLABS
    block_count = bin_count // 128
    padded = with_halo(spectrum_rows, (("rg", 2),), 128)
    local_band = lax.dynamic_slice_in_dim(band_start, rg_index * block_count, block_count, 1)
    starts = (local_band - rg_index * block_count) * 128 + 128
    remapped = stolt(padded, stolt_weights, starts, slab_rows)
    long_inverse = dft_table(LINES_DEV, 1.0, 1.0 / math.sqrt(LINES_DEV))
    lines_back = jnp.einsum(
        "dmck,ckr->dmr", long_inverse, remapped, precision=lax.Precision.HIGHEST
    )
    all_lines = jnp.arange(LINES_DEV, dtype=jnp.int32)
    back_index = all_lines * az_index % line_total
    real_part, imag_part = rotate(
        lines_back[0], lines_back[1], back_index[:, None], line_total, 1.0
    )
    unrolled = jnp.stack([real_part, imag_part])[:, :, None, :]
    short_inverse = dft_table(groups, 1.0, 1.0 / math.sqrt(groups))
    focused = jnp.einsum(
        "dpck,cmkr->dmpr",
        short_inverse,
        lax.all_to_all(unrolled, "az", split_axis=1, concat_axis=2, tiled=True),
        precision=lax.Precision.HIGHEST,
    )
    return focused.astype(jnp.bfloat16)


NDEV = 8
MLOC = LINES_DEV // NDEV
ROWS = 2 * MLOC
HALF = 16
TAIL = 8
TILES = 8
LINES = 2 * LINES_DEV
SIDE = LINES_DEV // 2
EARLY = (6, 2, 4, 5, 1, 0)
LATE = (3, 7)
EARLY_ROWS = 192
VMEM_LIMIT = 20 * 1024 * 1024


def split2(x):
    hi = x.astype(BF16)
    lo = (x - hi.astype(F32)).astype(BF16)
    return hi, lo


def mm(a, b):
    return jnp.dot(a, b, preferred_element_type=F32)


def product3(table, pair):
    return mm(table[0], pair[0]) + mm(table[0], pair[1]) + mm(table[1], pair[0])


def short_table(me):
    row = lax.broadcasted_iota(jnp.int32, (16, 256), 0)
    column = lax.broadcasted_iota(jnp.int32, (16, 256), 1)
    residue = (row // 2) ^ me
    quarter = row % 2 - column // 128
    turn = (residue * (2 * (column % 8) + me // 4) + 4 * quarter + 16) % 16
    value = jnp.cos(turn.astype(F32) * (2.0 * math.pi / 16))
    line = lax.broadcasted_iota(jnp.int32, (HALF, 256), 1) // 8 % HALF
    same = line == lax.broadcasted_iota(jnp.int32, (HALF, 256), 0)
    return jnp.concatenate([jnp.where(same, value[n : n + 1], 0.0) for n in range(16)], 0)


def long_base():
    k2 = np.arange(LINES_DEV).reshape(-1, 2).T.reshape(1, -1)
    angle = 2 * np.pi * (np.arange(SIDE).reshape(-1, 1) * k2 % LINES_DEV) / LINES_DEV
    return np.stack([np.cos(angle), np.sin(angle)]).astype(np.float32)


def rows_at(index, size):
    return pl.ds(pl.multiple_of(index * size, size), size)


def tiles_of(ref):
    return (ref.shape[-2] - TAIL) // ROWS


def store_coded(out_ref, pieces):
    tiles = tiles_of(out_ref)
    peak = None
    for _, value in pieces:
        top = jnp.max(jnp.abs(value), axis=0, keepdims=True)
        peak = top if peak is None else jnp.maximum(peak, top)
    code = jnp.ceil(jnp.log2(jnp.maximum(peak, 1e-30) * (1.0 / FULL)) * CODE_STEPS + 0.01)
    inverse = jnp.exp2(code * (-1.0 / CODE_STEPS))
    for row, value in pieces:
        coded = jnp.round(value * inverse).astype(jnp.int32).astype(jnp.int16)
        for tile in range(tiles):
            at = tile * ROWS + row
            out_ref[at : at + value.shape[0], :] = coded[:, tile * TILE : (tile + 1) * TILE]
    which = lax.broadcasted_iota(jnp.int32, (TAIL, TILE), 0)
    scales = jnp.zeros((TAIL, TILE), F32)
    for tile in range(tiles):
        scales = jnp.where(which == tile, code[:, tile * TILE : (tile + 1) * TILE], scales)
    out_ref[tiles * ROWS : tiles * ROWS + TAIL, :] = scales.astype(jnp.int32).astype(jnp.int16)


def load_scales(ref):
    at = tiles_of(ref) * ROWS
    code = ref[at : at + TAIL, :].astype(jnp.int32).astype(F32)
    return jnp.exp2(code * (1.0 / CODE_STEPS))


def load_columns(ref, scales, tiles):
    parts = []
    for t in tiles:
        value = ref[t * ROWS : (t + 1) * ROWS, :].astype(jnp.int32).astype(F32)
        parts.append(value * scales[t : t + 1, :])
    return jnp.concatenate(parts, 1)


def tile_pairs(tiles):
    return [(t, t + 1) for t in range(0, tiles, 2)]


def stacked3(pair):
    return jnp.concatenate([pair[0], pair[1], pair[0]], 0)


def late_table(rows):
    hi, lo = (v.astype(F32) for v in split2(rows))
    return jnp.concatenate([hi, hi, lo], 0).T.astype(BF16)


def sign_of(me):
    return (1 - 2 * (me // 4)).astype(F32)


def spread_kernel(me_ref, x_ref, *out_refs):
    hi, lo = split2(short_table(me_ref[0]))
    halves = []
    for h in range(2):
        at = h * 128
        x = jnp.concatenate([x_ref[at : at + 128, :], x_ref[256 + at : 256 + at + 128, :]], 0)
        halves.append(mm(hi, x) + mm(lo, x))
    for n, out_ref in enumerate(out_refs):
        pieces = []
        for c in range(2):
            for h in range(2):
                at = n * 32 + c * HALF
                pieces.append((c * MLOC + h * HALF, halves[h][at : at + HALF, :]))
        store_coded(out_ref, pieces)


def tables_kernel(me_ref, band_ref, base_ref, *refs):
    forward_ref, forward_late_ref, inverse_ref, image_ref, image_late_ref, starts_ref = refs
    me = me_ref[0]
    step = 2.0 * math.pi / (NDEV * LINES_DEV)
    blocks = []
    for i in range(4):
        slot = (me & 3) ^ i
        line = lax.broadcasted_iota(jnp.int32, (MLOC, TILE), 0) + slot * MLOC
        angle = (line * me).astype(F32) * step
        turn_cos, turn_sin = jnp.cos(angle) * (1.0 / 64.0), jnp.sin(angle) * (1.0 / 64.0)
        cosine, sine = [base_ref[n, rows_at(slot, MLOC), :] for n in range(2)]
        turn_cos = jnp.concatenate([turn_cos, turn_cos], 1)
        turn_sin = jnp.concatenate([turn_sin, turn_sin], 1)
        blocks.append((cosine * turn_cos - sine * turn_sin, sine * turn_cos + cosine * turn_sin))
    whole = [jnp.concatenate([b[n] for b in blocks], 0) for n in range(2)]
    for parity in range(2):
        co, si = [w[:, parity * SIDE : (parity + 1) * SIDE] for w in whole]
        inverse = jnp.concatenate([jnp.concatenate([co, -si], 1), jnp.concatenate([si, co], 1)], 0)
        inverse_ref[0, parity], inverse_ref[1, parity] = split2(inverse)
        early = jnp.concatenate([inverse[:96], inverse[128:224]], 0).T * 2.0
        forward_ref[0, parity], forward_ref[1, parity] = split2(early)
        forward_late_ref[parity] = late_table(jnp.concatenate([inverse[96:128], inverse[224:]], 0) * 2.0)
    short = short_table(me)
    early, late = [
        jnp.concatenate([short[i * 32 : (i + 1) * 32] for i in which], 0) for which in (EARLY, LATE)
    ]
    image_ref[0], image_ref[1] = split2(early.T)
    image_late_ref[...] = late_table(late)
    starts_ref[...] = band_ref[...]


def side_lines(values, pairs, sign):
    sums = [values[i] + values[i + 4] for i in pairs]
    gaps = [(values[i] - values[i + 4]) * sign for i in pairs]
    for lines in (sums, gaps):
        yield split2(jnp.concatenate([v[:MLOC] for v in lines] + [v[MLOC:] for v in lines], 0))


def forward_early_kernel(me_ref, table_ref, *refs):
    in_refs, sum_ref = dict(zip(EARLY, refs)), refs[len(EARLY)]
    sign = sign_of(me_ref[0])
    scales = {i: load_scales(ref) for i, ref in in_refs.items()}
    for tiles in tile_pairs(TILES):
        values = {i: load_columns(ref, scales[i], tiles) for i, ref in in_refs.items()}
        for parity, pair in enumerate(side_lines(values, (0, 1, 2), sign)):
            columns = slice(tiles[0] * TILE, (tiles[0] + 2) * TILE)
            sum_ref[parity, :, columns] = product3((table_ref[0, parity], table_ref[1, parity]), pair)


def forward_kernel(me_ref, rg_ref, table_ref, sum_ref, *refs):
    in_refs, (out_ref, edge_ref) = dict(zip(LATE, refs)), refs[len(LATE) :]
    sign = sign_of(me_ref[0])
    scales = {i: load_scales(ref) for i, ref in in_refs.items()}
    for tiles in tile_pairs(TILES):
        values = {i: load_columns(ref, scales[i], tiles) for i, ref in in_refs.items()}
        for parity, pair in enumerate(side_lines(values, (3,), sign)):
            columns = slice(tiles[0] * TILE, (tiles[0] + 2) * TILE)
            result = sum_ref[parity, :, columns] + mm(table_ref[parity], stacked3(pair))
            for at, t in enumerate(tiles):
                for part, half in enumerate(split2(result[:, at * TILE : (at + 1) * TILE])):
                    out_ref[t, part, parity * 256 : (parity + 1) * 256, :] = half
    edge_ref[...] = out_ref[(1 - rg_ref[0]) * (TILES - 1)]


def remap_block(starts_ref, weights_ref, rg, j, tile_at):
    for g in range(SLABS):
        at = starts_ref[g, rg * TILES + j] - rg * TILES
        window = []
        for part in range(2):
            for parity in range(2):
                for c in range(2):
                    row = parity * 256 + c * 128 + g * 32
                    rows = slice(row, row + 32)
                    window.append(jnp.concatenate([tile_at(at + n, part, rows) for n in range(2)], 1))
        both = mm(jnp.concatenate(window, 0), weights_ref[g, j])
        yield g, split2(both[:128] + both[128:])


def focus_rows(g):
    return [(parity, c * 128 + g * 32) for parity in range(2) for c in range(2)]


def inner_kernel(rg_ref, starts_ref, spectrum_ref, weights_ref, focus_ref):
    rg = rg_ref[0]
    for n in range(TILES - 1):
        j = n + rg
        for g, pair in remap_block(
            starts_ref, weights_ref, rg, j, lambda t, part, rows: spectrum_ref[t, part, rows, :]
        ):
            for part, half in enumerate(pair):
                for at, (parity, row) in enumerate(focus_rows(g)):
                    focus_ref[part, parity, n, row : row + 32, :] = half[at * 32 : (at + 1) * 32]


def outer_kernel(me_ref, rg_ref, starts_ref, spectrum_ref, halo_ref, weights_ref, table_ref, focus_ref, *refs):
    out_refs, window_ref = refs[:NDEV], refs[NDEV]
    me, rg = me_ref[0], rg_ref[0]
    first = 6 - 7 * rg
    window_ref[2 - 2 * rg] = halo_ref[...]
    for n in range(2):
        window_ref[rg + n] = spectrum_ref[(1 - rg) * 6 + n]
    face = [[[None] * 8 for _ in range(2)] for _ in range(2)]
    for g, pair in remap_block(
        starts_ref,
        weights_ref,
        rg,
        (1 - rg) * (TILES - 1),
        lambda t, part, rows: window_ref[t - first, part, rows, :],
    ):
        for part, half in enumerate(pair):
            for at, (parity, row) in enumerate(focus_rows(g)):
                face[part][parity][row // 32] = half[at * 32 : (at + 1) * 32]
    results = []
    for parity in range(2):
        pair = []
        for part in range(2):
            block = jnp.concatenate(face[part][parity], 0)
            inner = [focus_ref[part, parity, n] for n in range(TILES - 1)]
            pair.append(
                jnp.concatenate(
                    [jnp.where(rg == 1, block, inner[0])]
                    + [jnp.where(rg == 1, inner[n - 1], inner[n]) for n in range(1, TILES - 1)]
                    + [jnp.where(rg == 1, inner[-1], block)],
                    1,
                )
            )
        results.append(product3((table_ref[0, parity], table_ref[1, parity]), pair))
    even, odd = results[0], results[1] * sign_of(me)
    for i, out_ref in enumerate(out_refs):
        lines = even + odd if i < 4 else even - odd
        pieces = []
        for c in range(2):
            at = c * SIDE + (i % 4) * MLOC
            pieces.append((c * MLOC, lines[at : at + MLOC, :]))
        store_coded(out_ref, pieces)


def image_lines(values, h):
    rows = [v[c * MLOC + h * HALF : c * MLOC + (h + 1) * HALF] for v in values for c in range(2)]
    return split2(jnp.concatenate(rows, 0))


def image_early_kernel(table_ref, *refs):
    in_refs, sum_ref = refs[: len(EARLY)], refs[len(EARLY)]
    scales = [load_scales(ref) for ref in in_refs]
    for tiles in tile_pairs(TILES):
        values = [load_columns(ref, scale, tiles) for ref, scale in zip(in_refs, scales)]
        for h in range(2):
            columns = slice(tiles[0] * TILE, (tiles[0] + 2) * TILE)
            sum_ref[h, :, columns] = product3(table_ref, image_lines(values, h))


def image_kernel(table_ref, sum_ref, *refs):
    in_refs, out_ref = refs[: len(LATE)], refs[len(LATE)]
    scales = [load_scales(ref) for ref in in_refs]
    for tiles in tile_pairs(TILES):
        values = [load_columns(ref, scale, tiles) for ref, scale in zip(in_refs, scales)]
        for h in range(2):
            columns = slice(tiles[0] * TILE, (tiles[0] + 2) * TILE)
            result = sum_ref[h, :, columns] + mm(table_ref[...], stacked3(image_lines(values, h)))
            for c in range(2):
                at = c * 256 + h * 128
                out_ref[at : at + 128, columns] = result[c * 128 : (c + 1) * 128].astype(BF16)


def vmem_call(kernel, name, out_shape, smem=0, vmem=0, scratch=()):
    return pl.pallas_call(
        kernel,
        name=name,
        out_shape=out_shape,
        in_specs=[pl.BlockSpec(memory_space=pltpu.SMEM)] * smem
        + [pl.BlockSpec(memory_space=pltpu.VMEM)] * vmem,
        out_specs=jax.tree.map(lambda _: pl.BlockSpec(memory_space=pltpu.VMEM), out_shape),
        scratch_shapes=scratch,
        compiler_params=pltpu.CompilerParams(vmem_limit_bytes=VMEM_LIMIT),
    )


def after(value, *others):
    return lax.optimization_barrier((value, *others))[0]


def exchange(messages):
    return [
        [
            lax.ppermute(messages[i], "az", [(d, d ^ i) for d in range(NDEV)]) if i else messages[0]
            for i in which
        ]
        for which in (EARLY, LATE)
    ]


def fast_body(raw, stolt_weights, band_start):
    me = lax.axis_index("az").astype(jnp.int32)[None]
    rg = lax.axis_index("rg").astype(jnp.int32)[None]
    bins = raw.shape[3]
    message = jax.ShapeDtypeStruct((TILES * ROWS + TAIL, TILE), jnp.int16)
    early_shape = (2, LINES_DEV, EARLY_ROWS)

    sent = vmem_call(spread_kernel, "spread", [message] * NDEV, smem=1, vmem=1)(
        me, raw.reshape(LINES, bins)
    )
    got_early, got_late = exchange(sent)
    forward_table, forward_late, inverse_table, image_table, image_late, starts = vmem_call(
        tables_kernel,
        "tables",
        [
            jax.ShapeDtypeStruct((2,) + early_shape, BF16),
            jax.ShapeDtypeStruct(early_shape, BF16),
            jax.ShapeDtypeStruct((2, 2, LINES_DEV, LINES_DEV), BF16),
            jax.ShapeDtypeStruct((2, 256, EARLY_ROWS), BF16),
            jax.ShapeDtypeStruct((256, EARLY_ROWS), BF16),
            jax.ShapeDtypeStruct(band_start.shape, band_start.dtype),
        ],
        smem=1,
        vmem=2,
    )(after(me, sent[0]), band_start, jnp.asarray(long_base()))

    partial = vmem_call(
        forward_early_kernel,
        "forward_early",
        jax.ShapeDtypeStruct((2, LINES_DEV, bins), F32),
        smem=1,
        vmem=1 + len(EARLY),
    )(me, forward_table, *got_early)
    spectrum, edge = vmem_call(
        forward_kernel,
        "forward",
        [jax.ShapeDtypeStruct((TILES, 2, LINES, TILE), BF16), jax.ShapeDtypeStruct((2, LINES, TILE), BF16)],
        smem=2,
        vmem=2 + len(LATE),
    )(me, rg, forward_late, partial, *got_late)
    halo = lax.ppermute(edge, "rg", [(0, 1), (1, 0)])
    focus = vmem_call(
        inner_kernel,
        "inner",
        jax.ShapeDtypeStruct((2, 2, TILES - 1, LINES_DEV, TILE), BF16),
        smem=2,
        vmem=2,
    )(rg, starts, spectrum, stolt_weights)
    back = vmem_call(
        outer_kernel,
        "outer",
        [message] * NDEV,
        smem=3,
        vmem=5,
        scratch=[pltpu.VMEM((3, 2, LINES, TILE), BF16)],
    )(me, rg, starts, spectrum, halo, stolt_weights, inverse_table, focus)
    early_lines, late_lines = exchange(back)
    image_sum = vmem_call(
        image_early_kernel, "image_early", jax.ShapeDtypeStruct((2, 256, bins), F32), vmem=1 + len(EARLY)
    )(image_table, *early_lines)
    image = vmem_call(
        image_kernel, "image", jax.ShapeDtypeStruct((LINES, bins), BF16), vmem=2 + len(LATE)
    )(image_late, image_sum, *late_lines)
    return image.reshape(2, MLOC, NDEV, bins)


def body(raw, stolt_weights, band_start):
    fast = (
        lax.axis_size("az") == NDEV
        and lax.axis_size("rg") == 2
        and raw.shape[1:3] == (MLOC, NDEV)
        and raw.shape[3] == TILES * TILE
    )
    return (fast_body if fast else generic_body)(raw, stolt_weights, band_start)


def solution(mesh):
    placed = (P(None, ("frames", "az"), None, "rg"), P(None, "rg", None, None), P())
    return jax.shard_map(
        body,
        mesh=mesh,
        in_specs=placed,
        out_specs=P(None, ("frames", "az"), None, "rg"),
        check_vma=False,
    )
```

```python
import functools
import math

import jax
import jax.numpy as jnp
import numpy as np
from jax import lax
from jax.experimental import pallas as pl
from jax.experimental.pallas import tpu as pltpu
from jax.sharding import PartitionSpec as P

LINES_DEV = 256
SLABS = 4
TILE = 128
BF16 = jnp.bfloat16
F32 = jnp.float32
CODE_STEPS = 256.0
FULL = 32767.0


def with_halo(cells, sides, width):
    for axis, dim in sides:
        count = lax.axis_size(axis)
        ends = count - 1
        head = lax.slice_in_dim(cells, 0, width, axis=dim)
        tail = lax.slice_in_dim(cells, cells.shape[dim] - width, cells.shape[dim], axis=dim)
        cells = jnp.concatenate(
            [
                lax.ppermute(tail, axis, [(i, (i + 1) % count) for i in range(ends)]),
                cells,
                lax.ppermute(head, axis, [((i + 1) % count, i) for i in range(ends)]),
            ],
            axis=dim,
        )
    return cells


def dft_table(length, direction, factor):
    counter = jnp.arange(length, dtype=jnp.int32)
    product = counter[:, None] * counter[None, :] % length
    angles = product.astype(jnp.float32) * (2.0 * math.pi / length)
    cosine = jnp.cos(angles) * factor
    sines = jnp.sin(angles) * (factor * direction)
    return jnp.stack([jnp.stack([cosine, -sines], 1), jnp.stack([sines, cosine], 1)], 0)


def rotate(real_part, imag_part, phase_index, line_total, direction):
    angles = phase_index.astype(jnp.float32) * (2.0 * math.pi / line_total)
    cosine = jnp.cos(angles)
    sines = jnp.sin(angles) * direction
    return (real_part * cosine - imag_part * sines, imag_part * cosine + real_part * sines)


def stolt(slab_source, weights, starts, slab_rows):
    pieces = []
    for slab_index in range(weights.shape[0]):
        slab_data = slab_source[:, slab_index * slab_rows : (slab_index + 1) * slab_rows, :]

        def window_at(start_bin):
            return lax.dynamic_slice_in_dim(slab_data, start_bin, 256, 2)

        windows = jax.vmap(window_at)(starts[slab_index])
        remixed = jnp.einsum(
            "jcmb,jbo->cmjo",
            windows,
            weights[slab_index].astype(jnp.float32),
            precision=lax.Precision.HIGHEST,
        )
        pieces.append(remixed.reshape(2, slab_rows, -1))
    return jnp.concatenate(pieces, 1)


def generic_body(raw, stolt_weights, band_start):
    groups = lax.axis_size("az")
    az_index = lax.axis_index("az")
    rg_index = lax.axis_index("rg")
    part_lines = raw.shape[1]
    bin_count = raw.shape[3]
    line_total = LINES_DEV * groups
    short_forward = dft_table(groups, -1.0, 1.0 / math.sqrt(groups))
    spread = jnp.einsum(
        "dkcp,cmpr->dmkr", short_forward, raw.astype(jnp.float32), precision=lax.Precision.HIGHEST
    )
    line_index = az_index * part_lines + jnp.arange(part_lines, dtype=jnp.int32)
    freq_index = jnp.arange(groups, dtype=jnp.int32)
    phase_index = line_index[:, None] * freq_index[None, :] % line_total
    real_part, imag_part = rotate(spread[0], spread[1], phase_index[:, :, None], line_total, -1.0)
    twisted = jnp.stack([real_part, imag_part])
    long_forward = dft_table(LINES_DEV, -1.0, 1.0 / math.sqrt(LINES_DEV))
    spectrum = jnp.einsum(
        "dkcm,cmjr->dkjr",
        long_forward,
        lax.all_to_all(twisted, "az", split_axis=2, concat_axis=1, tiled=True),
        precision=lax.Precision.HIGHEST,
    )
    spectrum_rows = spectrum[:, :, 0, :]
    slab_rows = LINES_DEV // SLABS
    block_count = bin_count // 128
    padded = with_halo(spectrum_rows, (("rg", 2),), 128)
    local_band = lax.dynamic_slice_in_dim(band_start, rg_index * block_count, block_count, 1)
    starts = (local_band - rg_index * block_count) * 128 + 128
    remapped = stolt(padded, stolt_weights, starts, slab_rows)
    long_inverse = dft_table(LINES_DEV, 1.0, 1.0 / math.sqrt(LINES_DEV))
    lines_back = jnp.einsum(
        "dmck,ckr->dmr", long_inverse, remapped, precision=lax.Precision.HIGHEST
    )
    all_lines = jnp.arange(LINES_DEV, dtype=jnp.int32)
    back_index = all_lines * az_index % line_total
    real_part, imag_part = rotate(
        lines_back[0], lines_back[1], back_index[:, None], line_total, 1.0
    )
    unrolled = jnp.stack([real_part, imag_part])[:, :, None, :]
    short_inverse = dft_table(groups, 1.0, 1.0 / math.sqrt(groups))
    focused = jnp.einsum(
        "dpck,cmkr->dmpr",
        short_inverse,
        lax.all_to_all(unrolled, "az", split_axis=1, concat_axis=2, tiled=True),
        precision=lax.Precision.HIGHEST,
    )
    return focused.astype(jnp.bfloat16)


NDEV = 8
MLOC = LINES_DEV // NDEV
ROWS = 2 * MLOC
HALF = 16
TAIL = 8
TILES = 8
LINES = 2 * LINES_DEV
SIDE = LINES_DEV // 2
EARLY = (6, 2, 4, 5, 1, 0)
LATE = (3, 7)
EARLY_ROWS = 192
LEAD = (2,)
REST = (0, 1, 3)
VMEM_LIMIT = 20 * 1024 * 1024


def split2(x):
    hi = x.astype(BF16)
    lo = (x - hi.astype(F32)).astype(BF16)
    return hi, lo


def mm(a, b):
    return jnp.dot(a, b, preferred_element_type=F32)


def product3(table, pair):
    return mm(table[0], pair[0]) + mm(table[0], pair[1]) + mm(table[1], pair[0])


def short_table(me):
    row = lax.broadcasted_iota(jnp.int32, (16, 256), 0)
    column = lax.broadcasted_iota(jnp.int32, (16, 256), 1)
    residue = (row // 2) ^ me
    quarter = row % 2 - column // 128
    turn = (residue * (2 * (column % 8) + me // 4) + 4 * quarter + 16) % 16
    value = jnp.cos(turn.astype(F32) * (2.0 * math.pi / 16))
    line = lax.broadcasted_iota(jnp.int32, (HALF, 256), 1) // 8 % HALF
    same = line == lax.broadcasted_iota(jnp.int32, (HALF, 256), 0)
    return jnp.concatenate([jnp.where(same, value[n : n + 1], 0.0) for n in range(16)], 0)


def long_base():
    k2 = np.arange(LINES_DEV).reshape(-1, 2).T.reshape(1, -1)
    angle = 2 * np.pi * (np.arange(SIDE).reshape(-1, 1) * k2 % LINES_DEV) / LINES_DEV
    return np.stack([np.cos(angle), np.sin(angle)]).astype(np.float32)


def rows_at(index, size):
    return pl.ds(pl.multiple_of(index * size, size), size)


def tiles_of(ref):
    return (ref.shape[-2] - TAIL) // ROWS


def store_coded(out_ref, pieces):
    tiles = tiles_of(out_ref)
    peak = None
    for _, value in pieces:
        top = jnp.max(jnp.abs(value), axis=0, keepdims=True)
        peak = top if peak is None else jnp.maximum(peak, top)
    code = jnp.ceil(jnp.log2(jnp.maximum(peak, 1e-30) * (1.0 / FULL)) * CODE_STEPS + 0.01)
    inverse = jnp.exp2(code * (-1.0 / CODE_STEPS))
    for row, value in pieces:
        coded = jnp.round(value * inverse).astype(jnp.int32).astype(jnp.int16)
        for tile in range(tiles):
            at = tile * ROWS + row
            out_ref[at : at + value.shape[0], :] = coded[:, tile * TILE : (tile + 1) * TILE]
    which = lax.broadcasted_iota(jnp.int32, (TAIL, TILE), 0)
    scales = jnp.zeros((TAIL, TILE), F32)
    for tile in range(tiles):
        scales = jnp.where(which == tile, code[:, tile * TILE : (tile + 1) * TILE], scales)
    out_ref[tiles * ROWS : tiles * ROWS + TAIL, :] = scales.astype(jnp.int32).astype(jnp.int16)


def load_scales(ref):
    at = tiles_of(ref) * ROWS
    code = ref[at : at + TAIL, :].astype(jnp.int32).astype(F32)
    return jnp.exp2(code * (1.0 / CODE_STEPS))


def load_columns(ref, scales, tiles):
    parts = []
    for t in tiles:
        value = ref[t * ROWS : (t + 1) * ROWS, :].astype(jnp.int32).astype(F32)
        parts.append(value * scales[t : t + 1, :])
    return jnp.concatenate(parts, 1)


def tile_pairs(tiles):
    return [(t, t + 1) for t in range(0, tiles, 2)]


def stacked3(pair):
    return jnp.concatenate([pair[0], pair[1], pair[0]], 0)


def late_table(rows):
    hi, lo = (v.astype(F32) for v in split2(rows))
    return jnp.concatenate([hi, hi, lo], 0).T.astype(BF16)


def sign_of(me):
    return (1 - 2 * (me // 4)).astype(F32)


def spread_kernel(me_ref, x_ref, *out_refs):
    hi, lo = split2(short_table(me_ref[0]))
    halves = []
    for h in range(2):
        at = h * 128
        x = jnp.concatenate([x_ref[at : at + 128, :], x_ref[256 + at : 256 + at + 128, :]], 0)
        halves.append(mm(hi, x) + mm(lo, x))
    for n, out_ref in enumerate(out_refs):
        pieces = []
        for c in range(2):
            for h in range(2):
                at = n * 32 + c * HALF
                pieces.append((c * MLOC + h * HALF, halves[h][at : at + HALF, :]))
        store_coded(out_ref, pieces)


def tables_kernel(me_ref, band_ref, base_ref, *refs):
    forward_ref, forward_late_ref, inverse_ref, image_ref, image_late_ref, starts_ref = refs
    me = me_ref[0]
    step = 2.0 * math.pi / (NDEV * LINES_DEV)
    blocks = []
    for i in range(4):
        slot = (me & 3) ^ i
        line = lax.broadcasted_iota(jnp.int32, (MLOC, TILE), 0) + slot * MLOC
        angle = (line * me).astype(F32) * step
        turn_cos, turn_sin = jnp.cos(angle) * (1.0 / 64.0), jnp.sin(angle) * (1.0 / 64.0)
        cosine, sine = [base_ref[n, rows_at(slot, MLOC), :] for n in range(2)]
        turn_cos = jnp.concatenate([turn_cos, turn_cos], 1)
        turn_sin = jnp.concatenate([turn_sin, turn_sin], 1)
        blocks.append((cosine * turn_cos - sine * turn_sin, sine * turn_cos + cosine * turn_sin))
    whole = [jnp.concatenate([b[n] for b in blocks], 0) for n in range(2)]
    for parity in range(2):
        co, si = [w[:, parity * SIDE : (parity + 1) * SIDE] for w in whole]
        inverse = jnp.concatenate([jnp.concatenate([co, -si], 1), jnp.concatenate([si, co], 1)], 0)
        inverse_ref[0, parity], inverse_ref[1, parity] = split2(inverse)
        early = jnp.concatenate([inverse[:96], inverse[128:224]], 0).T * 2.0
        forward_ref[0, parity], forward_ref[1, parity] = split2(early)
        forward_late_ref[parity] = late_table(jnp.concatenate([inverse[96:128], inverse[224:]], 0) * 2.0)
    short = short_table(me)
    early, late = [
        jnp.concatenate([short[i * 32 : (i + 1) * 32] for i in which], 0) for which in (EARLY, LATE)
    ]
    image_ref[0], image_ref[1] = split2(early.T)
    image_late_ref[...] = late_table(late)
    starts_ref[...] = band_ref[...]


def side_lines(values, pairs, sign):
    sums = [values[i] + values[i + 4] for i in pairs]
    gaps = [(values[i] - values[i + 4]) * sign for i in pairs]
    for lines in (sums, gaps):
        yield split2(jnp.concatenate([v[:MLOC] for v in lines] + [v[MLOC:] for v in lines], 0))


def forward_early_kernel(me_ref, table_ref, *refs):
    in_refs, sum_ref = dict(zip(EARLY, refs)), refs[len(EARLY)]
    sign = sign_of(me_ref[0])
    scales = {i: load_scales(ref) for i, ref in in_refs.items()}
    for tiles in tile_pairs(TILES):
        values = {i: load_columns(ref, scales[i], tiles) for i, ref in in_refs.items()}
        for parity, pair in enumerate(side_lines(values, (0, 1, 2), sign)):
            columns = slice(tiles[0] * TILE, (tiles[0] + 2) * TILE)
            sum_ref[parity, :, columns] = product3((table_ref[0, parity], table_ref[1, parity]), pair)


def forward_kernel(me_ref, rg_ref, table_ref, sum_ref, *refs):
    in_refs, (out_ref, edge_ref) = dict(zip(LATE, refs)), refs[len(LATE) :]
    sign = sign_of(me_ref[0])
    scales = {i: load_scales(ref) for i, ref in in_refs.items()}
    for tiles in tile_pairs(TILES):
        values = {i: load_columns(ref, scales[i], tiles) for i, ref in in_refs.items()}
        for parity, pair in enumerate(side_lines(values, (3,), sign)):
            columns = slice(tiles[0] * TILE, (tiles[0] + 2) * TILE)
            result = sum_ref[parity, :, columns] + mm(table_ref[parity], stacked3(pair))
            for at, t in enumerate(tiles):
                for part, half in enumerate(split2(result[:, at * TILE : (at + 1) * TILE])):
                    out_ref[t, part, parity * 256 : (parity + 1) * 256, :] = half
    edge_ref[...] = out_ref[(1 - rg_ref[0]) * (TILES - 1)]


def remap_block(starts_ref, weights_ref, rg, j, tile_at):
    for g in range(SLABS):
        at = starts_ref[g, rg * TILES + j] - rg * TILES
        window = []
        for part in range(2):
            for parity in range(2):
                for c in range(2):
                    row = parity * 256 + c * 128 + g * 32
                    rows = slice(row, row + 32)
                    window.append(jnp.concatenate([tile_at(at + n, part, rows) for n in range(2)], 1))
        both = mm(jnp.concatenate(window, 0), weights_ref[g, j])
        yield g, split2(both[:128] + both[128:])


def focus_rows(g):
    return [(parity, c * 128 + g * 32) for parity in range(2) for c in range(2)]


def inner_kernel(rg_ref, starts_ref, spectrum_ref, weights_ref, focus_ref):
    rg = rg_ref[0]
    for n in range(TILES - 1):
        j = n + rg
        for g, pair in remap_block(
            starts_ref, weights_ref, rg, j, lambda t, part, rows: spectrum_ref[t, part, rows, :]
        ):
            for part, half in enumerate(pair):
                for at, (parity, row) in enumerate(focus_rows(g)):
                    focus_ref[part, parity, j, row : row + 32, :] = half[at * 32 : (at + 1) * 32]


def back_messages(me, rg, slots, table_ref, focus_ref, face_ref, out_refs):
    results = []
    for parity in range(2):
        table = [
            jnp.concatenate(
                [
                    table_ref[part, parity, c * SIDE + i * MLOC : c * SIDE + (i + 1) * MLOC, :]
                    for i in slots
                    for c in range(2)
                ],
                0,
            )
            for part in range(2)
        ]
        pair = []
        for part in range(2):
            block = face_ref[part, parity]
            inner = [focus_ref[part, parity, n] for n in range(TILES)]
            inner[0] = jnp.where(rg == 1, block, inner[0])
            inner[-1] = jnp.where(rg == 1, inner[-1], block)
            pair.append(jnp.concatenate(inner, 1))
        results.append(product3(table, pair))
    even, odd = results[0], results[1] * sign_of(me)
    for upper, lines in enumerate((even + odd, even - odd)):
        for n in range(len(slots)):
            store_coded(out_refs[2 * n + upper], [(0, lines[n * ROWS : (n + 1) * ROWS, :])])


def outer_kernel(me_ref, rg_ref, starts_ref, spectrum_ref, halo_ref, weights_ref, table_ref, focus_ref, *refs):
    out_refs, face_ref, window_ref = refs[:2], refs[2], refs[3]
    rg = rg_ref[0]
    first = 6 - 7 * rg
    window_ref[2 - 2 * rg] = halo_ref[...]
    for n in range(2):
        window_ref[rg + n] = spectrum_ref[(1 - rg) * 6 + n]
    for g, pair in remap_block(
        starts_ref,
        weights_ref,
        rg,
        (1 - rg) * (TILES - 1),
        lambda t, part, rows: window_ref[t - first, part, rows, :],
    ):
        for part, half in enumerate(pair):
            for at, (parity, row) in enumerate(focus_rows(g)):
                face_ref[part, parity, row : row + 32, :] = half[at * 32 : (at + 1) * 32]
    back_messages(me_ref[0], rg, LEAD, table_ref, focus_ref, face_ref, out_refs)


def rest_kernel(me_ref, rg_ref, table_ref, focus_ref, face_ref, *out_refs):
    back_messages(me_ref[0], rg_ref[0], REST, table_ref, focus_ref, face_ref, out_refs)


def image_lines(values, h):
    rows = [v[c * MLOC + h * HALF : c * MLOC + (h + 1) * HALF] for v in values for c in range(2)]
    return split2(jnp.concatenate(rows, 0))


def image_early_kernel(table_ref, *refs):
    in_refs, sum_ref = refs[: len(EARLY)], refs[len(EARLY)]
    scales = [load_scales(ref) for ref in in_refs]
    for tiles in tile_pairs(TILES):
        values = [load_columns(ref, scale, tiles) for ref, scale in zip(in_refs, scales)]
        for h in range(2):
            columns = slice(tiles[0] * TILE, (tiles[0] + 2) * TILE)
            sum_ref[h, :, columns] = product3(table_ref, image_lines(values, h))


def image_kernel(table_ref, sum_ref, *refs):
    in_refs, (out_hbm, out_ref, sems) = refs[: len(LATE)], refs[len(LATE) :]
    stores = []
    scales = [load_scales(ref) for ref in in_refs]
    for tiles in tile_pairs(TILES):
        values = [load_columns(ref, scale, tiles) for ref, scale in zip(in_refs, scales)]
        for h in range(2):
            columns = slice(tiles[0] * TILE, (tiles[0] + 2) * TILE)
            result = sum_ref[h, :, columns] + mm(table_ref[...], stacked3(image_lines(values, h)))
            for c in range(2):
                at = c * 256 + h * 128
                out_ref[at : at + 128, columns] = result[c * 128 : (c + 1) * 128].astype(BF16)
        stores.append(
            pltpu.make_async_copy(out_ref.at[:, columns], out_hbm.at[:, columns], sems.at[tiles[0] // 2])
        )
        stores[-1].start()
    for store in stores:
        store.wait()


def vmem_call(kernel, name, out_shape, smem=0, vmem=0, scratch=(), out_space=pltpu.VMEM):
    return pl.pallas_call(
        kernel,
        name=name,
        out_shape=out_shape,
        in_specs=[pl.BlockSpec(memory_space=pltpu.SMEM)] * smem
        + [pl.BlockSpec(memory_space=pltpu.VMEM)] * vmem,
        out_specs=jax.tree.map(lambda _: pl.BlockSpec(memory_space=out_space), out_shape),
        scratch_shapes=scratch,
        compiler_params=pltpu.CompilerParams(vmem_limit_bytes=VMEM_LIMIT),
    )


def after(value, *others):
    return lax.optimization_barrier((value, *others))[0]


def exchange(messages):
    return [
        [
            lax.ppermute(messages[i], "az", [(d, d ^ i) for d in range(NDEV)]) if i else messages[0]
            for i in which
        ]
        for which in (EARLY, LATE)
    ]


def fast_body(raw, stolt_weights, band_start):
    me = lax.axis_index("az").astype(jnp.int32)[None]
    rg = lax.axis_index("rg").astype(jnp.int32)[None]
    bins = raw.shape[3]
    message = jax.ShapeDtypeStruct((TILES * ROWS + TAIL, TILE), jnp.int16)
    early_shape = (2, LINES_DEV, EARLY_ROWS)

    sent = vmem_call(spread_kernel, "spread", [message] * NDEV, smem=1, vmem=1)(
        me, raw.reshape(LINES, bins)
    )
    got_early, got_late = exchange(sent)
    forward_table, forward_late, inverse_table, image_table, image_late, starts = vmem_call(
        tables_kernel,
        "tables",
        [
            jax.ShapeDtypeStruct((2,) + early_shape, BF16),
            jax.ShapeDtypeStruct(early_shape, BF16),
            jax.ShapeDtypeStruct((2, 2, LINES_DEV, LINES_DEV), BF16),
            jax.ShapeDtypeStruct((2, 256, EARLY_ROWS), BF16),
            jax.ShapeDtypeStruct((256, EARLY_ROWS), BF16),
            jax.ShapeDtypeStruct(band_start.shape, band_start.dtype),
        ],
        smem=1,
        vmem=2,
    )(after(me, sent[0]), band_start, jnp.asarray(long_base()))

    partial = vmem_call(
        forward_early_kernel,
        "forward_early",
        jax.ShapeDtypeStruct((2, LINES_DEV, bins), F32),
        smem=1,
        vmem=1 + len(EARLY),
    )(me, forward_table, *got_early)
    spectrum, edge = vmem_call(
        forward_kernel,
        "forward",
        [jax.ShapeDtypeStruct((TILES, 2, LINES, TILE), BF16), jax.ShapeDtypeStruct((2, LINES, TILE), BF16)],
        smem=2,
        vmem=2 + len(LATE),
    )(me, rg, forward_late, partial, *got_late)
    halo = lax.ppermute(edge, "rg", [(0, 1), (1, 0)])
    focus = vmem_call(
        inner_kernel,
        "inner",
        jax.ShapeDtypeStruct((2, 2, TILES, LINES_DEV, TILE), BF16),
        smem=2,
        vmem=2,
    )(rg, starts, spectrum, stolt_weights)
    back = [None] * NDEV
    back[2], back[6], face = vmem_call(
        outer_kernel,
        "outer",
        [message, message, jax.ShapeDtypeStruct((2, 2, LINES_DEV, TILE), BF16)],
        smem=3,
        vmem=5,
        scratch=[pltpu.VMEM((3, 2, LINES, TILE), BF16)],
    )(me, rg, starts, spectrum, halo, stolt_weights, inverse_table, focus)
    rest = vmem_call(rest_kernel, "rest", [message] * 6, smem=2, vmem=3)(me, rg, inverse_table, focus, face)
    for n, i in enumerate(REST):
        back[i], back[i + 4] = rest[2 * n], rest[2 * n + 1]
    early_lines, late_lines = exchange(back)
    image_sum = vmem_call(
        image_early_kernel, "image_early", jax.ShapeDtypeStruct((2, 256, bins), F32), vmem=1 + len(EARLY)
    )(image_table, *early_lines)
    image = vmem_call(
        image_kernel,
        "image",
        jax.ShapeDtypeStruct((LINES, bins), BF16),
        vmem=2 + len(LATE),
        scratch=[pltpu.VMEM((LINES, bins), BF16), pltpu.SemaphoreType.DMA((TILES // 2,))],
        out_space=pltpu.HBM,
    )(image_late, image_sum, *late_lines)
    return image.reshape(2, MLOC, NDEV, bins)


def body(raw, stolt_weights, band_start):
    fast = (
        lax.axis_size("az") == NDEV
        and lax.axis_size("rg") == 2
        and raw.shape[1:3] == (MLOC, NDEV)
        and raw.shape[3] == TILES * TILE
    )
    return (fast_body if fast else generic_body)(raw, stolt_weights, band_start)


def solution(mesh):
    placed = (P(None, ("frames", "az"), None, "rg"), P(None, "rg", None, None), P())
    return jax.shard_map(
        body,
        mesh=mesh,
        in_specs=placed,
        out_specs=P(None, ("frames", "az"), None, "rg"),
        check_vma=False,
    )
```

```python
import functools
import math

import jax
import jax.numpy as jnp
import numpy as np
from jax import lax
from jax.experimental import pallas as pl
from jax.experimental.pallas import tpu as pltpu
from jax.sharding import PartitionSpec as P

LINES_DEV = 256
SLABS = 4
TILE = 128
BF16 = jnp.bfloat16
F32 = jnp.float32
CODE_STEPS = 256.0
FULL = 32767.0


def with_halo(cells, sides, width):
    for axis, dim in sides:
        count = lax.axis_size(axis)
        ends = count - 1
        head = lax.slice_in_dim(cells, 0, width, axis=dim)
        tail = lax.slice_in_dim(cells, cells.shape[dim] - width, cells.shape[dim], axis=dim)
        cells = jnp.concatenate(
            [
                lax.ppermute(tail, axis, [(i, (i + 1) % count) for i in range(ends)]),
                cells,
                lax.ppermute(head, axis, [((i + 1) % count, i) for i in range(ends)]),
            ],
            axis=dim,
        )
    return cells


def dft_table(length, direction, factor):
    counter = jnp.arange(length, dtype=jnp.int32)
    product = counter[:, None] * counter[None, :] % length
    angles = product.astype(jnp.float32) * (2.0 * math.pi / length)
    cosine = jnp.cos(angles) * factor
    sines = jnp.sin(angles) * (factor * direction)
    return jnp.stack([jnp.stack([cosine, -sines], 1), jnp.stack([sines, cosine], 1)], 0)


def rotate(real_part, imag_part, phase_index, line_total, direction):
    angles = phase_index.astype(jnp.float32) * (2.0 * math.pi / line_total)
    cosine = jnp.cos(angles)
    sines = jnp.sin(angles) * direction
    return (real_part * cosine - imag_part * sines, imag_part * cosine + real_part * sines)


def stolt(slab_source, weights, starts, slab_rows):
    pieces = []
    for slab_index in range(weights.shape[0]):
        slab_data = slab_source[:, slab_index * slab_rows : (slab_index + 1) * slab_rows, :]

        def window_at(start_bin):
            return lax.dynamic_slice_in_dim(slab_data, start_bin, 256, 2)

        windows = jax.vmap(window_at)(starts[slab_index])
        remixed = jnp.einsum(
            "jcmb,jbo->cmjo",
            windows,
            weights[slab_index].astype(jnp.float32),
            precision=lax.Precision.HIGHEST,
        )
        pieces.append(remixed.reshape(2, slab_rows, -1))
    return jnp.concatenate(pieces, 1)


def generic_body(raw, stolt_weights, band_start):
    groups = lax.axis_size("az")
    az_index = lax.axis_index("az")
    rg_index = lax.axis_index("rg")
    part_lines = raw.shape[1]
    bin_count = raw.shape[3]
    line_total = LINES_DEV * groups
    short_forward = dft_table(groups, -1.0, 1.0 / math.sqrt(groups))
    spread = jnp.einsum(
        "dkcp,cmpr->dmkr", short_forward, raw.astype(jnp.float32), precision=lax.Precision.HIGHEST
    )
    line_index = az_index * part_lines + jnp.arange(part_lines, dtype=jnp.int32)
    freq_index = jnp.arange(groups, dtype=jnp.int32)
    phase_index = line_index[:, None] * freq_index[None, :] % line_total
    real_part, imag_part = rotate(spread[0], spread[1], phase_index[:, :, None], line_total, -1.0)
    twisted = jnp.stack([real_part, imag_part])
    long_forward = dft_table(LINES_DEV, -1.0, 1.0 / math.sqrt(LINES_DEV))
    spectrum = jnp.einsum(
        "dkcm,cmjr->dkjr",
        long_forward,
        lax.all_to_all(twisted, "az", split_axis=2, concat_axis=1, tiled=True),
        precision=lax.Precision.HIGHEST,
    )
    spectrum_rows = spectrum[:, :, 0, :]
    slab_rows = LINES_DEV // SLABS
    block_count = bin_count // 128
    padded = with_halo(spectrum_rows, (("rg", 2),), 128)
    local_band = lax.dynamic_slice_in_dim(band_start, rg_index * block_count, block_count, 1)
    starts = (local_band - rg_index * block_count) * 128 + 128
    remapped = stolt(padded, stolt_weights, starts, slab_rows)
    long_inverse = dft_table(LINES_DEV, 1.0, 1.0 / math.sqrt(LINES_DEV))
    lines_back = jnp.einsum(
        "dmck,ckr->dmr", long_inverse, remapped, precision=lax.Precision.HIGHEST
    )
    all_lines = jnp.arange(LINES_DEV, dtype=jnp.int32)
    back_index = all_lines * az_index % line_total
    real_part, imag_part = rotate(
        lines_back[0], lines_back[1], back_index[:, None], line_total, 1.0
    )
    unrolled = jnp.stack([real_part, imag_part])[:, :, None, :]
    short_inverse = dft_table(groups, 1.0, 1.0 / math.sqrt(groups))
    focused = jnp.einsum(
        "dpck,cmkr->dmpr",
        short_inverse,
        lax.all_to_all(unrolled, "az", split_axis=1, concat_axis=2, tiled=True),
        precision=lax.Precision.HIGHEST,
    )
    return focused.astype(jnp.bfloat16)


NDEV = 8
MLOC = LINES_DEV // NDEV
ROWS = 2 * MLOC
HALF = 16
TAIL = 8
TILES = 8
LINES = 2 * LINES_DEV
SIDE = LINES_DEV // 2
EARLY = (6, 2, 4, 5, 1, 0)
LATE = (3, 7)
EARLY_ROWS = 192
LEAD = (2,)
SPREAD_LEAD = (6, )
SPREAD_REST = (2, 4, 5, 1, 3, 7, 0, )
REST = (0, 1, 3)
VMEM_LIMIT = 20 * 1024 * 1024


def split2(x):
    hi = x.astype(BF16)
    lo = (x - hi.astype(F32)).astype(BF16)
    return hi, lo


def mm(a, b):
    return jnp.dot(a, b, preferred_element_type=F32)


def product3(table, pair):
    return mm(table[0], pair[0]) + mm(table[0], pair[1]) + mm(table[1], pair[0])


def short_table(me):
    row = lax.broadcasted_iota(jnp.int32, (16, 256), 0)
    column = lax.broadcasted_iota(jnp.int32, (16, 256), 1)
    residue = (row // 2) ^ me
    quarter = row % 2 - column // 128
    turn = (residue * (2 * (column % 8) + me // 4) + 4 * quarter + 16) % 16
    value = jnp.cos(turn.astype(F32) * (2.0 * math.pi / 16))
    line = lax.broadcasted_iota(jnp.int32, (HALF, 256), 1) // 8 % HALF
    same = line == lax.broadcasted_iota(jnp.int32, (HALF, 256), 0)
    return jnp.concatenate([jnp.where(same, value[n : n + 1], 0.0) for n in range(16)], 0)


def long_base():
    k2 = np.arange(LINES_DEV).reshape(-1, 2).T.reshape(1, -1)
    angle = 2 * np.pi * (np.arange(SIDE).reshape(-1, 1) * k2 % LINES_DEV) / LINES_DEV
    return np.stack([np.cos(angle), np.sin(angle)]).astype(np.float32)


def rows_at(index, size):
    return pl.ds(pl.multiple_of(index * size, size), size)


def tiles_of(ref):
    return (ref.shape[-2] - TAIL) // ROWS


def store_coded(out_ref, pieces):
    tiles = tiles_of(out_ref)
    peak = None
    for _, value in pieces:
        top = jnp.max(jnp.abs(value), axis=0, keepdims=True)
        peak = top if peak is None else jnp.maximum(peak, top)
    code = jnp.ceil(jnp.log2(jnp.maximum(peak, 1e-30) * (1.0 / FULL)) * CODE_STEPS + 0.01)
    inverse = jnp.exp2(code * (-1.0 / CODE_STEPS))
    for row, value in pieces:
        coded = jnp.round(value * inverse).astype(jnp.int32).astype(jnp.int16)
        for tile in range(tiles):
            at = tile * ROWS + row
            out_ref[at : at + value.shape[0], :] = coded[:, tile * TILE : (tile + 1) * TILE]
    which = lax.broadcasted_iota(jnp.int32, (TAIL, TILE), 0)
    scales = jnp.zeros((TAIL, TILE), F32)
    for tile in range(tiles):
        scales = jnp.where(which == tile, code[:, tile * TILE : (tile + 1) * TILE], scales)
    out_ref[tiles * ROWS : tiles * ROWS + TAIL, :] = scales.astype(jnp.int32).astype(jnp.int16)


def load_scales(ref):
    at = tiles_of(ref) * ROWS
    code = ref[at : at + TAIL, :].astype(jnp.int32).astype(F32)
    return jnp.exp2(code * (1.0 / CODE_STEPS))


def load_columns(ref, scales, tiles):
    parts = []
    for t in tiles:
        value = ref[t * ROWS : (t + 1) * ROWS, :].astype(jnp.int32).astype(F32)
        parts.append(value * scales[t : t + 1, :])
    return jnp.concatenate(parts, 1)


def tile_pairs(tiles):
    return [(t, t + 1) for t in range(0, tiles, 2)]


def stacked3(pair):
    return jnp.concatenate([pair[0], pair[1], pair[0]], 0)


def late_table(rows):
    hi, lo = (v.astype(F32) for v in split2(rows))
    return jnp.concatenate([hi, hi, lo], 0).T.astype(BF16)


def sign_of(me):
    return (1 - 2 * (me // 4)).astype(F32)


def spread_kernel(which, me_ref, x_ref, *out_refs):
    table = short_table(me_ref[0])
    hi, lo = split2(jnp.concatenate([table[i * 32 : (i + 1) * 32] for i in which], 0))
    halves = []
    for h in range(2):
        at = h * 128
        x = jnp.concatenate([x_ref[at : at + 128, :], x_ref[256 + at : 256 + at + 128, :]], 0)
        halves.append(mm(hi, x) + mm(lo, x))
    for n, out_ref in enumerate(out_refs):
        pieces = []
        for c in range(2):
            for h in range(2):
                at = n * 32 + c * HALF
                pieces.append((c * MLOC + h * HALF, halves[h][at : at + HALF, :]))
        store_coded(out_ref, pieces)


def tables_kernel(me_ref, band_ref, base_ref, *refs):
    forward_ref, forward_late_ref, inverse_ref, image_ref, image_late_ref, starts_ref = refs
    me = me_ref[0]
    step = 2.0 * math.pi / (NDEV * LINES_DEV)
    blocks = []
    for i in range(4):
        slot = (me & 3) ^ i
        line = lax.broadcasted_iota(jnp.int32, (MLOC, TILE), 0) + slot * MLOC
        angle = (line * me).astype(F32) * step
        turn_cos, turn_sin = jnp.cos(angle) * (1.0 / 64.0), jnp.sin(angle) * (1.0 / 64.0)
        cosine, sine = [base_ref[n, rows_at(slot, MLOC), :] for n in range(2)]
        turn_cos = jnp.concatenate([turn_cos, turn_cos], 1)
        turn_sin = jnp.concatenate([turn_sin, turn_sin], 1)
        blocks.append((cosine * turn_cos - sine * turn_sin, sine * turn_cos + cosine * turn_sin))
    whole = [jnp.concatenate([b[n] for b in blocks], 0) for n in range(2)]
    for parity in range(2):
        co, si = [w[:, parity * SIDE : (parity + 1) * SIDE] for w in whole]
        inverse = jnp.concatenate([jnp.concatenate([co, -si], 1), jnp.concatenate([si, co], 1)], 0)
        inverse_ref[0, parity], inverse_ref[1, parity] = split2(inverse)
        early = jnp.concatenate([inverse[:96], inverse[128:224]], 0).T * 2.0
        forward_ref[0, parity], forward_ref[1, parity] = split2(early)
        forward_late_ref[parity] = late_table(jnp.concatenate([inverse[96:128], inverse[224:]], 0) * 2.0)
    short = short_table(me)
    early, late = [
        jnp.concatenate([short[i * 32 : (i + 1) * 32] for i in which], 0) for which in (EARLY, LATE)
    ]
    image_ref[0], image_ref[1] = split2(early.T)
    image_late_ref[...] = late_table(late)
    starts_ref[...] = band_ref[...]


def side_lines(values, pairs, sign):
    sums = [values[i] + values[i + 4] for i in pairs]
    gaps = [(values[i] - values[i + 4]) * sign for i in pairs]
    for lines in (sums, gaps):
        yield split2(jnp.concatenate([v[:MLOC] for v in lines] + [v[MLOC:] for v in lines], 0))


def forward_early_kernel(me_ref, table_ref, *refs):
    in_refs, sum_ref = dict(zip(EARLY, refs)), refs[len(EARLY)]
    sign = sign_of(me_ref[0])
    scales = {i: load_scales(ref) for i, ref in in_refs.items()}
    for tiles in tile_pairs(TILES):
        values = {i: load_columns(ref, scales[i], tiles) for i, ref in in_refs.items()}
        for parity, pair in enumerate(side_lines(values, (0, 1, 2), sign)):
            columns = slice(tiles[0] * TILE, (tiles[0] + 2) * TILE)
            sum_ref[parity, :, columns] = product3((table_ref[0, parity], table_ref[1, parity]), pair)


def forward_kernel(me_ref, rg_ref, table_ref, sum_ref, *refs):
    in_refs, (out_ref, edge_ref) = dict(zip(LATE, refs)), refs[len(LATE) :]
    sign = sign_of(me_ref[0])
    scales = {i: load_scales(ref) for i, ref in in_refs.items()}
    for tiles in tile_pairs(TILES):
        values = {i: load_columns(ref, scales[i], tiles) for i, ref in in_refs.items()}
        for parity, pair in enumerate(side_lines(values, (3,), sign)):
            columns = slice(tiles[0] * TILE, (tiles[0] + 2) * TILE)
            result = sum_ref[parity, :, columns] + mm(table_ref[parity], stacked3(pair))
            for at, t in enumerate(tiles):
                for part, half in enumerate(split2(result[:, at * TILE : (at + 1) * TILE])):
                    out_ref[t, part, parity * 256 : (parity + 1) * 256, :] = half
    edge_ref[...] = out_ref[(1 - rg_ref[0]) * (TILES - 1)]


def remap_block(starts_ref, weights_ref, rg, j, tile_at):
    for g in range(SLABS):
        at = starts_ref[g, rg * TILES + j] - rg * TILES
        window = []
        for part in range(2):
            for parity in range(2):
                for c in range(2):
                    row = parity * 256 + c * 128 + g * 32
                    rows = slice(row, row + 32)
                    window.append(jnp.concatenate([tile_at(at + n, part, rows) for n in range(2)], 1))
        both = mm(jnp.concatenate(window, 0), weights_ref[g, j])
        yield g, split2(both[:128] + both[128:])


def focus_rows(g):
    return [(parity, c * 128 + g * 32) for parity in range(2) for c in range(2)]


def inner_kernel(rg_ref, starts_ref, spectrum_ref, weights_ref, focus_ref):
    rg = rg_ref[0]
    for n in range(TILES - 1):
        j = n + rg
        for g, pair in remap_block(
            starts_ref, weights_ref, rg, j, lambda t, part, rows: spectrum_ref[t, part, rows, :]
        ):
            for part, half in enumerate(pair):
                for at, (parity, row) in enumerate(focus_rows(g)):
                    focus_ref[part, parity, j, row : row + 32, :] = half[at * 32 : (at + 1) * 32]


def back_messages(me, rg, slots, table_ref, focus_ref, face_ref, out_refs):
    results = []
    for parity in range(2):
        table = [
            jnp.concatenate(
                [
                    table_ref[part, parity, c * SIDE + i * MLOC : c * SIDE + (i + 1) * MLOC, :]
                    for i in slots
                    for c in range(2)
                ],
                0,
            )
            for part in range(2)
        ]
        pair = []
        for part in range(2):
            block = face_ref[part, parity]
            inner = [focus_ref[part, parity, n] for n in range(TILES)]
            inner[0] = jnp.where(rg == 1, block, inner[0])
            inner[-1] = jnp.where(rg == 1, inner[-1], block)
            pair.append(jnp.concatenate(inner, 1))
        results.append(product3(table, pair))
    even, odd = results[0], results[1] * sign_of(me)
    for upper, lines in enumerate((even + odd, even - odd)):
        for n in range(len(slots)):
            store_coded(out_refs[2 * n + upper], [(0, lines[n * ROWS : (n + 1) * ROWS, :])])


def outer_kernel(me_ref, rg_ref, starts_ref, spectrum_ref, halo_ref, weights_ref, table_ref, focus_ref, *refs):
    out_refs, face_ref, window_ref = refs[:2], refs[2], refs[3]
    rg = rg_ref[0]
    first = 6 - 7 * rg
    window_ref[2 - 2 * rg] = halo_ref[...]
    for n in range(2):
        window_ref[rg + n] = spectrum_ref[(1 - rg) * 6 + n]
    for g, pair in remap_block(
        starts_ref,
        weights_ref,
        rg,
        (1 - rg) * (TILES - 1),
        lambda t, part, rows: window_ref[t - first, part, rows, :],
    ):
        for part, half in enumerate(pair):
            for at, (parity, row) in enumerate(focus_rows(g)):
                face_ref[part, parity, row : row + 32, :] = half[at * 32 : (at + 1) * 32]
    back_messages(me_ref[0], rg, LEAD, table_ref, focus_ref, face_ref, out_refs)


def rest_kernel(me_ref, rg_ref, table_ref, focus_ref, face_ref, *out_refs):
    back_messages(me_ref[0], rg_ref[0], REST, table_ref, focus_ref, face_ref, out_refs)


def image_lines(values, h):
    rows = [v[c * MLOC + h * HALF : c * MLOC + (h + 1) * HALF] for v in values for c in range(2)]
    return split2(jnp.concatenate(rows, 0))


def image_early_kernel(table_ref, *refs):
    in_refs, sum_ref = refs[: len(EARLY)], refs[len(EARLY)]
    scales = [load_scales(ref) for ref in in_refs]
    for tiles in tile_pairs(TILES):
        values = [load_columns(ref, scale, tiles) for ref, scale in zip(in_refs, scales)]
        for h in range(2):
            columns = slice(tiles[0] * TILE, (tiles[0] + 2) * TILE)
            sum_ref[h, :, columns] = product3(table_ref, image_lines(values, h))


def image_kernel(table_ref, sum_ref, *refs):
    in_refs, (out_hbm, out_ref, sems) = refs[: len(LATE)], refs[len(LATE) :]
    stores = []
    scales = [load_scales(ref) for ref in in_refs]
    for tiles in tile_pairs(TILES):
        values = [load_columns(ref, scale, tiles) for ref, scale in zip(in_refs, scales)]
        for h in range(2):
            columns = slice(tiles[0] * TILE, (tiles[0] + 2) * TILE)
            result = sum_ref[h, :, columns] + mm(table_ref[...], stacked3(image_lines(values, h)))
            for c in range(2):
                at = c * 256 + h * 128
                out_ref[at : at + 128, columns] = result[c * 128 : (c + 1) * 128].astype(BF16)
        stores.append(
            pltpu.make_async_copy(out_ref.at[:, columns], out_hbm.at[:, columns], sems.at[tiles[0] // 2])
        )
        stores[-1].start()
    for store in stores:
        store.wait()


def vmem_call(kernel, name, out_shape, smem=0, vmem=0, scratch=(), out_space=pltpu.VMEM):
    return pl.pallas_call(
        kernel,
        name=name,
        out_shape=out_shape,
        in_specs=[pl.BlockSpec(memory_space=pltpu.SMEM)] * smem
        + [pl.BlockSpec(memory_space=pltpu.VMEM)] * vmem,
        out_specs=jax.tree.map(lambda _: pl.BlockSpec(memory_space=out_space), out_shape),
        scratch_shapes=scratch,
        compiler_params=pltpu.CompilerParams(vmem_limit_bytes=VMEM_LIMIT),
    )


def after(value, *others):
    return lax.optimization_barrier((value, *others))[0]


def exchange(messages):
    return [
        [
            lax.ppermute(messages[i], "az", [(d, d ^ i) for d in range(NDEV)]) if i else messages[0]
            for i in which
        ]
        for which in (EARLY, LATE)
    ]


def fast_body(raw, stolt_weights, band_start):
    me = lax.axis_index("az").astype(jnp.int32)[None]
    rg = lax.axis_index("rg").astype(jnp.int32)[None]
    bins = raw.shape[3]
    message = jax.ShapeDtypeStruct((TILES * ROWS + TAIL, TILE), jnp.int16)
    early_shape = (2, LINES_DEV, EARLY_ROWS)

    rows = raw.reshape(LINES, bins)
    sent = [None] * NDEV
    for name, which in (("spread", SPREAD_LEAD), ("spread_rest", SPREAD_REST)):
        own = me if name == "spread" else after(me, sent[SPREAD_LEAD[0]])
        made = vmem_call(functools.partial(spread_kernel, which), name, [message] * len(which), smem=1, vmem=1)(
            own, rows
        )
        for n, i in enumerate(which):
            sent[i] = made[n]
    got_early, got_late = exchange(sent)
    forward_table, forward_late, inverse_table, image_table, image_late, starts = vmem_call(
        tables_kernel,
        "tables",
        [
            jax.ShapeDtypeStruct((2,) + early_shape, BF16),
            jax.ShapeDtypeStruct(early_shape, BF16),
            jax.ShapeDtypeStruct((2, 2, LINES_DEV, LINES_DEV), BF16),
            jax.ShapeDtypeStruct((2, 256, EARLY_ROWS), BF16),
            jax.ShapeDtypeStruct((256, EARLY_ROWS), BF16),
            jax.ShapeDtypeStruct(band_start.shape, band_start.dtype),
        ],
        smem=1,
        vmem=2,
    )(after(me, sent[SPREAD_REST[0]]), band_start, jnp.asarray(long_base()))

    partial = vmem_call(
        forward_early_kernel,
        "forward_early",
        jax.ShapeDtypeStruct((2, LINES_DEV, bins), F32),
        smem=1,
        vmem=1 + len(EARLY),
    )(me, forward_table, *got_early)
    spectrum, edge = vmem_call(
        forward_kernel,
        "forward",
        [jax.ShapeDtypeStruct((TILES, 2, LINES, TILE), BF16), jax.ShapeDtypeStruct((2, LINES, TILE), BF16)],
        smem=2,
        vmem=2 + len(LATE),
    )(me, rg, forward_late, partial, *got_late)
    halo = lax.ppermute(edge, "rg", [(0, 1), (1, 0)])
    focus = vmem_call(
        inner_kernel,
        "inner",
        jax.ShapeDtypeStruct((2, 2, TILES, LINES_DEV, TILE), BF16),
        smem=2,
        vmem=2,
    )(rg, starts, spectrum, stolt_weights)
    back = [None] * NDEV
    back[2], back[6], face = vmem_call(
        outer_kernel,
        "outer",
        [message, message, jax.ShapeDtypeStruct((2, 2, LINES_DEV, TILE), BF16)],
        smem=3,
        vmem=5,
        scratch=[pltpu.VMEM((3, 2, LINES, TILE), BF16)],
    )(me, rg, starts, spectrum, halo, stolt_weights, inverse_table, focus)
    rest = vmem_call(rest_kernel, "rest", [message] * 6, smem=2, vmem=3)(me, rg, inverse_table, focus, face)
    for n, i in enumerate(REST):
        back[i], back[i + 4] = rest[2 * n], rest[2 * n + 1]
    early_lines, late_lines = exchange(back)
    image_sum = vmem_call(
        image_early_kernel, "image_early", jax.ShapeDtypeStruct((2, 256, bins), F32), vmem=1 + len(EARLY)
    )(image_table, *early_lines)
    image = vmem_call(
        image_kernel,
        "image",
        jax.ShapeDtypeStruct((LINES, bins), BF16),
        vmem=2 + len(LATE),
        scratch=[pltpu.VMEM((LINES, bins), BF16), pltpu.SemaphoreType.DMA((TILES // 2,))],
        out_space=pltpu.HBM,
    )(image_late, image_sum, *late_lines)
    return image.reshape(2, MLOC, NDEV, bins)


def body(raw, stolt_weights, band_start):
    fast = (
        lax.axis_size("az") == NDEV
        and lax.axis_size("rg") == 2
        and raw.shape[1:3] == (MLOC, NDEV)
        and raw.shape[3] == TILES * TILE
    )
    return (fast_body if fast else generic_body)(raw, stolt_weights, band_start)


def solution(mesh):
    placed = (P(None, ("frames", "az"), None, "rg"), P(None, "rg", None, None), P())
    return jax.shard_map(
        body,
        mesh=mesh,
        in_specs=placed,
        out_specs=P(None, ("frames", "az"), None, "rg"),
        check_vma=False,
    )
```

```python
import functools
import math

import jax
import jax.numpy as jnp
import numpy as np
from jax import lax
from jax.experimental import pallas as pl
from jax.experimental.pallas import tpu as pltpu
from jax.sharding import PartitionSpec as P

LINES_DEV = 256
SLABS = 4
TILE = 128
BF16 = jnp.bfloat16
F32 = jnp.float32
CODE_STEPS = 256.0
FULL = 32767.0


def with_halo(cells, sides, width):
    for axis, dim in sides:
        count = lax.axis_size(axis)
        ends = count - 1
        head = lax.slice_in_dim(cells, 0, width, axis=dim)
        tail = lax.slice_in_dim(cells, cells.shape[dim] - width, cells.shape[dim], axis=dim)
        cells = jnp.concatenate(
            [
                lax.ppermute(tail, axis, [(i, (i + 1) % count) for i in range(ends)]),
                cells,
                lax.ppermute(head, axis, [((i + 1) % count, i) for i in range(ends)]),
            ],
            axis=dim,
        )
    return cells


def dft_table(length, direction, factor):
    counter = jnp.arange(length, dtype=jnp.int32)
    product = counter[:, None] * counter[None, :] % length
    angles = product.astype(jnp.float32) * (2.0 * math.pi / length)
    cosine = jnp.cos(angles) * factor
    sines = jnp.sin(angles) * (factor * direction)
    return jnp.stack([jnp.stack([cosine, -sines], 1), jnp.stack([sines, cosine], 1)], 0)


def rotate(real_part, imag_part, phase_index, line_total, direction):
    angles = phase_index.astype(jnp.float32) * (2.0 * math.pi / line_total)
    cosine = jnp.cos(angles)
    sines = jnp.sin(angles) * direction
    return (real_part * cosine - imag_part * sines, imag_part * cosine + real_part * sines)


def stolt(slab_source, weights, starts, slab_rows):
    pieces = []
    for slab_index in range(weights.shape[0]):
        slab_data = slab_source[:, slab_index * slab_rows : (slab_index + 1) * slab_rows, :]

        def window_at(start_bin):
            return lax.dynamic_slice_in_dim(slab_data, start_bin, 256, 2)

        windows = jax.vmap(window_at)(starts[slab_index])
        remixed = jnp.einsum(
            "jcmb,jbo->cmjo",
            windows,
            weights[slab_index].astype(jnp.float32),
            precision=lax.Precision.HIGHEST,
        )
        pieces.append(remixed.reshape(2, slab_rows, -1))
    return jnp.concatenate(pieces, 1)


def generic_body(raw, stolt_weights, band_start):
    groups = lax.axis_size("az")
    az_index = lax.axis_index("az")
    rg_index = lax.axis_index("rg")
    part_lines = raw.shape[1]
    bin_count = raw.shape[3]
    line_total = LINES_DEV * groups
    short_forward = dft_table(groups, -1.0, 1.0 / math.sqrt(groups))
    spread = jnp.einsum(
        "dkcp,cmpr->dmkr", short_forward, raw.astype(jnp.float32), precision=lax.Precision.HIGHEST
    )
    line_index = az_index * part_lines + jnp.arange(part_lines, dtype=jnp.int32)
    freq_index = jnp.arange(groups, dtype=jnp.int32)
    phase_index = line_index[:, None] * freq_index[None, :] % line_total
    real_part, imag_part = rotate(spread[0], spread[1], phase_index[:, :, None], line_total, -1.0)
    twisted = jnp.stack([real_part, imag_part])
    long_forward = dft_table(LINES_DEV, -1.0, 1.0 / math.sqrt(LINES_DEV))
    spectrum = jnp.einsum(
        "dkcm,cmjr->dkjr",
        long_forward,
        lax.all_to_all(twisted, "az", split_axis=2, concat_axis=1, tiled=True),
        precision=lax.Precision.HIGHEST,
    )
    spectrum_rows = spectrum[:, :, 0, :]
    slab_rows = LINES_DEV // SLABS
    block_count = bin_count // 128
    padded = with_halo(spectrum_rows, (("rg", 2),), 128)
    local_band = lax.dynamic_slice_in_dim(band_start, rg_index * block_count, block_count, 1)
    starts = (local_band - rg_index * block_count) * 128 + 128
    remapped = stolt(padded, stolt_weights, starts, slab_rows)
    long_inverse = dft_table(LINES_DEV, 1.0, 1.0 / math.sqrt(LINES_DEV))
    lines_back = jnp.einsum(
        "dmck,ckr->dmr", long_inverse, remapped, precision=lax.Precision.HIGHEST
    )
    all_lines = jnp.arange(LINES_DEV, dtype=jnp.int32)
    back_index = all_lines * az_index % line_total
    real_part, imag_part = rotate(
        lines_back[0], lines_back[1], back_index[:, None], line_total, 1.0
    )
    unrolled = jnp.stack([real_part, imag_part])[:, :, None, :]
    short_inverse = dft_table(groups, 1.0, 1.0 / math.sqrt(groups))
    focused = jnp.einsum(
        "dpck,cmkr->dmpr",
        short_inverse,
        lax.all_to_all(unrolled, "az", split_axis=1, concat_axis=2, tiled=True),
        precision=lax.Precision.HIGHEST,
    )
    return focused.astype(jnp.bfloat16)


NDEV = 8
MLOC = LINES_DEV // NDEV
ROWS = 2 * MLOC
HALF = 16
TAIL = 8
TILES = 8
LINES = 2 * LINES_DEV
SIDE = LINES_DEV // 2
EARLY = (6, 2, 5, 4, 1, 0)
LATE = (3, 7)
EARLY_ROWS = 192
LEAD = (2,)
SPREAD_LEAD = (6, )
SPREAD_REST = (2, 4, 5, 1, 3, 7, 0, )
REST = (0, 1, 3)
VMEM_LIMIT = 20 * 1024 * 1024


def split2(x):
    hi = x.astype(BF16)
    lo = (x - hi.astype(F32)).astype(BF16)
    return hi, lo


def mm(a, b):
    return jnp.dot(a, b, preferred_element_type=F32)


def product3(table, pair):
    return mm(table[0], pair[0]) + mm(table[0], pair[1]) + mm(table[1], pair[0])


def short_table(me):
    row = lax.broadcasted_iota(jnp.int32, (16, 256), 0)
    column = lax.broadcasted_iota(jnp.int32, (16, 256), 1)
    residue = (row // 2) ^ me
    quarter = row % 2 - column // 128
    turn = (residue * (2 * (column % 8) + me // 4) + 4 * quarter + 16) % 16
    value = jnp.cos(turn.astype(F32) * (2.0 * math.pi / 16))
    line = lax.broadcasted_iota(jnp.int32, (HALF, 256), 1) // 8 % HALF
    same = line == lax.broadcasted_iota(jnp.int32, (HALF, 256), 0)
    return jnp.concatenate([jnp.where(same, value[n : n + 1], 0.0) for n in range(16)], 0)


def long_base():
    k2 = np.arange(LINES_DEV).reshape(-1, 2).T.reshape(1, -1)
    angle = 2 * np.pi * (np.arange(SIDE).reshape(-1, 1) * k2 % LINES_DEV) / LINES_DEV
    return np.stack([np.cos(angle), np.sin(angle)]).astype(np.float32)


def rows_at(index, size):
    return pl.ds(pl.multiple_of(index * size, size), size)


def tiles_of(ref):
    return (ref.shape[-2] - TAIL) // ROWS


def store_coded(out_ref, pieces):
    tiles = tiles_of(out_ref)
    peak = None
    for _, value in pieces:
        top = jnp.max(jnp.abs(value), axis=0, keepdims=True)
        peak = top if peak is None else jnp.maximum(peak, top)
    code = jnp.ceil(jnp.log2(jnp.maximum(peak, 1e-33) * (1.0 / FULL)) * CODE_STEPS + 0.01)
    inverse = jnp.exp2(code * (-1.0 / CODE_STEPS))
    for row, value in pieces:
        coded = jnp.round(value * inverse).astype(jnp.int32).astype(jnp.int16)
        for tile in range(tiles):
            at = tile * ROWS + row
            out_ref[at : at + value.shape[0], :] = coded[:, tile * TILE : (tile + 1) * TILE]
    which = lax.broadcasted_iota(jnp.int32, (TAIL, TILE), 0)
    scales = jnp.zeros((TAIL, TILE), F32)
    for tile in range(tiles):
        scales = jnp.where(which == tile, code[:, tile * TILE : (tile + 1) * TILE], scales)
    out_ref[tiles * ROWS : tiles * ROWS + TAIL, :] = scales.astype(jnp.int32).astype(jnp.int16)


def load_scales(ref):
    at = tiles_of(ref) * ROWS
    code = ref[at : at + TAIL, :].astype(jnp.int32).astype(F32)
    return jnp.exp2(code * (1.0 / CODE_STEPS))


def load_columns(ref, scales, tiles):
    parts = []
    for t in tiles:
        value = ref[t * ROWS : (t + 1) * ROWS, :].astype(jnp.int32).astype(F32)
        parts.append(value * scales[t : t + 1, :])
    return jnp.concatenate(parts, 1)


def tile_pairs(tiles):
    return [(t, t + 1) for t in range(0, tiles, 2)]


def stacked3(pair):
    return jnp.concatenate([pair[0], pair[1], pair[0]], 0)


def late_table(rows):
    hi, lo = (v.astype(F32) for v in split2(rows))
    return jnp.concatenate([hi, hi, lo], 0).T.astype(BF16)


def sign_of(me):
    return (1 - 2 * (me // 4)).astype(F32)


def spread_kernel(which, me_ref, x_ref, *out_refs):
    table = short_table(me_ref[0])
    hi, lo = split2(jnp.concatenate([table[i * 32 : (i + 1) * 32] for i in which], 0))
    halves = []
    for h in range(2):
        at = h * 128
        x = jnp.concatenate([x_ref[at : at + 128, :], x_ref[256 + at : 256 + at + 128, :]], 0)
        halves.append(mm(hi, x) + mm(lo, x))
    for n, out_ref in enumerate(out_refs):
        pieces = []
        for c in range(2):
            for h in range(2):
                at = n * 32 + c * HALF
                pieces.append((c * MLOC + h * HALF, halves[h][at : at + HALF, :]))
        store_coded(out_ref, pieces)


def tables_kernel(me_ref, band_ref, base_ref, *refs):
    forward_ref, forward_late_ref, inverse_ref, image_ref, image_late_ref, starts_ref = refs
    me = me_ref[0]
    step = 2.0 * math.pi / (NDEV * LINES_DEV)
    blocks = []
    for i in range(4):
        slot = (me & 3) ^ i
        line = lax.broadcasted_iota(jnp.int32, (MLOC, TILE), 0) + slot * MLOC
        angle = (line * me).astype(F32) * step
        turn_cos, turn_sin = jnp.cos(angle) * (1.0 / 64.0), jnp.sin(angle) * (1.0 / 64.0)
        cosine, sine = [base_ref[n, rows_at(slot, MLOC), :] for n in range(2)]
        turn_cos = jnp.concatenate([turn_cos, turn_cos], 1)
        turn_sin = jnp.concatenate([turn_sin, turn_sin], 1)
        blocks.append((cosine * turn_cos - sine * turn_sin, sine * turn_cos + cosine * turn_sin))
    whole = [jnp.concatenate([b[n] for b in blocks], 0) for n in range(2)]
    for parity in range(2):
        co, si = [w[:, parity * SIDE : (parity + 1) * SIDE] for w in whole]
        inverse = jnp.concatenate([jnp.concatenate([co, -si], 1), jnp.concatenate([si, co], 1)], 0)
        inverse_ref[0, parity], inverse_ref[1, parity] = split2(inverse)
        early = jnp.concatenate([inverse[:96], inverse[128:224]], 0).T * 2.0
        forward_ref[0, parity], forward_ref[1, parity] = split2(early)
        forward_late_ref[parity] = late_table(jnp.concatenate([inverse[96:128], inverse[224:]], 0) * 2.0)
    short = short_table(me)
    early, late = [
        jnp.concatenate([short[i * 32 : (i + 1) * 32] for i in which], 0) for which in (EARLY, LATE)
    ]
    image_ref[0], image_ref[1] = split2(early.T)
    image_late_ref[...] = late_table(late)
    starts_ref[...] = band_ref[...]


def side_lines(values, pairs, sign):
    sums = [values[i] + values[i + 4] for i in pairs]
    gaps = [(values[i] - values[i + 4]) * sign for i in pairs]
    for lines in (sums, gaps):
        yield split2(jnp.concatenate([v[:MLOC] for v in lines] + [v[MLOC:] for v in lines], 0))


def forward_early_kernel(me_ref, table_ref, *refs):
    in_refs, sum_ref = dict(zip(EARLY, refs)), refs[len(EARLY)]
    sign = sign_of(me_ref[0])
    scales = {i: load_scales(ref) for i, ref in in_refs.items()}
    for tiles in tile_pairs(TILES):
        values = {i: load_columns(ref, scales[i], tiles) for i, ref in in_refs.items()}
        for parity, pair in enumerate(side_lines(values, (0, 1, 2), sign)):
            columns = slice(tiles[0] * TILE, (tiles[0] + 2) * TILE)
            sum_ref[parity, :, columns] = product3((table_ref[0, parity], table_ref[1, parity]), pair)


def forward_kernel(me_ref, rg_ref, table_ref, sum_ref, *refs):
    in_refs, (out_ref, edge_ref) = dict(zip(LATE, refs)), refs[len(LATE) :]
    sign = sign_of(me_ref[0])
    scales = {i: load_scales(ref) for i, ref in in_refs.items()}
    for tiles in tile_pairs(TILES):
        values = {i: load_columns(ref, scales[i], tiles) for i, ref in in_refs.items()}
        for parity, pair in enumerate(side_lines(values, (3,), sign)):
            columns = slice(tiles[0] * TILE, (tiles[0] + 2) * TILE)
            result = sum_ref[parity, :, columns] + mm(table_ref[parity], stacked3(pair))
            for at, t in enumerate(tiles):
                for part, half in enumerate(split2(result[:, at * TILE : (at + 1) * TILE])):
                    out_ref[t, part, parity * 256 : (parity + 1) * 256, :] = half
    edge_ref[...] = out_ref[(1 - rg_ref[0]) * (TILES - 1)]


def remap_block(starts_ref, weights_ref, rg, j, tile_at):
    for g in range(SLABS):
        at = starts_ref[g, rg * TILES + j] - rg * TILES
        window = []
        for part in range(2):
            for parity in range(2):
                for c in range(2):
                    row = parity * 256 + c * 128 + g * 32
                    rows = slice(row, row + 32)
                    window.append(jnp.concatenate([tile_at(at + n, part, rows) for n in range(2)], 1))
        both = mm(jnp.concatenate(window, 0), weights_ref[g, j])
        yield g, split2(both[:128] + both[128:])


def focus_rows(g):
    return [(parity, c * 128 + g * 32) for parity in range(2) for c in range(2)]


def inner_kernel(rg_ref, starts_ref, spectrum_ref, weights_ref, focus_ref):
    rg = rg_ref[0]
    for n in range(TILES - 1):
        j = n + rg
        for g, pair in remap_block(
            starts_ref, weights_ref, rg, j, lambda t, part, rows: spectrum_ref[t, part, rows, :]
        ):
            for part, half in enumerate(pair):
                for at, (parity, row) in enumerate(focus_rows(g)):
                    focus_ref[part, parity, j, row : row + 32, :] = half[at * 32 : (at + 1) * 32]


def back_messages(me, rg, slots, table_ref, focus_ref, face_ref, out_refs):
    results = []
    for parity in range(2):
        table = [
            jnp.concatenate(
                [
                    table_ref[part, parity, c * SIDE + i * MLOC : c * SIDE + (i + 1) * MLOC, :]
                    for i in slots
                    for c in range(2)
                ],
                0,
            )
            for part in range(2)
        ]
        pair = []
        for part in range(2):
            block = face_ref[part, parity]
            inner = [focus_ref[part, parity, n] for n in range(TILES)]
            inner[0] = jnp.where(rg == 1, block, inner[0])
            inner[-1] = jnp.where(rg == 1, inner[-1], block)
            pair.append(jnp.concatenate(inner, 1))
        results.append(product3(table, pair))
    even, odd = results[0], results[1] * sign_of(me)
    for upper, lines in enumerate((even + odd, even - odd)):
        for n in range(len(slots)):
            store_coded(out_refs[2 * n + upper], [(0, lines[n * ROWS : (n + 1) * ROWS, :])])


def outer_kernel(me_ref, rg_ref, starts_ref, spectrum_ref, halo_ref, weights_ref, table_ref, focus_ref, *refs):
    out_refs, face_ref, window_ref = refs[:2], refs[2], refs[3]
    rg = rg_ref[0]
    first = 6 - 7 * rg
    window_ref[2 - 2 * rg] = halo_ref[...]
    for n in range(2):
        window_ref[rg + n] = spectrum_ref[(1 - rg) * 6 + n]
    for g, pair in remap_block(
        starts_ref,
        weights_ref,
        rg,
        (1 - rg) * (TILES - 1),
        lambda t, part, rows: window_ref[t - first, part, rows, :],
    ):
        for part, half in enumerate(pair):
            for at, (parity, row) in enumerate(focus_rows(g)):
                face_ref[part, parity, row : row + 32, :] = half[at * 32 : (at + 1) * 32]
    back_messages(me_ref[0], rg, LEAD, table_ref, focus_ref, face_ref, out_refs)


def rest_kernel(me_ref, rg_ref, table_ref, focus_ref, face_ref, *out_refs):
    back_messages(me_ref[0], rg_ref[0], REST, table_ref, focus_ref, face_ref, out_refs)


def image_lines(values, h):
    rows = [v[c * MLOC + h * HALF : c * MLOC + (h + 1) * HALF] for v in values for c in range(2)]
    return split2(jnp.concatenate(rows, 0))


def image_early_kernel(table_ref, *refs):
    in_refs, sum_ref = refs[: len(EARLY)], refs[len(EARLY)]
    scales = [load_scales(ref) for ref in in_refs]
    for tiles in tile_pairs(TILES):
        values = [load_columns(ref, scale, tiles) for ref, scale in zip(in_refs, scales)]
        for h in range(2):
            columns = slice(tiles[0] * TILE, (tiles[0] + 2) * TILE)
            sum_ref[h, :, columns] = product3(table_ref, image_lines(values, h))


def image_kernel(table_ref, sum_ref, *refs):
    in_refs, (out_hbm, out_ref, sems) = refs[: len(LATE)], refs[len(LATE) :]
    stores = []
    scales = [load_scales(ref) for ref in in_refs]
    for tiles in tile_pairs(TILES):
        values = [load_columns(ref, scale, tiles) for ref, scale in zip(in_refs, scales)]
        for h in range(2):
            columns = slice(tiles[0] * TILE, (tiles[0] + 2) * TILE)
            result = sum_ref[h, :, columns] + mm(table_ref[...], stacked3(image_lines(values, h)))
            for c in range(2):
                at = c * 256 + h * 128
                out_ref[at : at + 128, columns] = result[c * 128 : (c + 1) * 128].astype(BF16)
        stores.append(
            pltpu.make_async_copy(out_ref.at[:, columns], out_hbm.at[:, columns], sems.at[tiles[0] // 2])
        )
        stores[-1].start()
    for store in stores:
        store.wait()


def vmem_call(kernel, name, out_shape, smem=0, vmem=0, scratch=(), out_space=pltpu.VMEM):
    return pl.pallas_call(
        kernel,
        name=name,
        out_shape=out_shape,
        in_specs=[pl.BlockSpec(memory_space=pltpu.SMEM)] * smem
        + [pl.BlockSpec(memory_space=pltpu.VMEM)] * vmem,
        out_specs=jax.tree.map(lambda _: pl.BlockSpec(memory_space=out_space), out_shape),
        scratch_shapes=scratch,
        compiler_params=pltpu.CompilerParams(vmem_limit_bytes=VMEM_LIMIT),
    )


def after(value, *others):
    return lax.optimization_barrier((value, *others))[0]


def exchange(messages):
    return [
        [
            lax.ppermute(messages[i], "az", [(d, d ^ i) for d in range(NDEV)]) if i else messages[0]
            for i in which
        ]
        for which in (EARLY, LATE)
    ]


def fast_body(raw, stolt_weights, band_start):
    me = lax.axis_index("az").astype(jnp.int32)[None]
    rg = lax.axis_index("rg").astype(jnp.int32)[None]
    bins = raw.shape[3]
    message = jax.ShapeDtypeStruct((TILES * ROWS + TAIL, TILE), jnp.int16)
    early_shape = (2, LINES_DEV, EARLY_ROWS)

    rows = raw.reshape(LINES, bins)
    sent = [None] * NDEV
    for name, which in (("spread", SPREAD_LEAD), ("spread_rest", SPREAD_REST)):
        own = me if name == "spread" else after(me, sent[SPREAD_LEAD[0]])
        made = vmem_call(functools.partial(spread_kernel, which), name, [message] * len(which), smem=1, vmem=1)(
            own, rows
        )
        for n, i in enumerate(which):
            sent[i] = made[n]
    got_early, got_late = exchange(sent)
    forward_table, forward_late, inverse_table, image_table, image_late, starts = vmem_call(
        tables_kernel,
        "tables",
        [
            jax.ShapeDtypeStruct((2,) + early_shape, BF16),
            jax.ShapeDtypeStruct(early_shape, BF16),
            jax.ShapeDtypeStruct((2, 2, LINES_DEV, LINES_DEV), BF16),
            jax.ShapeDtypeStruct((2, 256, EARLY_ROWS), BF16),
            jax.ShapeDtypeStruct((256, EARLY_ROWS), BF16),
            jax.ShapeDtypeStruct(band_start.shape, band_start.dtype),
        ],
        smem=1,
        vmem=2,
    )(after(me, sent[SPREAD_REST[0]]), band_start, jnp.asarray(long_base()))

    partial = vmem_call(
        forward_early_kernel,
        "forward_early",
        jax.ShapeDtypeStruct((2, LINES_DEV, bins), F32),
        smem=1,
        vmem=1 + len(EARLY),
    )(me, forward_table, *got_early)
    spectrum, edge = vmem_call(
        forward_kernel,
        "forward",
        [jax.ShapeDtypeStruct((TILES, 2, LINES, TILE), BF16), jax.ShapeDtypeStruct((2, LINES, TILE), BF16)],
        smem=2,
        vmem=2 + len(LATE),
    )(me, rg, forward_late, partial, *got_late)
    halo = lax.ppermute(edge, "rg", [(0, 1), (1, 0)])
    focus = vmem_call(
        inner_kernel,
        "inner",
        jax.ShapeDtypeStruct((2, 2, TILES, LINES_DEV, TILE), BF16),
        smem=2,
        vmem=2,
    )(rg, starts, spectrum, stolt_weights)
    back = [None] * NDEV
    back[2], back[6], face = vmem_call(
        outer_kernel,
        "outer",
        [message, message, jax.ShapeDtypeStruct((2, 2, LINES_DEV, TILE), BF16)],
        smem=3,
        vmem=5,
        scratch=[pltpu.VMEM((3, 2, LINES, TILE), BF16)],
    )(me, rg, starts, spectrum, halo, stolt_weights, inverse_table, focus)
    rest = vmem_call(rest_kernel, "rest", [message] * 6, smem=2, vmem=3)(me, rg, inverse_table, focus, face)
    for n, i in enumerate(REST):
        back[i], back[i + 4] = rest[2 * n], rest[2 * n + 1]
    early_lines, late_lines = exchange(back)
    image_sum = vmem_call(
        image_early_kernel, "image_early", jax.ShapeDtypeStruct((2, 256, bins), F32), vmem=1 + len(EARLY)
    )(image_table, *early_lines)
    image = vmem_call(
        image_kernel,
        "image",
        jax.ShapeDtypeStruct((LINES, bins), BF16),
        vmem=2 + len(LATE),
        scratch=[pltpu.VMEM((LINES, bins), BF16), pltpu.SemaphoreType.DMA((TILES // 2,))],
        out_space=pltpu.HBM,
    )(image_late, image_sum, *late_lines)
    return image.reshape(2, MLOC, NDEV, bins)


def body(raw, stolt_weights, band_start):
    fast = (
        lax.axis_size("az") == NDEV
        and lax.axis_size("rg") == 2
        and raw.shape[1:3] == (MLOC, NDEV)
        and raw.shape[3] == TILES * TILE
    )
    return (fast_body if fast else generic_body)(raw, stolt_weights, band_start)


def solution(mesh):
    placed = (P(None, ("frames", "az"), None, "rg"), P(None, "rg", None, None), P())
    return jax.shard_map(
        body,
        mesh=mesh,
        in_specs=placed,
        out_specs=P(None, ("frames", "az"), None, "rg"),
        check_vma=False,
    )
```

```python
import functools
import math

import jax
import jax.numpy as jnp
import numpy as np
from jax import lax
from jax.experimental import pallas as pl
from jax.experimental.pallas import tpu as pltpu
from jax.sharding import PartitionSpec as P

LINES_DEV = 256
SLABS = 4
TILE = 128
BF16 = jnp.bfloat16
F32 = jnp.float32
CODE_STEPS = 256.0
FULL = 32767.0


def with_halo(cells, sides, width):
    for axis, dim in sides:
        count = lax.axis_size(axis)
        ends = count - 1
        head = lax.slice_in_dim(cells, 0, width, axis=dim)
        tail = lax.slice_in_dim(cells, cells.shape[dim] - width, cells.shape[dim], axis=dim)
        cells = jnp.concatenate(
            [
                lax.ppermute(tail, axis, [(i, (i + 1) % count) for i in range(ends)]),
                cells,
                lax.ppermute(head, axis, [((i + 1) % count, i) for i in range(ends)]),
            ],
            axis=dim,
        )
    return cells


def dft_table(length, direction, factor):
    counter = jnp.arange(length, dtype=jnp.int32)
    product = counter[:, None] * counter[None, :] % length
    angles = product.astype(jnp.float32) * (2.0 * math.pi / length)
    cosine = jnp.cos(angles) * factor
    sines = jnp.sin(angles) * (factor * direction)
    return jnp.stack([jnp.stack([cosine, -sines], 1), jnp.stack([sines, cosine], 1)], 0)


def rotate(real_part, imag_part, phase_index, line_total, direction):
    angles = phase_index.astype(jnp.float32) * (2.0 * math.pi / line_total)
    cosine = jnp.cos(angles)
    sines = jnp.sin(angles) * direction
    return (real_part * cosine - imag_part * sines, imag_part * cosine + real_part * sines)


def stolt(slab_source, weights, starts, slab_rows):
    pieces = []
    for slab_index in range(weights.shape[0]):
        slab_data = slab_source[:, slab_index * slab_rows : (slab_index + 1) * slab_rows, :]

        def window_at(start_bin):
            return lax.dynamic_slice_in_dim(slab_data, start_bin, 256, 2)

        windows = jax.vmap(window_at)(starts[slab_index])
        remixed = jnp.einsum(
            "jcmb,jbo->cmjo",
            windows,
            weights[slab_index].astype(jnp.float32),
            precision=lax.Precision.HIGHEST,
        )
        pieces.append(remixed.reshape(2, slab_rows, -1))
    return jnp.concatenate(pieces, 1)


def generic_body(raw, stolt_weights, band_start):
    groups = lax.axis_size("az")
    az_index = lax.axis_index("az")
    rg_index = lax.axis_index("rg")
    part_lines = raw.shape[1]
    bin_count = raw.shape[3]
    line_total = LINES_DEV * groups
    short_forward = dft_table(groups, -1.0, 1.0 / math.sqrt(groups))
    spread = jnp.einsum(
        "dkcp,cmpr->dmkr", short_forward, raw.astype(jnp.float32), precision=lax.Precision.HIGHEST
    )
    line_index = az_index * part_lines + jnp.arange(part_lines, dtype=jnp.int32)
    freq_index = jnp.arange(groups, dtype=jnp.int32)
    phase_index = line_index[:, None] * freq_index[None, :] % line_total
    real_part, imag_part = rotate(spread[0], spread[1], phase_index[:, :, None], line_total, -1.0)
    twisted = jnp.stack([real_part, imag_part])
    long_forward = dft_table(LINES_DEV, -1.0, 1.0 / math.sqrt(LINES_DEV))
    spectrum = jnp.einsum(
        "dkcm,cmjr->dkjr",
        long_forward,
        lax.all_to_all(twisted, "az", split_axis=2, concat_axis=1, tiled=True),
        precision=lax.Precision.HIGHEST,
    )
    spectrum_rows = spectrum[:, :, 0, :]
    slab_rows = LINES_DEV // SLABS
    block_count = bin_count // 128
    padded = with_halo(spectrum_rows, (("rg", 2),), 128)
    local_band = lax.dynamic_slice_in_dim(band_start, rg_index * block_count, block_count, 1)
    starts = (local_band - rg_index * block_count) * 128 + 128
    remapped = stolt(padded, stolt_weights, starts, slab_rows)
    long_inverse = dft_table(LINES_DEV, 1.0, 1.0 / math.sqrt(LINES_DEV))
    lines_back = jnp.einsum(
        "dmck,ckr->dmr", long_inverse, remapped, precision=lax.Precision.HIGHEST
    )
    all_lines = jnp.arange(LINES_DEV, dtype=jnp.int32)
    back_index = all_lines * az_index % line_total
    real_part, imag_part = rotate(
        lines_back[0], lines_back[1], back_index[:, None], line_total, 1.0
    )
    unrolled = jnp.stack([real_part, imag_part])[:, :, None, :]
    short_inverse = dft_table(groups, 1.0, 1.0 / math.sqrt(groups))
    focused = jnp.einsum(
        "dpck,cmkr->dmpr",
        short_inverse,
        lax.all_to_all(unrolled, "az", split_axis=1, concat_axis=2, tiled=True),
        precision=lax.Precision.HIGHEST,
    )
    return focused.astype(jnp.bfloat16)


NDEV = 8
MLOC = LINES_DEV // NDEV
ROWS = 2 * MLOC
HALF = 16
TAIL = 8
TILES = 8
LINES = 2 * LINES_DEV
SIDE = LINES_DEV // 2
EARLY = (6, 2, 5, 4, 1, 0)
LATE = (3, 7)
EARLY_ROWS = 192
LEAD = (2,)
SPREAD_LEAD = (6, )
SPREAD_REST = (2, 5, 4, 1, 3, 7, 0)
REST = (0, 1, 3)
VMEM_LIMIT = 20 * 1024 * 1024


def split2(x):
    hi = x.astype(BF16)
    lo = (x - hi.astype(F32)).astype(BF16)
    return hi, lo


def mm(a, b):
    return jnp.dot(a, b, preferred_element_type=F32)


def product3(table, pair):
    return mm(table[0], pair[0]) + mm(table[0], pair[1]) + mm(table[1], pair[0])


def short_table(me):
    row = lax.broadcasted_iota(jnp.int32, (16, 256), 0)
    column = lax.broadcasted_iota(jnp.int32, (16, 256), 1)
    residue = (row // 2) ^ me
    quarter = row % 2 - column // 128
    turn = (residue * (2 * (column % 8) + me // 4) + 4 * quarter + 16) % 16
    value = jnp.cos(turn.astype(F32) * (2.0 * math.pi / 16))
    line = lax.broadcasted_iota(jnp.int32, (HALF, 256), 1) // 8 % HALF
    same = line == lax.broadcasted_iota(jnp.int32, (HALF, 256), 0)
    return jnp.concatenate([jnp.where(same, value[n : n + 1], 0.0) for n in range(16)], 0)


def long_base():
    k2 = np.arange(LINES_DEV).reshape(-1, 2).T.reshape(1, -1)
    angle = 2 * np.pi * (np.arange(SIDE).reshape(-1, 1) * k2 % LINES_DEV) / LINES_DEV
    return np.stack([np.cos(angle), np.sin(angle)]).astype(np.float32)


def rows_at(index, size):
    return pl.ds(pl.multiple_of(index * size, size), size)


def tiles_of(ref):
    return (ref.shape[-2] - TAIL) // ROWS


def store_coded(out_ref, pieces):
    tiles = tiles_of(out_ref)
    peak = None
    for _, value in pieces:
        top = jnp.max(jnp.abs(value), axis=0, keepdims=True)
        peak = top if peak is None else jnp.maximum(peak, top)
    code = jnp.ceil(jnp.log2(jnp.maximum(peak, 1e-33) * (1.0 / FULL)) * CODE_STEPS + 0.01)
    inverse = jnp.exp2(code * (-1.0 / CODE_STEPS))
    for row, value in pieces:
        coded = jnp.round(value * inverse).astype(jnp.int32).astype(jnp.int16)
        for tile in range(tiles):
            at = tile * ROWS + row
            out_ref[at : at + value.shape[0], :] = coded[:, tile * TILE : (tile + 1) * TILE]
    which = lax.broadcasted_iota(jnp.int32, (TAIL, TILE), 0)
    scales = jnp.zeros((TAIL, TILE), F32)
    for tile in range(tiles):
        scales = jnp.where(which == tile, code[:, tile * TILE : (tile + 1) * TILE], scales)
    out_ref[tiles * ROWS : tiles * ROWS + TAIL, :] = scales.astype(jnp.int32).astype(jnp.int16)


def load_scales(ref):
    at = tiles_of(ref) * ROWS
    code = ref[at : at + TAIL, :].astype(jnp.int32).astype(F32)
    return jnp.exp2(code * (1.0 / CODE_STEPS))


def load_columns(ref, scales, tiles):
    parts = []
    for t in tiles:
        value = ref[t * ROWS : (t + 1) * ROWS, :].astype(jnp.int32).astype(F32)
        parts.append(value * scales[t : t + 1, :])
    return jnp.concatenate(parts, 1)


def tile_pairs(tiles):
    return [(t, t + 1) for t in range(0, tiles, 2)]


def stacked3(pair):
    return jnp.concatenate([pair[0], pair[1], pair[0]], 0)


def late_table(rows):
    hi, lo = (v.astype(F32) for v in split2(rows))
    return jnp.concatenate([hi, hi, lo], 0).T.astype(BF16)


def sign_of(me):
    return (1 - 2 * (me // 4)).astype(F32)


def spread_kernel(which, me_ref, x_ref, *out_refs):
    table = short_table(me_ref[0])
    hi, lo = split2(jnp.concatenate([table[i * 32 : (i + 1) * 32] for i in which], 0))
    halves = []
    for h in range(2):
        at = h * 128
        x = jnp.concatenate([x_ref[at : at + 128, :], x_ref[256 + at : 256 + at + 128, :]], 0)
        halves.append(mm(hi, x) + mm(lo, x))
    for n, out_ref in enumerate(out_refs):
        pieces = []
        for c in range(2):
            for h in range(2):
                at = n * 32 + c * HALF
                pieces.append((c * MLOC + h * HALF, halves[h][at : at + HALF, :]))
        store_coded(out_ref, pieces)


def tables_kernel(me_ref, band_ref, base_ref, *refs):
    forward_ref, forward_late_ref, inverse_ref, image_ref, image_late_ref, starts_ref = refs
    me = me_ref[0]
    step = 2.0 * math.pi / (NDEV * LINES_DEV)
    blocks = []
    for i in range(4):
        slot = (me & 3) ^ i
        line = lax.broadcasted_iota(jnp.int32, (MLOC, TILE), 0) + slot * MLOC
        angle = (line * me).astype(F32) * step
        turn_cos, turn_sin = jnp.cos(angle) * (1.0 / 64.0), jnp.sin(angle) * (1.0 / 64.0)
        cosine, sine = [base_ref[n, rows_at(slot, MLOC), :] for n in range(2)]
        turn_cos = jnp.concatenate([turn_cos, turn_cos], 1)
        turn_sin = jnp.concatenate([turn_sin, turn_sin], 1)
        blocks.append((cosine * turn_cos - sine * turn_sin, sine * turn_cos + cosine * turn_sin))
    whole = [jnp.concatenate([b[n] for b in blocks], 0) for n in range(2)]
    for parity in range(2):
        co, si = [w[:, parity * SIDE : (parity + 1) * SIDE] for w in whole]
        inverse = jnp.concatenate([jnp.concatenate([co, -si], 1), jnp.concatenate([si, co], 1)], 0)
        inverse_ref[0, parity], inverse_ref[1, parity] = split2(inverse)
        early = jnp.concatenate([inverse[:96], inverse[128:224]], 0).T * 2.0
        forward_ref[0, parity], forward_ref[1, parity] = split2(early)
        forward_late_ref[parity] = late_table(jnp.concatenate([inverse[96:128], inverse[224:]], 0) * 2.0)
    short = short_table(me)
    early, late = [
        jnp.concatenate([short[i * 32 : (i + 1) * 32] for i in which], 0) for which in (EARLY, LATE)
    ]
    image_ref[0], image_ref[1] = split2(early.T)
    image_late_ref[...] = late_table(late)
    starts_ref[...] = band_ref[...]


def side_lines(values, pairs, sign):
    sums = [values[i] + values[i + 4] for i in pairs]
    gaps = [(values[i] - values[i + 4]) * sign for i in pairs]
    for lines in (sums, gaps):
        yield split2(jnp.concatenate([v[:MLOC] for v in lines] + [v[MLOC:] for v in lines], 0))


def forward_early_kernel(me_ref, table_ref, *refs):
    in_refs, sum_ref = dict(zip(EARLY, refs)), refs[len(EARLY)]
    sign = sign_of(me_ref[0])
    scales = {i: load_scales(ref) for i, ref in in_refs.items()}
    for tiles in tile_pairs(TILES):
        values = {i: load_columns(ref, scales[i], tiles) for i, ref in in_refs.items()}
        for parity, pair in enumerate(side_lines(values, (0, 1, 2), sign)):
            columns = slice(tiles[0] * TILE, (tiles[0] + 2) * TILE)
            sum_ref[parity, :, columns] = product3((table_ref[0, parity], table_ref[1, parity]), pair)


def forward_kernel(me_ref, rg_ref, table_ref, sum_ref, *refs):
    in_refs, (out_ref, edge_ref) = dict(zip(LATE, refs)), refs[len(LATE) :]
    sign = sign_of(me_ref[0])
    scales = {i: load_scales(ref) for i, ref in in_refs.items()}
    for tiles in tile_pairs(TILES):
        values = {i: load_columns(ref, scales[i], tiles) for i, ref in in_refs.items()}
        for parity, pair in enumerate(side_lines(values, (3,), sign)):
            columns = slice(tiles[0] * TILE, (tiles[0] + 2) * TILE)
            result = sum_ref[parity, :, columns] + mm(table_ref[parity], stacked3(pair))
            for at, t in enumerate(tiles):
                for part, half in enumerate(split2(result[:, at * TILE : (at + 1) * TILE])):
                    out_ref[t, part, parity * 256 : (parity + 1) * 256, :] = half
    edge_ref[...] = out_ref[(1 - rg_ref[0]) * (TILES - 1)]


def remap_block(starts_ref, weights_ref, rg, j, tile_at):
    for g in range(SLABS):
        at = starts_ref[g, rg * TILES + j] - rg * TILES
        window = []
        for part in range(2):
            for parity in range(2):
                for c in range(2):
                    row = parity * 256 + c * 128 + g * 32
                    rows = slice(row, row + 32)
                    window.append(jnp.concatenate([tile_at(at + n, part, rows) for n in range(2)], 1))
        both = mm(jnp.concatenate(window, 0), weights_ref[g, j])
        yield g, split2(both[:128] + both[128:])


def focus_rows(g):
    return [(parity, c * 128 + g * 32) for parity in range(2) for c in range(2)]


def inner_kernel(rg_ref, starts_ref, spectrum_ref, weights_ref, focus_ref):
    rg = rg_ref[0]
    for n in range(TILES - 1):
        j = n + rg
        for g, pair in remap_block(
            starts_ref, weights_ref, rg, j, lambda t, part, rows: spectrum_ref[t, part, rows, :]
        ):
            for part, half in enumerate(pair):
                for at, (parity, row) in enumerate(focus_rows(g)):
                    focus_ref[part, parity, j, row : row + 32, :] = half[at * 32 : (at + 1) * 32]


def back_messages(me, rg, slots, table_ref, focus_ref, face_ref, out_refs):
    results = []
    for parity in range(2):
        table = [
            jnp.concatenate(
                [
                    table_ref[part, parity, c * SIDE + i * MLOC : c * SIDE + (i + 1) * MLOC, :]
                    for i in slots
                    for c in range(2)
                ],
                0,
            )
            for part in range(2)
        ]
        pair = []
        for part in range(2):
            block = face_ref[part, parity]
            inner = [focus_ref[part, parity, n] for n in range(TILES)]
            inner[0] = jnp.where(rg == 1, block, inner[0])
            inner[-1] = jnp.where(rg == 1, inner[-1], block)
            pair.append(jnp.concatenate(inner, 1))
        results.append(product3(table, pair))
    even, odd = results[0], results[1] * sign_of(me)
    for upper, lines in enumerate((even + odd, even - odd)):
        for n in range(len(slots)):
            store_coded(out_refs[2 * n + upper], [(0, lines[n * ROWS : (n + 1) * ROWS, :])])


def outer_kernel(me_ref, rg_ref, starts_ref, spectrum_ref, halo_ref, weights_ref, table_ref, focus_ref, *refs):
    out_refs, face_ref, window_ref = refs[:2], refs[2], refs[3]
    rg = rg_ref[0]
    first = 6 - 7 * rg
    window_ref[2 - 2 * rg] = halo_ref[...]
    for n in range(2):
        window_ref[rg + n] = spectrum_ref[(1 - rg) * 6 + n]
    for g, pair in remap_block(
        starts_ref,
        weights_ref,
        rg,
        (1 - rg) * (TILES - 1),
        lambda t, part, rows: window_ref[t - first, part, rows, :],
    ):
        for part, half in enumerate(pair):
            for at, (parity, row) in enumerate(focus_rows(g)):
                face_ref[part, parity, row : row + 32, :] = half[at * 32 : (at + 1) * 32]
    back_messages(me_ref[0], rg, LEAD, table_ref, focus_ref, face_ref, out_refs)


def rest_kernel(me_ref, rg_ref, table_ref, focus_ref, face_ref, *out_refs):
    back_messages(me_ref[0], rg_ref[0], REST, table_ref, focus_ref, face_ref, out_refs)


def image_lines(values, h):
    rows = [v[c * MLOC + h * HALF : c * MLOC + (h + 1) * HALF] for v in values for c in range(2)]
    return split2(jnp.concatenate(rows, 0))


def image_early_kernel(table_ref, *refs):
    in_refs, sum_ref = refs[: len(EARLY)], refs[len(EARLY)]
    scales = [load_scales(ref) for ref in in_refs]
    for tiles in tile_pairs(TILES):
        values = [load_columns(ref, scale, tiles) for ref, scale in zip(in_refs, scales)]
        for h in range(2):
            columns = slice(tiles[0] * TILE, (tiles[0] + 2) * TILE)
            sum_ref[h, :, columns] = product3(table_ref, image_lines(values, h))


def image_kernel(table_ref, sum_ref, *refs):
    in_refs, (out_hbm, out_ref, sems) = refs[: len(LATE)], refs[len(LATE) :]
    stores = []
    scales = [load_scales(ref) for ref in in_refs]
    for tiles in tile_pairs(TILES):
        values = [load_columns(ref, scale, tiles) for ref, scale in zip(in_refs, scales)]
        for h in range(2):
            columns = slice(tiles[0] * TILE, (tiles[0] + 2) * TILE)
            result = sum_ref[h, :, columns] + mm(table_ref[...], stacked3(image_lines(values, h)))
            for c in range(2):
                at = c * 256 + h * 128
                out_ref[at : at + 128, columns] = result[c * 128 : (c + 1) * 128].astype(BF16)
        stores.append(
            pltpu.make_async_copy(out_ref.at[:, columns], out_hbm.at[:, columns], sems.at[tiles[0] // 2])
        )
        stores[-1].start()
    for store in stores:
        store.wait()


def vmem_call(kernel, name, out_shape, smem=0, vmem=0, scratch=(), out_space=pltpu.VMEM):
    return pl.pallas_call(
        kernel,
        name=name,
        out_shape=out_shape,
        in_specs=[pl.BlockSpec(memory_space=pltpu.SMEM)] * smem
        + [pl.BlockSpec(memory_space=pltpu.VMEM)] * vmem,
        out_specs=jax.tree.map(lambda _: pl.BlockSpec(memory_space=out_space), out_shape),
        scratch_shapes=scratch,
        compiler_params=pltpu.CompilerParams(vmem_limit_bytes=VMEM_LIMIT),
    )


def after(value, *others):
    return lax.optimization_barrier((value, *others))[0]


def exchange(messages):
    return [
        [
            lax.ppermute(messages[i], "az", [(d, d ^ i) for d in range(NDEV)]) if i else messages[0]
            for i in which
        ]
        for which in (EARLY, LATE)
    ]


def fast_body(raw, stolt_weights, band_start):
    me = lax.axis_index("az").astype(jnp.int32)[None]
    rg = lax.axis_index("rg").astype(jnp.int32)[None]
    bins = raw.shape[3]
    message = jax.ShapeDtypeStruct((TILES * ROWS + TAIL, TILE), jnp.int16)
    early_shape = (2, LINES_DEV, EARLY_ROWS)

    rows = raw.reshape(LINES, bins)
    sent = [None] * NDEV
    for name, which in (("spread", SPREAD_LEAD), ("spread_rest", SPREAD_REST)):
        own = me if name == "spread" else after(me, sent[SPREAD_LEAD[0]])
        made = vmem_call(functools.partial(spread_kernel, which), name, [message] * len(which), smem=1, vmem=1)(
            own, rows
        )
        for n, i in enumerate(which):
            sent[i] = made[n]
    got_early, got_late = exchange(sent)
    forward_table, forward_late, inverse_table, image_table, image_late, starts = vmem_call(
        tables_kernel,
        "tables",
        [
            jax.ShapeDtypeStruct((2,) + early_shape, BF16),
            jax.ShapeDtypeStruct(early_shape, BF16),
            jax.ShapeDtypeStruct((2, 2, LINES_DEV, LINES_DEV), BF16),
            jax.ShapeDtypeStruct((2, 256, EARLY_ROWS), BF16),
            jax.ShapeDtypeStruct((256, EARLY_ROWS), BF16),
            jax.ShapeDtypeStruct(band_start.shape, band_start.dtype),
        ],
        smem=1,
        vmem=2,
    )(after(me, sent[SPREAD_REST[0]]), band_start, jnp.asarray(long_base()))

    partial = vmem_call(
        forward_early_kernel,
        "forward_early",
        jax.ShapeDtypeStruct((2, LINES_DEV, bins), F32),
        smem=1,
        vmem=1 + len(EARLY),
    )(me, forward_table, *got_early)
    spectrum, edge = vmem_call(
        forward_kernel,
        "forward",
        [jax.ShapeDtypeStruct((TILES, 2, LINES, TILE), BF16), jax.ShapeDtypeStruct((2, LINES, TILE), BF16)],
        smem=2,
        vmem=2 + len(LATE),
    )(me, rg, forward_late, partial, *got_late)
    halo = lax.ppermute(edge, "rg", [(0, 1), (1, 0)])
    focus = vmem_call(
        inner_kernel,
        "inner",
        jax.ShapeDtypeStruct((2, 2, TILES, LINES_DEV, TILE), BF16),
        smem=2,
        vmem=2,
    )(rg, starts, spectrum, stolt_weights)
    back = [None] * NDEV
    back[2], back[6], face = vmem_call(
        outer_kernel,
        "outer",
        [message, message, jax.ShapeDtypeStruct((2, 2, LINES_DEV, TILE), BF16)],
        smem=3,
        vmem=5,
        scratch=[pltpu.VMEM((3, 2, LINES, TILE), BF16)],
    )(me, rg, starts, spectrum, halo, stolt_weights, inverse_table, focus)
    rest = vmem_call(rest_kernel, "rest", [message] * 6, smem=2, vmem=3)(me, rg, inverse_table, focus, face)
    for n, i in enumerate(REST):
        back[i], back[i + 4] = rest[2 * n], rest[2 * n + 1]
    early_lines, late_lines = exchange(back)
    image_sum = vmem_call(
        image_early_kernel, "image_early", jax.ShapeDtypeStruct((2, 256, bins), F32), vmem=1 + len(EARLY)
    )(image_table, *early_lines)
    image = vmem_call(
        image_kernel,
        "image",
        jax.ShapeDtypeStruct((LINES, bins), BF16),
        vmem=2 + len(LATE),
        scratch=[pltpu.VMEM((LINES, bins), BF16), pltpu.SemaphoreType.DMA((TILES // 2,))],
        out_space=pltpu.HBM,
    )(image_late, image_sum, *late_lines)
    return image.reshape(2, MLOC, NDEV, bins)


def body(raw, stolt_weights, band_start):
    fast = (
        lax.axis_size("az") == NDEV
        and lax.axis_size("rg") == 2
        and raw.shape[1:3] == (MLOC, NDEV)
        and raw.shape[3] == TILES * TILE
    )
    return (fast_body if fast else generic_body)(raw, stolt_weights, band_start)


def solution(mesh):
    placed = (P(None, ("frames", "az"), None, "rg"), P(None, "rg", None, None), P())
    return jax.shard_map(
        body,
        mesh=mesh,
        in_specs=placed,
        out_specs=P(None, ("frames", "az"), None, "rg"),
        check_vma=False,
    )
```
